32 devices in a mesh: dp: 8 (over z, x), mp: 4 (over y, core).
Axes of the slice: x: 2, y: 2, z: 4, core: 2. Of those that a mesh axis runs over, the one named last changes fastest.
Arguments:
- tokens: bfloat16 [256, 48, 3584], P('dp', None, 'mp'), may hold values from -180 to 180
- norm_gain: float32 [3584], replicated, may hold values from 0.1 to 1.9
- w_query: bfloat16 [3584, 3584], P('dp', 'mp'), may hold values from -0.16 to 0.16
- w_keyval: bfloat16 [3584, 2, 512], P('dp', None, 'mp'), may hold values from -0.16 to 0.16
- w_out: bfloat16 [3584, 3584], P('mp', 'dp'), may hold values from -0.09375 to 0.09375
- residents: bfloat16 [8, 2048, 3584], P('dp', 'mp'), may hold values from -6 to 6
- lengths: int32 [256], P('dp'), may hold values from 6 to 48
- cluster: int32 [256, 1], P('dp'), may hold values from 0 to 7; in each aligned block of 32 rows (0 to 31, 32 to 63, ...) at most 4 rows name the same one
- owner: int32 [8], replicated, may hold values from 0 to 7, each once
- counts: int32 [8], replicated, may hold values from 256 to 2048
- flags: int32 [256], P('dp'), may hold values 0 or 1
Outputs:
- similarity: float32 [256, 2048], P('dp', 'mp')
The draws below stay inside these ranges and needn't reach their ends.
Inputs may be any that keep to these rules, and one draw needn't show every extreme that they name: Each dialogue's cluster; among the 32 dialogues of one index of dp (aligned blocks of rows) no cluster is named more than 4 times. owner gives every cluster a distinct index of dp that holds its residents.
All inputs are finite; a program needn't handle non-finite values. No bound on the sum of `flags` on one device may be relied on, other than what follows from the above.
Results may differ from the reference program's by a relative error of at most 0.013.
Values may be sent and summed in bfloat16 or wider, within the bound.
A program may use at most 128 MiB of HBM per device.

```python
import math
import jax
import jax.numpy as jnp
import numpy as np
from jax import lax

D = 3584
HEADS = 28
KV_HEADS = 4
HEAD_DIM = 128
LEN = 48
MEMBERS = 2048
DLG_DEV = 32
DIALOGUES = 256
CLUSTERS = 8
CAP = 4


def draw_w_query(key, part):
    spread_scale = D ** (-0.5)
    noise_key = jax.random.fold_in(key, 11)
    shape_full = (D, HEADS * HEAD_DIM)
    drawn = jnp.clip(jax.random.normal(noise_key, shape_full, jnp.float32), -6.0, 6.0) * spread_scale
    return drawn.astype(jnp.bfloat16)


def draw_w_keyval(key, part):
    spread_scale = D ** (-0.5)
    noise_key = jax.random.fold_in(key, 13)
    shape_full = (D, 2, KV_HEADS * HEAD_DIM)
    drawn = jnp.clip(jax.random.normal(noise_key, shape_full, jnp.float32), -6.0, 6.0) * spread_scale
    return drawn.astype(jnp.bfloat16)


def draw_tokens(key, part):
    noise_key = jax.random.fold_in(key, 17)
    shape_full = (DIALOGUES, LEN, D)
    drawn = jnp.clip(jax.random.normal(noise_key, shape_full, jnp.float32), -6.0, 6.0)
    return drawn.astype(jnp.bfloat16)


def set_ends(array, rng, least, top_value):
    extent = array.shape
    index_at = [jax.random.randint(jax.random.fold_in(rng, axis), (), 0, extent[axis]) for axis in range(len(extent))]
    array = array.at[tuple(index_at)].set(least)
    longest = extent.index(max(extent))
    index_at[longest] = (index_at[longest] + 1) % extent[longest]
    return array.at[tuple(index_at)].set(top_value)


def levels(stream_key, shape, split, least, largest):
    loudness = 1.0
    for axis_at, blocks in split:
        steps = jax.random.uniform(jax.random.fold_in(jax.random.fold_in(stream_key, 6), axis_at), (blocks,), jnp.float32, least / len(split), largest / len(split))
        loudness = loudness * jnp.repeat(jnp.exp(steps), shape[axis_at] // blocks).reshape((-1,) + (1,) * (len(shape) - 1 - axis_at))
    return loudness


def assign_block(own_key, own, number, rows, amount, top, reach, skew):
    sequence = jax.random.permutation(own_key, amount)
    packed, usual = portions_of(amount, rows * top, reach, skew, True), portions_of(amount, rows * top, reach, skew, False)
    places = jnp.arange(amount)

    def named(sizes, rotation):
        used = int((sizes > 0).sum())
        fixed = max(1, used // 4)
        shifted = fixed + (places - fixed + rotation * (used - fixed)) % max(1, amount - fixed)
        return jnp.zeros((amount,), jnp.int32).at[sequence[jnp.where(places < fixed, places, shifted)]].set(jnp.asarray(sizes, jnp.int32))

    sizes = jnp.where(number % 4 == 0, named(packed, number // 4), named(usual, number - number // 4 - 1))
    mixed = jax.random.permutation(jax.random.fold_in(own, 3), amount)
    source_of, receiver = mixed[0:amount // 2 * 2:2], mixed[1:amount // 2 * 2:2]
    margin = jnp.minimum(sizes[source_of] - 1, reach - sizes[receiver]) // 2
    margin = jnp.where((source_of == sequence[0]) | (receiver == sequence[0]) | (sizes[receiver] == 0), 0, jnp.maximum(margin, 0))
    shifted = jax.random.randint(jax.random.fold_in(own, 4), (amount // 2,), 0, 1 << 20) % (margin + 1)
    sizes = sizes.at[source_of].add(-shifted).at[receiver].add(shifted)
    items = jnp.searchsorted(jnp.cumsum(sizes), jnp.arange(rows * top), side="right").astype(jnp.int32)
    listing = items.reshape(top, rows).T
    listing = listing[jax.random.permutation(jax.random.fold_in(own, 1), rows)]
    rotation = jax.random.randint(jax.random.fold_in(own, 2), (rows, 1), 0, top)
    return jnp.take_along_axis(listing, (jnp.arange(top)[None, :] + rotation) % top, axis=1)


def portions_of(amount, total, bound, skew, full):
    portions = [(1 << 20) // math.isqrt(rank ** skew) + 1 for rank in range(1, amount + 1)]
    largest = bound if full else min(bound, max(-(-total // amount), total * portions[0] // sum(portions)))
    least = 1 if total - largest >= amount - 1 else 0
    holding, rest = [largest] + [least] * (amount - 1), total - largest - least * (amount - 1)
    while rest > 0:
        free = [i for i in range(1, amount) if holding[i] < largest] or [i for i in range(1, amount) if holding[i] < bound]
        pool, left = sum([portions[i] for i in free]), rest
        for i in free:
            more = min(bound - holding[i], max(1, left * portions[i] // pool), rest)
            holding[i] = holding[i] + more
            rest = rest - more
    return np.array(holding)


def scatter_about(stream_key, shape, scale, most, pieces=(), kind=jnp.bfloat16):
    loudness = levels(stream_key, shape, pieces, -0.22, 0.18) if pieces else 1.0
    array = jax.random.normal(stream_key, shape, jnp.float32) * scale * loudness
    return jnp.minimum(jnp.maximum(array, -most), most).astype(kind)


def setup_inputs(seed: int = 0) -> dict:
    key_of = jax.random.split(jax.random.key(seed), 12)
    tokens = draw_tokens(jax.random.fold_in(key_of[11], 71), 0)
    norm_gain = jnp.clip(1.0 + 0.18 * jax.random.normal(key_of[1], (D,), jnp.float32), 0.1, 1.9)
    w_query = draw_w_query(jax.random.fold_in(key_of[11], 71), 0)
    w_keyval = draw_w_keyval(jax.random.fold_in(key_of[11], 71), 0)
    w_out = scatter_about(key_of[4], (HEADS * HEAD_DIM, D), (HEADS * HEAD_DIM) ** -0.5, 0.09375, ((0, 4), (1, 8)))
    residents = scatter_about(key_of[5], (CLUSTERS, MEMBERS, D), 1.0, 6.0, ((0, 8), (1, 4)))
    lengths = set_ends(jax.random.randint(key_of[6], (DIALOGUES,), LEN // 8, LEN + 1), jax.random.fold_in(key_of[6], 1), LEN // 8, LEN).astype(jnp.int32)
    cluster_keys = jax.random.split(jax.random.fold_in(key_of[7], 1), DIALOGUES // DLG_DEV)
    cluster_turns = jax.random.permutation(jax.random.fold_in(key_of[7], 3), DIALOGUES // DLG_DEV)
    cluster = jax.vmap(lambda own, number: assign_block(jax.random.fold_in(key_of[7], 2), own, number, DLG_DEV, CLUSTERS, 1, CAP, 2))(cluster_keys, cluster_turns).reshape((DIALOGUES, 1))
    owner = jax.random.permutation(key_of[8], CLUSTERS).astype(jnp.int32)
    counts = set_ends(jax.random.randint(key_of[9], (CLUSTERS,), MEMBERS // 8, MEMBERS + 1), jax.random.fold_in(key_of[9], 1), MEMBERS // 8, MEMBERS).astype(jnp.int32)
    flags = set_ends((jax.random.randint(key_of[10], (DIALOGUES,), 0, 4) < 3).astype(jnp.int32), jax.random.fold_in(key_of[10], 1), 0, 1)
    return {"tokens": tokens, "norm_gain": norm_gain, "w_query": w_query, "w_keyval": w_keyval, "w_out": w_out, "residents": residents, "lengths": lengths, "cluster": cluster, "owner": owner, "counts": counts, "flags": flags}


rope_base = 1000000.0
logit_scale = 100.0

def rotate(values, positions):
    half = values.shape[-1] // 2
    freqs = rope_base ** (-jnp.arange(half, dtype=jnp.float32) * 2.0 / values.shape[-1])
    angles = positions.astype(jnp.float32)[:, None] * freqs[None, :]
    cosine = jnp.cos(angles)[:, None, :]
    sine = jnp.sin(angles)[:, None, :]
    first = values[..., :half]
    second = values[..., half:]
    return jnp.concatenate([first * cosine - second * sine, second * cosine + first * sine], axis=-1)

def attend(query, keys, values, length):
    seq_len = query.shape[0]
    kv_count = keys.shape[1]
    group = query.shape[1] // kv_count
    grouped = query.reshape(seq_len, kv_count, group, query.shape[-1]).astype(jnp.float32)
    scores = jnp.einsum('qkgd,pkd->kgqp', grouped, keys.astype(jnp.float32)) / math.sqrt(query.shape[-1])
    row_pos = jnp.arange(seq_len)[:, None]
    col_pos = jnp.arange(seq_len)[None, :]
    allowed = (col_pos <= row_pos) & (col_pos < length)
    scores = jnp.where(allowed, scores, -1e+30)
    highest = lax.optimization_barrier(jnp.max(scores, axis=-1, keepdims=True))
    expanded = jnp.exp(scores - highest)
    weights = (expanded / lax.optimization_barrier(jnp.sum(expanded, axis=-1, keepdims=True))).astype(jnp.bfloat16)
    context = jnp.einsum('kgqp,pkd->qkgd', weights.astype(jnp.float32), values.astype(jnp.float32))
    valid = (jnp.arange(seq_len) < length).astype(jnp.float32)
    pooled = lax.optimization_barrier(jnp.sum(context * valid[:, None, None, None], axis=0)) / length.astype(jnp.float32)
    return pooled.reshape(-1)

def reference(tokens, norm_gain, w_query, w_keyval, w_out, residents, lengths, cluster, owner, counts, flags):
    keyval_flat = w_keyval.reshape(D, 2 * KV_HEADS * HEAD_DIM)
    positions = jnp.arange(LEN)

    def one_dialogue(inputs):
        dialogue, length = inputs
        hidden = dialogue.astype(jnp.float32)
        normed = (hidden * lax.rsqrt(lax.optimization_barrier(jnp.mean(hidden * hidden, axis=-1, keepdims=True)) + 1e-06) * norm_gain).astype(jnp.bfloat16)
        query = jnp.dot(normed, w_query, preferred_element_type=jnp.float32).reshape(LEN, HEADS, HEAD_DIM)
        keyval = jnp.dot(normed, keyval_flat, preferred_element_type=jnp.float32).reshape(LEN, 2, KV_HEADS, HEAD_DIM)
        query = rotate(query, positions).astype(jnp.bfloat16)
        keys = rotate(keyval[:, 0], positions).astype(jnp.bfloat16)
        values = keyval[:, 1].astype(jnp.bfloat16)
        context = attend(query, keys, values, length).astype(jnp.bfloat16)
        valid = (positions < length).astype(jnp.float32)
        pooled_input = lax.optimization_barrier(jnp.sum(hidden * valid[:, None], axis=0)) / length.astype(jnp.float32)
        return (context, pooled_input)
    pooled_context, pooled_input = lax.map(one_dialogue, (tokens, lengths))
    embedding = pooled_input + jnp.dot(pooled_context, w_out, preferred_element_type=jnp.float32)
    unit = embedding * lax.rsqrt(lax.optimization_barrier(jnp.sum(embedding * embedding, axis=-1, keepdims=True)) + 1e-06)
    unit = (unit * flags.astype(jnp.float32)[:, None]).astype(jnp.bfloat16)

    def resident_norm(members):
        wide = members.astype(jnp.float32)
        return lax.rsqrt(lax.optimization_barrier(jnp.sum(wide * wide, axis=-1)) + 1e-06)
    inverse_norm = lax.map(resident_norm, residents)
    cluster_ids = cluster[:, 0].astype(jnp.int32)
    slots = owner[cluster_ids].astype(jnp.int32)
    limits = counts[cluster_ids]

    def one_row(inputs):
        query_unit, slot, limit = inputs
        members = lax.dynamic_index_in_dim(residents, slot, 0, keepdims=False)
        dots = jnp.dot(members, query_unit, preferred_element_type=jnp.float32)
        scale_row = lax.dynamic_index_in_dim(inverse_norm, slot, 0, keepdims=False)
        live = jnp.arange(MEMBERS) < limit
        return jnp.where(live, logit_scale * dots * scale_row, 0.0)
    return lax.map(one_row, (unit, slots, limits))
```

```python
import math

import jax
import jax.numpy as jnp
import numpy as np
from jax import lax
from jax.experimental import pallas as pl
from jax.experimental.pallas import tpu as pltpu
from jax.sharding import PartitionSpec as P

HEAD_DIM = 128


rope_base = 1000000.0
logit_scale = 100.0


def rotate(values, positions):
    half = values.shape[-1] // 2
    freqs = rope_base ** (-jnp.arange(half, dtype=jnp.float32) * 2.0 / values.shape[-1])
    angles = positions.astype(jnp.float32)[:, None] * freqs[None, :]
    cosine = jnp.cos(angles)[:, None, :]
    sine = jnp.sin(angles)[:, None, :]
    first = values[..., :half]
    second = values[..., half:]
    return jnp.concatenate(
        [first * cosine - second * sine, second * cosine + first * sine], axis=-1
    )


def attend(query, keys, values, length):
    seq_len = query.shape[0]
    kv_count = keys.shape[1]
    group = query.shape[1] // kv_count
    grouped = query.reshape(seq_len, kv_count, group, query.shape[-1])
    scores = jnp.einsum(
        "qkgd,pkd->kgqp", grouped, keys, preferred_element_type=jnp.float32
    ) / math.sqrt(query.shape[-1])
    row_pos = jnp.arange(seq_len)[:, None]
    col_pos = jnp.arange(seq_len)[None, :]
    allowed = (col_pos <= row_pos) & (col_pos < length)
    scores = jnp.where(allowed, scores, -1e30)
    highest = jnp.max(scores, axis=-1, keepdims=True)
    expanded = jnp.exp(scores - highest)
    weights = (expanded / jnp.sum(expanded, axis=-1, keepdims=True)).astype(jnp.bfloat16)
    context = jnp.einsum("kgqp,pkd->qkgd", weights, values, preferred_element_type=jnp.float32)
    valid = (jnp.arange(seq_len) < length).astype(jnp.float32)
    pooled = jnp.sum(context * valid[:, None, None, None], axis=0) / length.astype(jnp.float32)
    return pooled.reshape(-1)


MESH = pl.DeviceIdType.MESH
HALF, FULL = jnp.bfloat16, jnp.float32
CHUNK = 4
NT = (((1,), (1,)), ((), ()))
Z_EXTRA = (0, 2)


def fused_kernel(
    lens, cluster, owner, counts, flags,
    tin, query_in, keyval_in, gain, w_out_in, members_in, cosine, sine,
    out,
    tok, wide, narrow, wot, members, qstage, kvstage, gcol, rs, kst, vst, qst, ctx, mask,
    pool_out, pool_in, cout, cin, sums, rows_in, joined, squares, replies, arrived,
    l_sem, ty_send, ty_recv, tc_send, tc_recv, tf_send, tf_recv, wsend, wrecv,
    o_send, o_recv, p_send, p_recv, c_send, c_recv, d_send, d_recv, f_send, f_recv,
):
    dp = lax.axis_index("dp")
    mp = lax.axis_index("mp")
    z, x = dp // 2, dp % 2
    high = z // 2
    core_peer = mp + 1 - 2 * (mp % 2)
    y_peer = (mp + 2) % 4
    far = (core_peer + 2) % 4
    pair_z = z + 1 - 2 * (z % 2)
    x_peer = 2 * z + 1 - x
    total, part = tin.shape
    depth, queries = query_in.shape
    width = tok.shape[1]
    dialogs = lens.shape[0]
    seq_len = total // dialogs
    rows_each = CHUNK * seq_len
    chunks = total // rows_each
    end = (z == 0) | (z == 3)
    mid = (z == 1) | (z == 2)

    def across(k):
        return k + high * (3 - 2 * k)

    def slot_of(kind):
        k, prime = kind
        return 2 * across(k) + (1 - x if prime else x)

    def lanes_of(m):
        return pl.ds(pl.multiple_of(m * part, 128), part)

    def rows_of(r):
        return pl.ds(pl.multiple_of(r * rows_each, 64), rows_each)

    def remote(source, target, send, recv, dp_to, mp_to):
        return pltpu.make_async_remote_copy(
            src_ref=source, dst_ref=target, send_sem=send, recv_sem=recv,
            device_id={"dp": dp_to, "mp": mp_to}, device_id_type=MESH,
        )

    load_query = pltpu.make_async_copy(query_in, qstage, l_sem.at[0])
    load_keyval = pltpu.make_async_copy(keyval_in, kvstage, l_sem.at[1])
    load_tokens = pltpu.make_async_copy(tin, tok.at[:, lanes_of(mp)], l_sem.at[2])
    load_members = pltpu.make_async_copy(members_in, members, l_sem.at[3])
    load_out = pltpu.make_async_copy(w_out_in, wot.at[:, lanes_of(mp)], l_sem.at[4])
    load_keyval.start()
    load_query.start()
    load_tokens.start()

    barrier = pltpu.get_barrier_semaphore()
    for i in range(8):
        for j in range(4):
            if i or j:
                pl.semaphore_signal(
                    barrier, inc=1, device_id={"dp": (dp + i) % 8, "mp": (mp + j) % 4},
                    device_id_type=MESH,
                )
    load_members.start()
    load_out.start()

    first = (7 * dp) // 2
    for i in range(4):
        row = gain[pl.ds(first + i, 1), :]
        gcol[i * 128 : (i + 1) * 128, :] = jnp.broadcast_to(row, (128, 128)).T
    factor = gcol[pl.ds(pl.multiple_of((dp % 2) * 64, 64), depth), :]
    own_rows = pl.ds(pl.multiple_of(dp * depth, 64), depth)
    load_keyval.wait()
    for i in range(2):
        span = slice(i * 128, (i + 1) * 128)
        wide[0, own_rows, span] = (kvstage[:, span].astype(FULL) * factor).astype(HALF)
    load_query.wait()
    for h in range(queries // 128):
        piece = (qstage[:, h * 128 : (h + 1) * 128].astype(FULL) * factor).astype(HALF)
        if h < 6:
            wide[1 + h // 2, own_rows, (h % 2) * 128 : (h % 2 + 1) * 128] = piece
        else:
            narrow[own_rows, :] = piece
    pl.semaphore_wait(barrier, 31)

    def block_ref(c, slot):
        rows = pl.ds(pl.multiple_of(slot * depth, 64), depth)
        return wide.at[c, rows, :] if c < 4 else narrow.at[rows, :]

    ways = (x_peer, 2 * pair_z + x, 2 * across(2) + x)
    own_kind = {"end": (0, 0), "mid": (1, 0)}
    sent = {"end": [], "mid": []}
    waited = {"end": set(), "mid": set()}
    every = {
        "end": [(0, 1), (1, 0), (1, 1), (2, 0), (2, 1), (3, 0), (3, 1)],
        "mid": [(0, 0), (0, 1), (1, 1), (2, 0), (2, 1), (3, 0), (3, 1)],
    }

    def weight_copy(way, c, kind):
        slot = slot_of(kind)
        return remote(
            block_ref(c, slot), block_ref(c, slot), wsend.at[way, c, slot], wrecv.at[c, slot],
            ways[way], mp,
        )

    def send(role, way, c, kind):
        sent[role].append((way, c, kind))
        weight_copy(way, c, kind).start()

    def own(role, way, c):
        send(role, way, c, own_kind[role])

    def arrive(role, c, kind):
        if (c, kind) not in waited[role]:
            waited[role].add((c, kind))
            weight_copy(0, c, kind).wait_recv()

    def onward(role, c, kind, *to):
        arrive(role, c, kind)
        for way in to:
            send(role, way, c, kind)

    def at_end(f):
        pl.when(end)(f)

    def at_mid(f):
        pl.when(mid)(f)

    def rest(c):
        @at_end
        def _():
            for kind in every["end"]:
                arrive("end", c, kind)

        @at_mid
        def _():
            for kind in every["mid"]:
                arrive("mid", c, kind)

    def y_copy(r, m):
        return remote(
            tin.at[rows_of(r), :], tok.at[rows_of(r), lanes_of(m)], ty_send.at[r], ty_recv.at[r],
            dp, y_peer,
        )

    def forward_copy(r, m):
        return remote(
            tok.at[rows_of(r), lanes_of(m)], tok.at[rows_of(r), lanes_of(m)],
            tf_send.at[r], tf_recv.at[r], dp, core_peer,
        )

    def core_copy(m):
        return remote(tin, tok.at[:, lanes_of(m)], tc_send, tc_recv, dp, core_peer)

    def relay_tokens(r):
        y_copy(r, y_peer).wait_recv()
        forward_copy(r, y_peer).start()

    def out_copy(i, m, mp_to):
        return remote(
            wot.at[:, lanes_of(m)], wot.at[:, lanes_of(m)], o_send.at[i], o_recv.at[i], dp, mp_to
        )

    y_copy(0, mp).start()

    @at_end
    def _():
        for c in range(4):
            own("end", 0, c)
            own("end", 1, c)
        own("end", 1, 4)

    @at_mid
    def _():
        for c in range(2):
            own("mid", 1, c)
            own("mid", 0, c)
            own("mid", 2, c)
        for c in range(2, 5):
            own("mid", 0, c)

    for r in range(1, chunks):
        y_copy(r, mp).start()
    core_copy(mp).start()

    lane = lax.broadcasted_iota(jnp.int32, (dialogs, 128), 1)
    sub = lax.broadcasted_iota(jnp.int32, (dialogs, 128), 0)
    lane_dialog = CHUNK * (lane // 8) + lane % CHUNK
    to_col = jnp.zeros((dialogs, 128), jnp.int32)
    to_row = jnp.full((dialogs, 128), -64, jnp.int32)
    to_wide = jnp.full((dialogs, 128), -64, jnp.int32)
    len_col = jnp.zeros((dialogs, 128), jnp.int32)
    flag_col = jnp.zeros((dialogs, 128), jnp.int32)
    for d in range(dialogs):
        target = owner[cluster[d]]
        to_col = jnp.where(sub == d, target, to_col)
        to_row = jnp.where(lane == d, target, to_row)
        to_wide = jnp.where((lane_dialog == d) & (lane < 64), target, to_wide)
        len_col = jnp.where(sub == d, lens[d], len_col)
        flag_col = jnp.where(sub == d, flags[d], flag_col)
    len_col = len_col.astype(FULL)
    flag_col = flag_col.astype(FULL)
    rank_col = jnp.sum(
        jnp.where((to_col == to_row) & (lane < sub), 1.0, 0.0), axis=1, keepdims=True
    )
    rank_row = jnp.sum(
        jnp.where((to_col == to_row) & (sub < lane), 1.0, 0.0), axis=0, keepdims=True
    )
    rank_wide = jnp.sum(
        jnp.where((to_col == to_wide) & (sub < lane_dialog), 1.0, 0.0), axis=0, keepdims=True
    )
    slot_row = to_row[0:1].astype(FULL) * CHUNK + rank_row
    slot_wide = to_wide[0:1].astype(FULL) * CHUNK + rank_wide
    reply_place = to_col[:, 0:1].astype(FULL) * 16.0 + rank_col
    place = lax.broadcasted_iota(jnp.int32, (64, 128), 0)
    place_lane = lax.broadcasted_iota(jnp.int32, (64, 128), 1)
    upper = place % 16 < 8
    held = ((place // 16) * 8 + place % 8).astype(FULL)
    pool_pick = jnp.where(upper & (held == slot_row), 1.0, 0.0).astype(HALF)[:, :dialogs]

    index = lax.broadcasted_iota(jnp.int32, mask.shape, 1)
    start = lax.broadcasted_iota(jnp.int32, mask.shape, 0) * seq_len
    ahead = (index - start).astype(FULL)
    mask[...] = jnp.where((ahead >= 0.0) & (ahead < len_col[:, 0:1]), 1.0, 0.0).astype(HALF)
    load_tokens.wait()
    mean = jnp.dot(mask[...], tok[:, lanes_of(mp)], preferred_element_type=FULL) / len_col[:, 0:1]
    picked = jnp.dot(pool_pick, mean.astype(HALF), preferred_element_type=FULL).astype(HALF)
    pool_out[0] = picked[:, : part // 2].reshape(pool_out.shape[1:])
    pool_out[1] = picked[:, part // 2 :].reshape(pool_out.shape[1:])

    def pool_copy(j, m, source):
        return remote(
            pool_out.at[j, m], pool_in.at[source], p_send.at[j, m], p_recv.at[source],
            2 * mp + j, m,
        )

    for j in range(2):
        for m in range(4):
            mine = (2 * mp + j == dp) & (mp == m)

            @pl.when(jnp.logical_not(mine))
            def _():
                pool_copy(j, m, dp).start()

            @pl.when(mine)
            def _():
                pool_in[dp] = pool_out[j, m]

    def normalize(r):
        for half in range(2):
            rows = pl.ds(pl.multiple_of(r * rows_each + half * (rows_each // 2), 32), rows_each // 2)
            values = tok[rows, :].astype(FULL)
            mean_square = jnp.sum(values * values, axis=-1, keepdims=True) * (1.0 / width)
            rs[rows, :] = jnp.broadcast_to(lax.rsqrt(mean_square + 1e-06), (rows_each // 2, 128))

    def turn(piece):
        return piece * cosine[...] + pltpu.roll(piece, HEAD_DIM // 2, 1) * sine[...]

    def keyval_rows(r):
        forward_copy(r, far).wait_recv()
        normalize(r)
        rows = rows_of(r)
        product = jnp.dot(tok[rows, :], wide[0], preferred_element_type=FULL)
        kst[rows, :] = turn(product[:, :HEAD_DIM] * rs[rows, :]).astype(HALF)
        vst[rows, :] = (product[:, HEAD_DIM:] * rs[rows, :]).astype(HALF)

    def query_rows(c, r, slot):
        rows = rows_of(r)
        weights = wide[c] if c < 4 else narrow[...]
        product = jnp.dot(tok[rows, :], weights, preferred_element_type=FULL)
        for h in range(product.shape[1] // HEAD_DIM):
            span = slice(h * HEAD_DIM, (h + 1) * HEAD_DIM)
            qst[slot, :, span] = turn(product[:, span] * rs[rows, :]).astype(HALF)

    def attend_rows(c, r, slot):
        heads = 2 if c < 4 else 1
        lanes = heads * seq_len
        key_pos = lax.broadcasted_iota(jnp.int32, (seq_len, lanes), 0)
        query_pos = lax.broadcasted_iota(jnp.int32, (seq_len, lanes), 1) % seq_len
        causal = key_pos <= query_pos
        position = lax.broadcasted_iota(jnp.int32, (1, lanes), 1) % seq_len
        pieces = []
        for item in range(CHUNK):
            here = slice(item * seq_len, (item + 1) * seq_len)
            keys = kst[pl.ds(pl.multiple_of(r * rows_each + item * seq_len, 16), seq_len), :]
            stacked = qst[slot, here, :HEAD_DIM]
            if heads == 2:
                stacked = jnp.concatenate([stacked, qst[slot, here, HEAD_DIM:]], axis=0)
            scores = lax.dot_general(keys, stacked, NT, preferred_element_type=FULL)
            scores = jnp.where(causal, scores * (1.0 / math.sqrt(HEAD_DIM)), -1e30)
            expanded = jnp.exp(scores - jnp.max(scores, axis=0, keepdims=True))
            length = lens[r * CHUNK + item]
            share = jnp.where(position < length, 1.0, 0.0) / (
                jnp.sum(expanded, axis=0, keepdims=True)
                * jnp.full((1, lanes), length, jnp.int32).astype(FULL)
            )
            pieces.append((expanded * share).astype(HALF))
        weights = jnp.concatenate(pieces, axis=0)
        head_row = lax.broadcasted_iota(jnp.int32, (8, lanes), 0) // CHUNK
        head_lane = lax.broadcasted_iota(jnp.int32, (8, lanes), 1) // seq_len
        chosen = jnp.where(head_row == head_lane, 1.0, 0.0).astype(HALF)
        sums_of = lax.dot_general(chosen, weights, NT, preferred_element_type=FULL)
        item_row = lax.broadcasted_iota(jnp.int32, sums_of.shape, 0) % CHUNK
        item_lane = lax.broadcasted_iota(jnp.int32, sums_of.shape, 1) // seq_len
        sums_of = jnp.where(item_row == item_lane, sums_of, 0.0)
        coarse = sums_of.astype(HALF).astype(FULL)
        both = jnp.concatenate([coarse, sums_of - coarse], axis=0).astype(HALF)
        mixed = jnp.dot(both, vst[rows_of(r), :], preferred_element_type=FULL)
        ctx[c - 1, r] = mixed[:8] + mixed[8:]

    def query_block(c, low, top):
        query_rows(c, low, low % 2)

        @pl.loop(low + 1, top)
        def _(r):
            query_rows(c, r, r % 2)
            attend_rows(c, r - 1, (r - 1) % 2)

        attend_rows(c, top - 1, (top - 1) % 2)

    def member_squares(low, top):
        @pl.loop(low, top)
        def _(step):
            rows = pl.ds(pl.multiple_of(step * 64, 64), 64)
            values = members[rows, :].astype(FULL)
            squares[rows, :] = jnp.broadcast_to(
                jnp.sum(values * values, axis=-1, keepdims=True), (64, 128)
            )

    @at_mid
    def _():
        onward("mid", 0, (1, 1), 1)
        onward("mid", 0, (0, 0), 2)
        own("mid", 2, 2)
        onward("mid", 0, (2, 0), 1, 0)

    @at_end
    def _():
        onward("end", 0, (0, 1), 1)

    load_members.wait()
    member_squares(0, 4)

    @at_mid
    def _():
        onward("mid", 1, (0, 0), 2)
        own("mid", 2, 3)

    @at_end
    def _():
        onward("end", 1, (0, 1), 1)
        onward("end", 1, (1, 0), 0)

    member_squares(4, 8)
    relay_tokens(0)

    @at_mid
    def _():
        onward("mid", 0, (3, 0), 1, 0)
        own("mid", 1, 2)
        onward("mid", 1, (2, 0), 1, 0)
        onward("mid", 2, (0, 0), 2)
        own("mid", 2, 4)

    @at_end
    def _():
        onward("end", 2, (0, 1), 1)

    relay_tokens(1)

    @at_mid
    def _():
        onward("mid", 3, (0, 0), 2)

    @at_end
    def _():
        onward("end", 3, (0, 1), 1)
        onward("end", 0, (2, 0), 0)

    relay_tokens(2)

    @at_mid
    def _():
        onward("mid", 1, (3, 0), 1, 0)
        own("mid", 1, 3)
        onward("mid", 2, (1, 1), 1)
        onward("mid", 2, (2, 0), 1, 0)
        onward("mid", 4, (0, 0), 2)

    @at_end
    def _():
        onward("end", 0, (3, 0), 0)
        own("end", 0, 4)
        onward("end", 4, (0, 1), 1)

    relay_tokens(3)

    @at_mid
    def _():
        onward("mid", 2, (3, 0), 1, 0)
        own("mid", 1, 4)
        onward("mid", 3, (2, 0), 1, 0)

    @at_end
    def _():
        onward("end", 1, (2, 0), 0)

    rest(0)
    core_copy(core_peer).wait_recv()
    keyval_rows(0)
    keyval_rows(1)

    @at_end
    def _():
        onward("end", 1, (3, 0), 0)

    relay_tokens(4)
    keyval_rows(2)
    keyval_rows(3)

    @at_mid
    def _():
        onward("mid", 3, (3, 0), 1, 0)
        onward("mid", 4, (2, 0), 1, 0)

    @at_end
    def _():
        onward("end", 3, (1, 0), 0)

    relay_tokens(5)
    keyval_rows(4)

    @at_mid
    def _():
        onward("mid", 4, (3, 0), 1, 0)

    rest(1)
    query_block(1, 0, 4)
    relay_tokens(6)
    load_out.wait()
    own_out = out_copy(0, mp, y_peer)
    own_out.start()
    beside_out = out_copy(1, mp, core_peer)
    beside_out.start()
    keyval_rows(5)

    @at_end
    def _():
        onward("end", 2, (2, 0), 0)

    keyval_rows(6)
    relay_tokens(7)

    @at_end
    def _():
        onward("end", 2, (3, 0), 0)

    keyval_rows(7)
    query_block(1, 4, 8)

    @at_end
    def _():
        onward("end", 4, (1, 0), 0)
        onward("end", 3, (2, 0), 0)

    rest(2)
    query_block(2, 0, 4)

    @at_end
    def _():
        onward("end", 3, (3, 0), 0)

    query_block(2, 4, 8)

    @at_end
    def _():
        onward("end", 4, (2, 0), 0)
        onward("end", 4, (3, 0), 0)

    limit = counts[0] * 0
    for c in range(counts.shape[0]):
        limit = limit + jnp.where(owner[c] == dp, counts[c], 0)
    member_count = members.shape[0]
    member = mp * member_count + lax.broadcasted_iota(jnp.int32, (1, member_count), 1)
    scale = jnp.where(member < limit, logit_scale, 0.0) * lax.rsqrt(squares[...].T[0:1, :] + 1e-06)
    rest(3)
    query_block(3, 0, 8)
    out_copy(0, y_peer, y_peer).wait_recv()
    onward_out = out_copy(2, y_peer, core_peer)
    onward_out.start()
    rest(4)
    query_block(4, 0, 8)

    lane_head = (place_lane // CHUNK) % 2

    def pick(h):
        right = (upper if h < 4 else jnp.logical_not(upper)) & (lane_head == h % 2)
        return jnp.where(right & (held == slot_wide), 1.0, 0.0).astype(HALF)[:, :64]

    for block in range(4):
        value = jnp.zeros((64, 128), FULL)
        for h in (block, block + 4):
            if h < 7:
                rows = ctx[h // 2].reshape(64, 128).astype(HALF)
                value = value + jnp.dot(pick(h), rows, preferred_element_type=FULL)
        cout[:, :, block * 128 : (block + 1) * 128] = value.astype(HALF).reshape(4, 16, 128)

    def context_copy(i, j, m_slot, d_slot):
        to = (mp + j) % 4
        return remote(
            cout.at[to], cin.at[m_slot, d_slot], c_send.at[i, j], c_recv.at[m_slot, d_slot],
            (dp + i) % 8, to,
        )

    partners = [(i, j) for i in range(8) for j in range(4) if i or j]
    for i, j in sorted(partners, key=lambda ij: -abs(ij[0] - 4) * 0 + (ij[0] in (0, 1, 7))):
        context_copy(i, j, mp, dp).start()
    cin[mp, dp] = cout[mp]
    out_copy(1, core_peer, core_peer).wait_recv()
    out_copy(2, far, core_peer).wait_recv()
    for source in range(8):
        @pl.when(jnp.logical_not((dp // 2 == mp) & (dp == source)))
        def _():
            pool_copy(0, 0, source).wait_recv()

    half_out = wot.shape[0]
    total_a = jnp.zeros((128, half_out), FULL)
    total_b = jnp.zeros((128, half_out), FULL)
    for j in range(4):
        m = (mp + j) % 4
        for i in range(8):
            if i or j:
                context_copy(i, j, m, (dp + i) % 8).wait_recv()
        have = cin[m].reshape(128, 512)
        total_a = total_a + lax.dot_general(
            have, wot[:, pl.ds(pl.multiple_of(m * part, 128), 512)], NT,
            preferred_element_type=FULL,
        )
        total_b = total_b + lax.dot_general(
            have[:, : part - 512],
            wot[:, pl.ds(pl.multiple_of(m * part + 512, 128), part - 512)], NT,
            preferred_element_type=FULL,
        )
    embedded = (
        total_a.reshape(8, 16, half_out)[:, :8]
        + total_b.reshape(8, 16, half_out)[:, 8:]
        + pool_in[...].astype(FULL)[:, :8]
    ).reshape(64, half_out)
    row = lax.broadcasted_iota(jnp.int32, (64, 64), 0)
    column = lax.broadcasted_iota(jnp.int32, (64, 64), 1)
    order = jnp.where(
        column == ((row // 4) % 8) * 8 + (row // 32) * 4 + row % 4, 1.0, 0.0
    ).astype(HALF)
    sums[...] = (
        jnp.dot(order, embedded.astype(HALF), preferred_element_type=FULL)
        .astype(HALF)
        .reshape(sums.shape)
    )

    def sum_copy(j, i, slot):
        return remote(
            sums.at[j], rows_in.at[slot], d_send.at[j, i], d_recv.at[slot],
            2 * mp + j, (mp + i) % 4,
        )

    for j in range(2):
        mine = 2 * mp + j == dp
        for i in range(1, 4):
            sum_copy(j, i, dp).start()

        @pl.when(jnp.logical_not(mine))
        def _():
            sum_copy(j, 0, dp).start()

        @pl.when(mine)
        def _():
            rows_in[dp] = sums[j]

    for slot in range(8):
        @pl.when(jnp.logical_not((dp // 2 == mp) & (dp == slot)))
        def _():
            sum_copy(0, 0, slot).wait_recv()

    for slot in range(8):
        joined[:, slot * half_out : (slot + 1) * half_out] = rows_in[slot].astype(FULL)
    embedding = joined[...]
    dots = lax.dot_general(
        embedding.astype(HALF), members[...], NT, preferred_element_type=FULL
    )
    inverse = lax.rsqrt(jnp.sum(embedding * embedding, axis=-1, keepdims=True) + 1e-06)
    found = (dots * inverse * scale).astype(HALF)
    row = lax.broadcasted_iota(jnp.int32, (128, 32), 0)
    column = lax.broadcasted_iota(jnp.int32, (128, 32), 1)
    value = jnp.zeros((128, 128), FULL)
    for q in range(4):
        spread = jnp.where(
            ((row % 16) // 4 == q) & (column == (row // 16) * 4 + row % 4), 1.0, 0.0
        ).astype(HALF)
        value = value + jnp.dot(
            spread, found[:, q * 128 : (q + 1) * 128], preferred_element_type=FULL
        )
    replies[...] = value.astype(HALF).reshape(replies.shape)

    def reply_copy(i, slot):
        to = (dp + i) % 8
        return remote(replies.at[to], arrived.at[slot], f_send.at[i], f_recv.at[slot], to, mp)

    for i in range(1, 8):
        reply_copy(i, dp).start()
    arrived[dp] = replies[dp]
    for i in range(1, 8):
        reply_copy(i, (dp + i) % 8).wait_recv()
    have = arrived[...].reshape(128, 128)
    column = lax.broadcasted_iota(jnp.int32, (dialogs, 128), 1).astype(FULL)
    for q in range(4):
        fetch = jnp.where(column == reply_place + 4.0 * q, flag_col, 0.0).astype(HALF)
        out[:, q * 128 : (q + 1) * 128] = jnp.dot(fetch, have, preferred_element_type=FULL)

    for r in range(chunks):
        y_copy(r, mp).wait_send()
        forward_copy(r, y_peer).wait_send()
    core_copy(mp).wait_send()
    own_out.wait_send()
    beside_out.wait_send()
    onward_out.wait_send()

    @at_end
    def _():
        for way, c, kind in sent["end"]:
            weight_copy(way, c, kind).wait_send()

    @at_mid
    def _():
        for way, c, kind in sent["mid"]:
            weight_copy(way, c, kind).wait_send()

    for j in range(2):
        for m in range(4):
            @pl.when(jnp.logical_not((2 * mp + j == dp) & (mp == m)))
            def _():
                pool_copy(j, m, dp).wait_send()

        @pl.when(2 * mp + j != dp)
        def _():
            sum_copy(j, 0, dp).wait_send()

        for i in range(1, 4):
            sum_copy(j, i, dp).wait_send()
    for i, j in partners:
        context_copy(i, j, mp, dp).wait_send()
    for i in range(1, 8):
        reply_copy(i, dp).wait_send()


def fused(
    tokens, norm_gain, w_query, w_keyval, w_out, residents, lengths, cluster, owner, counts, flags
):
    dialogs, seq_len, part = tokens.shape
    total = dialogs * seq_len
    depth, queries = w_query.shape
    width = norm_gain.shape[0]
    member_count = residents.shape[1]
    half_out = w_out.shape[1]
    half = HEAD_DIM // 2
    freqs = rope_base ** (-np.arange(half, dtype=np.float64) * 2.0 / HEAD_DIM)
    angles = np.arange(seq_len, dtype=np.float64)[:, None] * freqs[None, :]
    cosine, sine = np.cos(angles), np.sin(angles)
    cosine = np.tile(np.concatenate([cosine, cosine], axis=1), (CHUNK, 1)).astype(np.float32)
    sine = np.tile(np.concatenate([-sine, sine], axis=1), (CHUNK, 1)).astype(np.float32)
    vmem = pl.BlockSpec(memory_space=pltpu.VMEM)
    smem = pl.BlockSpec(memory_space=pltpu.SMEM)
    hbm = pl.BlockSpec(memory_space=pltpu.HBM)
    sem = pltpu.SemaphoreType.DMA
    return pl.pallas_call(
        fused_kernel,
        out_shape=jax.ShapeDtypeStruct((dialogs, member_count), FULL),
        in_specs=[smem] * 5 + [hbm, hbm, hbm, vmem, hbm, hbm, vmem, vmem],
        out_specs=vmem,
        scratch_shapes=[
            pltpu.VMEM((total, width), HALF),
            pltpu.VMEM((4, width, 256), HALF),
            pltpu.VMEM((width, 128), HALF),
            pltpu.VMEM((half_out, width), HALF),
            pltpu.VMEM((member_count, width), HALF),
            pltpu.VMEM((depth, queries), HALF),
            pltpu.VMEM((depth, 256), HALF),
            pltpu.VMEM((512, 128), FULL),
            pltpu.VMEM((total, 128), FULL),
            pltpu.VMEM((total, 128), HALF),
            pltpu.VMEM((total, 128), HALF),
            pltpu.VMEM((2, CHUNK * seq_len, 256), HALF),
            pltpu.VMEM((4, 8, 8, 128), FULL),
            pltpu.VMEM((dialogs, total), HALF),
            pltpu.VMEM((2, 4, 16, half_out), HALF),
            pltpu.VMEM((8, 16, half_out), HALF),
            pltpu.VMEM((4, 16, 512), HALF),
            pltpu.VMEM((4, 8, 16, 512), HALF),
            pltpu.VMEM((2, 32, half_out), HALF),
            pltpu.VMEM((8, 32, half_out), HALF),
            pltpu.VMEM((32, width), FULL),
            pltpu.VMEM((member_count, 128), FULL),
            pltpu.VMEM((8, 16, 128), HALF),
            pltpu.VMEM((8, 16, 128), HALF),
            sem((5,)),
            sem((8,)),
            sem((8,)),
            sem,
            sem,
            sem((8,)),
            sem((8,)),
            sem((3, 5, 8)),
            sem((5, 8)),
            sem((3,)),
            sem((3,)),
            sem((2, 4)),
            sem((8,)),
            sem((8, 4)),
            sem((4, 8)),
            sem((2, 4)),
            sem((8,)),
            sem((8,)),
            sem((8,)),
        ],
        compiler_params=pltpu.CompilerParams(
            collective_id=0, has_side_effects=True, vmem_limit_bytes=58 * 1024 * 1024
        ),
    )(
        lengths, cluster[:, 0], owner, counts, flags,
        tokens.reshape(total, part), w_query, w_keyval.reshape(depth, -1),
        norm_gain.reshape(-1, 128), w_out.T, residents[0], cosine, sine,
    )


def plain_project(tokens, norm_gain, w_query, w_keyval, lengths):
    gathered = lax.all_gather(tokens, "mp", axis=2, tiled=True)
    dialogs, seq_len, width = gathered.shape
    hidden = gathered.astype(jnp.float32)
    normed = (
        hidden * lax.rsqrt(jnp.mean(hidden * hidden, axis=-1, keepdims=True) + 1e-06) * norm_gain
    ).astype(jnp.bfloat16)
    normed_flat = normed.reshape(dialogs * seq_len, width)
    query_cols = w_query.shape[1]
    keyval_cols = w_keyval.shape[2]
    pieces = (
        lax.all_gather(w_query, "dp", axis=0, tiled=True),
        lax.all_gather(w_keyval, "dp", axis=0, tiled=True),
    )
    keyval_piece = pieces[1].reshape(pieces[1].shape[0], 2 * keyval_cols)
    query_sum = jnp.dot(normed_flat, pieces[0], preferred_element_type=jnp.float32)
    keyval_sum = jnp.dot(normed_flat, keyval_piece, preferred_element_type=jnp.float32)
    positions = jnp.arange(seq_len)
    local_heads = query_cols // HEAD_DIM
    local_kv = keyval_cols // HEAD_DIM
    query = jax.vmap(lambda block: rotate(block, positions))(
        query_sum.reshape(dialogs, seq_len, local_heads, HEAD_DIM)
    ).astype(jnp.bfloat16)
    keys = jax.vmap(lambda block: rotate(block, positions))(
        keyval_sum[:, :keyval_cols].reshape(dialogs, seq_len, local_kv, HEAD_DIM)
    ).astype(jnp.bfloat16)
    values = (
        keyval_sum[:, keyval_cols:]
        .reshape(dialogs, seq_len, local_kv, HEAD_DIM)
        .astype(jnp.bfloat16)
    )
    valid = (positions[None, :] < lengths[:, None]).astype(jnp.float32)
    pooled_input = (
        jnp.sum(hidden * valid[:, :, None], axis=1) / lengths.astype(jnp.float32)[:, None]
    )
    pooled_context = jax.vmap(attend)(query, keys, values, lengths).astype(jnp.bfloat16)
    return pooled_context, pooled_input


def plain_score(pooled_context, pooled_input, w_out, members, onehot, live):
    dialogs = pooled_context.shape[0]
    everyone = lax.all_gather(pooled_context, "dp", axis=0, tiled=True)
    slices = jnp.dot(everyone, w_out, preferred_element_type=jnp.float32).astype(jnp.bfloat16)
    slices = slices.reshape(-1, dialogs, w_out.shape[1])
    slices = lax.all_to_all(slices, "dp", split_axis=0, concat_axis=0, tiled=True)
    partial_out = slices.transpose(1, 0, 2).reshape(dialogs, -1)
    projected = lax.psum(partial_out, "mp").astype(jnp.float32)
    embedding = pooled_input + projected
    unit = embedding * lax.rsqrt(jnp.sum(embedding * embedding, axis=-1, keepdims=True) + 1e-06)
    unit = unit.astype(jnp.bfloat16)
    inverse_norm = lax.rsqrt(
        jnp.einsum("md,md->m", members, members, preferred_element_type=jnp.float32) + 1e-06
    )
    outgoing = jnp.einsum(
        "ocn,nd->ocd", onehot.astype(jnp.bfloat16), unit, preferred_element_type=jnp.float32
    ).astype(jnp.bfloat16)
    query_rows = lax.all_to_all(outgoing, "dp", split_axis=0, concat_axis=0, tiled=True)
    dots = lax.dot_general(
        query_rows,
        members,
        (((query_rows.ndim - 1,), (1,)), ((), ())),
        preferred_element_type=jnp.float32,
    )
    return lax.all_to_all(
        jnp.where(live[0] > 0, live[0] * dots * inverse_norm, 0.0).astype(jnp.bfloat16),
        "dp",
        split_axis=0,
        concat_axis=0,
        tiled=True,
    )


def general(
    tokens, norm_gain, w_query, w_keyval, w_out, residents, lengths, cluster, owner, counts, flags
):
    pooled_context, pooled_input = plain_project(tokens, norm_gain, w_query, w_keyval, lengths)
    dialogs = tokens.shape[0]
    my_index = lax.axis_index("dp")
    owner_count = lax.axis_size("dp")
    my_count = jnp.sum(jnp.where(owner == my_index, counts, 0))
    members = residents[0]
    member_count = members.shape[0]
    member_start = lax.axis_index("mp") * member_count
    live = jnp.where(member_start + jnp.arange(member_count) < my_count, logit_scale, 0.0)[None, :]
    table_size = owner.shape[0]
    cluster_ids = cluster[:, 0]
    destination = jnp.sum(
        jnp.where(jnp.arange(table_size)[None, :] == cluster_ids[:, None], owner[None, :], 0),
        axis=1,
    )
    capacity = max(1, -(-dialogs // owner_count))
    order = jnp.arange(dialogs)
    earlier = (destination[None, :] == destination[:, None]) & (order[None, :] < order[:, None])
    rank = jnp.sum(earlier.astype(jnp.int32), axis=1)
    onehot = (jnp.arange(owner_count)[:, None, None] == destination[None, None, :]) & (
        jnp.arange(capacity)[None, :, None] == rank[None, None, :]
    )
    returned = plain_score(pooled_context, pooled_input, w_out, members, onehot, live)
    similarity = jnp.einsum(
        "ocn,ocm->nm", onehot.astype(jnp.bfloat16), returned, preferred_element_type=jnp.float32
    )
    return similarity * flags.astype(jnp.float32)[:, None]


def local(*args):
    if lax.axis_size("dp") == 8 and lax.axis_size("mp") == 4:
        return fused(*args)
    return general(*args)


def solution(mesh):
    in_specs = (
        P("dp", None, "mp"),
        P(),
        P("dp", "mp"),
        P("dp", None, "mp"),
        P("mp", "dp"),
        P("dp", "mp"),
        P("dp"),
        P("dp"),
        P(),
        P(),
        P("dp"),
    )
    out_specs = P("dp", "mp")
    return jax.shard_map(local, mesh=mesh, in_specs=in_specs, out_specs=out_specs, check_vma=False)
```

```python
import math

import jax
import jax.numpy as jnp
import numpy as np
from jax import lax
from jax.experimental import pallas as pl
from jax.experimental.pallas import tpu as pltpu
from jax.sharding import PartitionSpec as P

HEAD_DIM = 128


rope_base = 1000000.0
logit_scale = 100.0


def rotate(values, positions):
    half = values.shape[-1] // 2
    freqs = rope_base ** (-jnp.arange(half, dtype=jnp.float32) * 2.0 / values.shape[-1])
    angles = positions.astype(jnp.float32)[:, None] * freqs[None, :]
    cosine = jnp.cos(angles)[:, None, :]
    sine = jnp.sin(angles)[:, None, :]
    first = values[..., :half]
    second = values[..., half:]
    return jnp.concatenate(
        [first * cosine - second * sine, second * cosine + first * sine], axis=-1
    )


def attend(query, keys, values, length):
    seq_len = query.shape[0]
    kv_count = keys.shape[1]
    group = query.shape[1] // kv_count
    grouped = query.reshape(seq_len, kv_count, group, query.shape[-1])
    scores = jnp.einsum(
        "qkgd,pkd->kgqp", grouped, keys, preferred_element_type=jnp.float32
    ) / math.sqrt(query.shape[-1])
    row_pos = jnp.arange(seq_len)[:, None]
    col_pos = jnp.arange(seq_len)[None, :]
    allowed = (col_pos <= row_pos) & (col_pos < length)
    scores = jnp.where(allowed, scores, -1e30)
    highest = jnp.max(scores, axis=-1, keepdims=True)
    expanded = jnp.exp(scores - highest)
    weights = (expanded / jnp.sum(expanded, axis=-1, keepdims=True)).astype(jnp.bfloat16)
    context = jnp.einsum("kgqp,pkd->qkgd", weights, values, preferred_element_type=jnp.float32)
    valid = (jnp.arange(seq_len) < length).astype(jnp.float32)
    pooled = jnp.sum(context * valid[:, None, None, None], axis=0) / length.astype(jnp.float32)
    return pooled.reshape(-1)


MESH = pl.DeviceIdType.MESH
HALF, FULL = jnp.bfloat16, jnp.float32
CHUNK = 4
GROUP = 8
NT = (((1,), (1,)), ((), ()))


def fused_kernel(
    lens, cluster, owner, counts, flags,
    tin, query_in, keyval_in, gain, w_out_in, members_in, cosine, sine,
    out,
    tok, wide, narrow, wot, members, qstage, kvstage, gcol, rs, kst, vst, qst, ctx, mask,
    pool_out, pool_in, cout, cin, sums, rows_in, joined, squares, replies, arrived,
    l_sem, ty_send, ty_recv, tc_send, tc_recv, tf_send, tf_recv, wsend, wrecv,
    o_send, o_recv, p_send, p_recv, c_send, c_recv, d_send, d_recv, f_send, f_recv,
):
    dp = lax.axis_index("dp")
    mp = lax.axis_index("mp")
    z, x = dp // 2, dp % 2
    high = z // 2
    core_peer = mp + 1 - 2 * (mp % 2)
    y_peer = (mp + 2) % 4
    far = (core_peer + 2) % 4
    pair_z = z + 1 - 2 * (z % 2)
    x_peer = 2 * z + 1 - x
    total, part = tin.shape
    depth, queries = query_in.shape
    width = tok.shape[1]
    dialogs = lens.shape[0]
    seq_len = total // dialogs
    rows_each = CHUNK * seq_len
    chunks = total // rows_each
    end = (z == 0) | (z == 3)
    mid = (z == 1) | (z == 2)

    def across(k):
        return k + high * (3 - 2 * k)

    def slot_of(kind):
        k, prime = kind
        return 2 * across(k) + (1 - x if prime else x)

    def lanes_of(m):
        return pl.ds(pl.multiple_of(m * part, 128), part)

    def rows_of(r):
        return pl.ds(pl.multiple_of(r * rows_each, 64), rows_each)

    def remote(source, target, send, recv, dp_to, mp_to):
        return pltpu.make_async_remote_copy(
            src_ref=source, dst_ref=target, send_sem=send, recv_sem=recv,
            device_id={"dp": dp_to, "mp": mp_to}, device_id_type=MESH,
        )

    load_query = pltpu.make_async_copy(query_in, qstage, l_sem.at[0])
    load_keyval = pltpu.make_async_copy(keyval_in, kvstage, l_sem.at[1])
    load_tokens = pltpu.make_async_copy(tin, tok.at[:, lanes_of(mp)], l_sem.at[2])
    load_members = pltpu.make_async_copy(members_in, members, l_sem.at[3])
    load_out = pltpu.make_async_copy(w_out_in, wot.at[:, lanes_of(mp)], l_sem.at[4])
    load_keyval.start()
    load_query.start()

    barrier = pltpu.get_barrier_semaphore()

    def greet(dp_to, mp_to):
        pl.semaphore_signal(
            barrier, inc=1, device_id={"dp": dp_to, "mp": mp_to}, device_id_type=MESH
        )

    greet(dp, core_peer)
    greet(dp, y_peer)
    greet(x_peer, mp)
    greet(2 * pair_z + x, mp)

    @pl.when(mid)
    def _():
        greet(2 * across(2) + x, mp)

    load_tokens.start()
    load_members.start()
    load_out.start()

    first = (7 * dp) // 2
    for i in range(4):
        row = gain[pl.ds(first + i, 1), :]
        gcol[i * 128 : (i + 1) * 128, :] = jnp.broadcast_to(row, (128, 128)).T
    own_rows = pl.ds(pl.multiple_of(dp * depth, 64), depth)

    def gained(piece):
        factor = gcol[pl.ds(pl.multiple_of((dp % 2) * 64, 64), depth), :]
        return (piece.astype(FULL) * factor).astype(HALF)

    def fill_keyval():
        for i in range(2):
            wide[0, own_rows, i * 128 : (i + 1) * 128] = gained(kvstage[:, i, :])

    def fill_query(c):
        for h in range(2 * c - 2, min(2 * c, 7)):
            piece = gained(qstage[:, h * 128 : (h + 1) * 128])
            if h < 6:
                wide[c, own_rows, (h % 2) * 128 : (h % 2 + 1) * 128] = piece
            else:
                narrow[own_rows, :] = piece

    load_keyval.wait()
    fill_keyval()

    @pl.when(end)
    def _():
        pl.semaphore_wait(barrier, 4)

    @pl.when(mid)
    def _():
        pl.semaphore_wait(barrier, 5)

    def block_ref(c, slot):
        rows = pl.ds(pl.multiple_of(slot * depth, 64), depth)
        return wide.at[c, rows, :] if c < 4 else narrow.at[rows, :]

    ways = (x_peer, 2 * pair_z + x, 2 * across(2) + x)
    own_kind = {"end": (0, 0), "mid": (1, 0)}
    sent = {"end": [], "mid": []}
    waited = {"end": set(), "mid": set()}
    every = {
        "end": [(0, 1), (1, 0), (1, 1), (2, 0), (2, 1), (3, 0), (3, 1)],
        "mid": [(0, 0), (0, 1), (1, 1), (2, 0), (2, 1), (3, 0), (3, 1)],
    }

    def weight_copy(way, c, kind):
        slot = slot_of(kind)
        return remote(
            block_ref(c, slot), block_ref(c, slot), wsend.at[way, c, slot], wrecv.at[c, slot],
            ways[way], mp,
        )

    def send(role, way, c, kind):
        sent[role].append((way, c, kind))
        weight_copy(way, c, kind).start()

    def own(role, way, c):
        send(role, way, c, own_kind[role])

    def arrive(role, c, kind):
        if (c, kind) not in waited[role]:
            waited[role].add((c, kind))
            weight_copy(0, c, kind).wait_recv()

    def onward(role, c, kind, *to):
        arrive(role, c, kind)
        for way in to:
            send(role, way, c, kind)

    def at_end(f):
        pl.when(end)(f)

    def at_mid(f):
        pl.when(mid)(f)

    def rest(c):
        @at_end
        def _():
            for kind in every["end"]:
                arrive("end", c, kind)

        @at_mid
        def _():
            for kind in every["mid"]:
                arrive("mid", c, kind)

    def y_copy(r, m):
        return remote(
            tin.at[rows_of(r), :], tok.at[rows_of(r), lanes_of(m)], ty_send.at[r], ty_recv.at[r],
            dp, y_peer,
        )

    def forward_copy(r, m):
        return remote(
            tok.at[rows_of(r), lanes_of(m)], tok.at[rows_of(r), lanes_of(m)],
            tf_send.at[r], tf_recv.at[r], dp, core_peer,
        )

    def core_copy(m):
        return remote(tin, tok.at[:, lanes_of(m)], tc_send, tc_recv, dp, core_peer)

    def relay_tokens(r):
        y_copy(r, y_peer).wait_recv()
        forward_copy(r, y_peer).start()

    def out_copy(i, m, mp_to):
        return remote(
            wot.at[:, lanes_of(m)], wot.at[:, lanes_of(m)], o_send.at[i], o_recv.at[i], dp, mp_to
        )

    @at_end
    def _():
        own("end", 0, 0)
        own("end", 1, 0)

    @at_mid
    def _():
        own("mid", 1, 0)
        own("mid", 0, 0)
        own("mid", 2, 0)

    @pl.loop(0, chunks)
    def _(r):
        y_copy(r, mp).start()

    core_copy(mp).start()
    load_query.wait()
    fill_query(1)

    @at_end
    def _():
        own("end", 0, 1)
        own("end", 1, 1)

    @at_mid
    def _():
        own("mid", 1, 1)
        own("mid", 0, 1)
        own("mid", 2, 1)

    fill_query(2)
    fill_query(3)
    fill_query(4)

    @at_end
    def _():
        for c in (2, 3):
            own("end", 0, c)
            own("end", 1, c)

    @at_mid
    def _():
        for c in (2, 3):
            own("mid", 0, c)

    lane = lax.broadcasted_iota(jnp.int32, (dialogs, 128), 1)
    sub = lax.broadcasted_iota(jnp.int32, (dialogs, 128), 0)
    lane_dialog = GROUP * (lane // 16) + lane % GROUP
    to_col = jnp.zeros((dialogs, 128), jnp.int32)
    to_row = jnp.full((dialogs, 128), -64, jnp.int32)
    to_wide = jnp.full((dialogs, 128), -64, jnp.int32)
    len_col = jnp.zeros((dialogs, 128), jnp.int32)
    flag_col = jnp.zeros((dialogs, 128), jnp.int32)
    for d in range(dialogs):
        target = owner[cluster[d]]
        to_col = jnp.where(sub == d, target, to_col)
        to_row = jnp.where(lane == d, target, to_row)
        to_wide = jnp.where((lane_dialog == d) & (lane < 64), target, to_wide)
        len_col = jnp.where(sub == d, lens[d], len_col)
        flag_col = jnp.where(sub == d, flags[d], flag_col)
    len_col = len_col.astype(FULL)
    flag_col = flag_col.astype(FULL)
    rank_col = jnp.sum(
        jnp.where((to_col == to_row) & (lane < sub), 1.0, 0.0), axis=1, keepdims=True
    )
    rank_row = jnp.sum(
        jnp.where((to_col == to_row) & (sub < lane), 1.0, 0.0), axis=0, keepdims=True
    )
    rank_wide = jnp.sum(
        jnp.where((to_col == to_wide) & (sub < lane_dialog), 1.0, 0.0), axis=0, keepdims=True
    )
    slot_row = to_row[0:1].astype(FULL) * CHUNK + rank_row
    slot_wide = to_wide[0:1].astype(FULL) * CHUNK + rank_wide
    reply_place = to_col[:, 0:1].astype(FULL) * 16.0 + rank_col
    place = lax.broadcasted_iota(jnp.int32, (64, 128), 0)
    place_lane = lax.broadcasted_iota(jnp.int32, (64, 128), 1)
    upper = place % 16 < 8
    held = ((place // 16) * 8 + place % 8).astype(FULL)
    pool_pick = jnp.where(upper & (held == slot_row), 1.0, 0.0).astype(HALF)[:, :dialogs]

    index = lax.broadcasted_iota(jnp.int32, mask.shape, 1)
    start = lax.broadcasted_iota(jnp.int32, mask.shape, 0) * seq_len
    ahead = (index - start).astype(FULL)
    mask[...] = jnp.where((ahead >= 0.0) & (ahead < len_col[:, 0:1]), 1.0, 0.0).astype(HALF)
    load_tokens.wait()
    mean = jnp.dot(mask[...], tok[:, lanes_of(mp)], preferred_element_type=FULL) / len_col[:, 0:1]
    picked = jnp.dot(pool_pick, mean.astype(HALF), preferred_element_type=FULL).astype(HALF)
    pool_out[0] = picked[:, : part // 2].reshape(pool_out.shape[1:])
    pool_out[1] = picked[:, part // 2 :].reshape(pool_out.shape[1:])

    def pool_copy(j, m, source):
        return remote(
            pool_out.at[j, m], pool_in.at[source], p_send.at[j, m], p_recv.at[source],
            2 * mp + j, m,
        )


    def normalize(r):
        for half in range(2):
            rows = pl.ds(pl.multiple_of(r * rows_each + half * (rows_each // 2), 32), rows_each // 2)
            values = tok[rows, :].astype(FULL)
            mean_square = jnp.sum(values * values, axis=-1, keepdims=True) * (1.0 / width)
            rs[rows, :] = jnp.broadcast_to(lax.rsqrt(mean_square + 1e-06), (rows_each // 2, 128))

    def turn(piece):
        return piece * cosine[...] + pltpu.roll(piece, HEAD_DIM // 2, 1) * sine[...]

    def keyval_rows(low, top):
        @pl.loop(low, top)
        def _(r):
            forward_copy(r, far).wait_recv()
            normalize(r)
            rows = rows_of(r)
            product = jnp.dot(tok[rows, :], wide[0], preferred_element_type=FULL)
            kst[rows, :] = turn(product[:, :HEAD_DIM] * rs[rows, :]).astype(HALF)
            vst[rows, :] = (product[:, HEAD_DIM:] * rs[rows, :]).astype(HALF)

    rows_group = GROUP * seq_len

    def query_rows(c, r, slot):
        rows = pl.ds(pl.multiple_of(r * rows_group, 128), rows_group)
        weights = wide[c] if c < 4 else narrow[...]
        product = jnp.dot(tok[rows, :], weights, preferred_element_type=FULL)
        for h in range(product.shape[1] // HEAD_DIM):
            span = slice(h * HEAD_DIM, (h + 1) * HEAD_DIM)
            for half in range(2):
                here = slice(half * rows_each, (half + 1) * rows_each)
                some = pl.ds(
                    pl.multiple_of(r * rows_group + half * rows_each, 64), rows_each
                )
                qst[slot, here, span] = turn(product[here, span] * rs[some, :]).astype(HALF)

    def attend_rows(c, r, slot):
        heads = 2 if c < 4 else 1
        lanes = heads * seq_len
        key_pos = lax.broadcasted_iota(jnp.int32, (seq_len, lanes), 0)
        query_pos = lax.broadcasted_iota(jnp.int32, (seq_len, lanes), 1) % seq_len
        causal = key_pos <= query_pos
        position = lax.broadcasted_iota(jnp.int32, (1, lanes), 1) % seq_len
        pieces = []
        for item in range(GROUP):
            here = slice(item * seq_len, (item + 1) * seq_len)
            keys = kst[pl.ds(pl.multiple_of(r * rows_group + item * seq_len, 16), seq_len), :]
            stacked = qst[slot, here, :HEAD_DIM]
            if heads == 2:
                stacked = jnp.concatenate([stacked, qst[slot, here, HEAD_DIM:]], axis=0)
            scores = lax.dot_general(keys, stacked, NT, preferred_element_type=FULL)
            scores = jnp.where(causal, scores * (1.0 / math.sqrt(HEAD_DIM)), -1e30)
            expanded = jnp.exp(scores - jnp.max(scores, axis=0, keepdims=True))
            length = lens[r * GROUP + item]
            share = jnp.where(position < length, 1.0, 0.0) / (
                jnp.sum(expanded, axis=0, keepdims=True)
                * jnp.full((1, lanes), length, jnp.int32).astype(FULL)
            )
            pieces.append((expanded * share).astype(HALF))
        weights = jnp.concatenate(pieces, axis=0)
        head_row = lax.broadcasted_iota(jnp.int32, (16, lanes), 0) // GROUP
        head_lane = lax.broadcasted_iota(jnp.int32, (16, lanes), 1) // seq_len
        chosen = jnp.where(head_row == head_lane, 1.0, 0.0).astype(HALF)
        sums_of = lax.dot_general(chosen, weights, NT, preferred_element_type=FULL)
        item_row = lax.broadcasted_iota(jnp.int32, sums_of.shape, 0) % GROUP
        item_lane = lax.broadcasted_iota(jnp.int32, sums_of.shape, 1) // seq_len
        sums_of = jnp.where(item_row == item_lane, sums_of, 0.0)
        coarse = sums_of.astype(HALF).astype(FULL)
        both = jnp.concatenate([coarse, sums_of - coarse], axis=0).astype(HALF)
        rows = pl.ds(pl.multiple_of(r * rows_group, 128), rows_group)
        mixed = jnp.dot(both, vst[rows, :], preferred_element_type=FULL)
        ctx[c - 1, r] = mixed[:16] + mixed[16:]

    def query_block(c, low, top):
        query_rows(c, low, low % 2)

        @pl.loop(low + 1, top)
        def _(r):
            attend_rows(c, r - 1, (r - 1) % 2)
            query_rows(c, r, r % 2)

        attend_rows(c, top - 1, (top - 1) % 2)

    def member_squares(low, top):
        @pl.loop(low, top)
        def _(step):
            rows = pl.ds(pl.multiple_of(step * 64, 64), 64)
            values = members[rows, :].astype(FULL)
            squares[rows, :] = jnp.broadcast_to(
                jnp.sum(values * values, axis=-1, keepdims=True), (64, 128)
            )

    @at_mid
    def _():
        onward("mid", 0, (2, 0), 1, 0)
        onward("mid", 0, (0, 0), 2)

    @at_end
    def _():
        onward("end", 0, (0, 1), 1)

    load_members.wait()
    member_squares(0, 4)
    relay_tokens(0)

    @at_mid
    def _():
        onward("mid", 1, (0, 0), 2)
        own("mid", 2, 2)
        onward("mid", 1, (2, 0), 0)
        own("mid", 0, 4)

    @at_end
    def _():
        onward("end", 1, (0, 1), 1)

    member_squares(4, 8)

    @at_mid
    def _():
        onward("mid", 0, (3, 0), 1, 0)
        onward("mid", 0, (1, 1), 1)
        send("mid", 1, 1, (2, 0))
        onward("mid", 2, (0, 0), 2)
        own("mid", 2, 3)

    @at_end
    def _():
        onward("end", 0, (2, 0), 0)
        onward("end", 2, (0, 1), 1)

    relay_tokens(1)

    @at_mid
    def _():
        onward("mid", 1, (3, 0), 1, 0)
        own("mid", 1, 2)
        onward("mid", 3, (0, 0), 2)
        own("mid", 2, 4)

    @at_end
    def _():
        onward("end", 0, (3, 0), 0)
        onward("end", 1, (1, 0), 0)
        own("end", 0, 4)
        onward("end", 3, (0, 1), 1)
        own("end", 1, 4)

    relay_tokens(2)

    @at_mid
    def _():
        onward("mid", 2, (2, 0), 1, 0)
        onward("mid", 4, (0, 0), 2)

    @at_end
    def _():
        onward("end", 1, (2, 0), 0)

    relay_tokens(3)

    @at_mid
    def _():
        onward("mid", 2, (3, 0), 1, 0)
        own("mid", 1, 3)
        onward("mid", 2, (1, 1), 1)
        onward("mid", 3, (2, 0), 1, 0)

    core_copy(core_peer).wait_recv()
    rest(0)
    keyval_rows(0, 4)

    @at_end
    def _():
        onward("end", 1, (3, 0), 0)
        onward("end", 4, (0, 1), 1)

    relay_tokens(4)

    @at_mid
    def _():
        onward("mid", 3, (3, 0), 1, 0)
        onward("mid", 4, (2, 0), 1, 0)

    relay_tokens(5)

    @at_end
    def _():
        onward("end", 2, (2, 0), 0)

    @at_mid
    def _():
        onward("mid", 4, (3, 0), 1, 0)
        own("mid", 1, 4)
        onward("mid", 4, (1, 1), 1)

    keyval_rows(4, 6)

    @at_end
    def _():
        onward("end", 2, (3, 0), 0)

    relay_tokens(6)
    load_out.wait()
    own_out = out_copy(0, mp, y_peer)
    own_out.start()
    beside_out = out_copy(1, mp, core_peer)
    beside_out.start()
    rest(1)
    query_block(1, 0, 3)

    @at_end
    def _():
        onward("end", 3, (1, 0), 0)

    relay_tokens(7)
    keyval_rows(6, 8)
    query_block(1, 3, 4)

    @at_end
    def _():
        onward("end", 3, (2, 0), 0)

    rest(2)
    query_block(2, 0, 2)

    @at_end
    def _():
        onward("end", 3, (3, 0), 0)

    query_block(2, 2, 4)

    @at_end
    def _():
        onward("end", 4, (2, 0), 0)
        onward("end", 4, (3, 0), 0)

    limit = counts[0] * 0
    for c in range(counts.shape[0]):
        limit = limit + jnp.where(owner[c] == dp, counts[c], 0)
    member_count = members.shape[0]
    member = mp * member_count + lax.broadcasted_iota(jnp.int32, (1, member_count), 1)
    scale = jnp.where(member < limit, logit_scale, 0.0) * lax.rsqrt(squares[...].T[0:1, :] + 1e-06)
    rest(3)
    query_block(3, 0, 4)
    out_copy(0, y_peer, y_peer).wait_recv()
    onward_out = out_copy(2, y_peer, core_peer)
    onward_out.start()
    rest(4)
    for j in range(2):
        for m in range(4):
            mine = (2 * mp + j == dp) & (mp == m)

            @pl.when(jnp.logical_not(mine))
            def _():
                pool_copy(j, m, dp).start()

            @pl.when(mine)
            def _():
                pool_in[dp] = pool_out[j, m]

    query_block(4, 0, 4)

    lane_head = (place_lane // GROUP) % 2

    def pick(h):
        right = (upper if h < 4 else jnp.logical_not(upper)) & (lane_head == h % 2)
        return jnp.where(right & (held == slot_wide), 1.0, 0.0).astype(HALF)[:, :64]

    for block in range(4):
        value = jnp.zeros((64, 128), FULL)
        for h in (block, block + 4):
            if h < 7:
                rows = ctx[h // 2].reshape(64, 128).astype(HALF)
                value = value + jnp.dot(pick(h), rows, preferred_element_type=FULL)
        cout[:, :, block * 128 : (block + 1) * 128] = value.astype(HALF).reshape(4, 16, 128)

    def context_copy(i, j, m_slot, d_slot):
        to = (mp + j) % 4
        return remote(
            cout.at[to], cin.at[m_slot, d_slot], c_send.at[i, j], c_recv.at[m_slot, d_slot],
            (dp + i) % 8, to,
        )

    partners = [(i, j) for i in range(8) for j in range(4) if i or j]
    for i, j in sorted(partners, key=lambda ij: -abs(ij[0] - 4) * 0 + (ij[0] in (0, 1, 7))):
        context_copy(i, j, mp, dp).start()
    cin[mp, dp] = cout[mp]
    out_copy(1, core_peer, core_peer).wait_recv()
    out_copy(2, far, core_peer).wait_recv()
    for source in range(8):
        @pl.when(jnp.logical_not((dp // 2 == mp) & (dp == source)))
        def _():
            pool_copy(0, 0, source).wait_recv()

    half_out = wot.shape[0]
    total_a = jnp.zeros((128, half_out), FULL)
    total_b = jnp.zeros((128, half_out), FULL)
    for j in range(4):
        m = (mp + j) % 4
        for i in range(8):
            if i or j:
                context_copy(i, j, m, (dp + i) % 8).wait_recv()
        have = cin[m].reshape(128, 512)
        total_a = total_a + lax.dot_general(
            have, wot[:, pl.ds(pl.multiple_of(m * part, 128), 512)], NT,
            preferred_element_type=FULL,
        )
        total_b = total_b + lax.dot_general(
            have[:, : part - 512],
            wot[:, pl.ds(pl.multiple_of(m * part + 512, 128), part - 512)], NT,
            preferred_element_type=FULL,
        )
    embedded = (
        total_a.reshape(8, 16, half_out)[:, :8]
        + total_b.reshape(8, 16, half_out)[:, 8:]
        + pool_in[...].astype(FULL)[:, :8]
    ).reshape(64, half_out)
    row = lax.broadcasted_iota(jnp.int32, (64, 64), 0)
    column = lax.broadcasted_iota(jnp.int32, (64, 64), 1)
    order = jnp.where(
        column == ((row // 4) % 8) * 8 + (row // 32) * 4 + row % 4, 1.0, 0.0
    ).astype(HALF)
    sums[...] = (
        jnp.dot(order, embedded.astype(HALF), preferred_element_type=FULL)
        .astype(HALF)
        .reshape(sums.shape)
    )

    def sum_copy(j, i, slot):
        return remote(
            sums.at[j], rows_in.at[slot], d_send.at[j, i], d_recv.at[slot],
            2 * mp + j, (mp + i) % 4,
        )

    for j in range(2):
        mine = 2 * mp + j == dp
        for i in range(1, 4):
            sum_copy(j, i, dp).start()

        @pl.when(jnp.logical_not(mine))
        def _():
            sum_copy(j, 0, dp).start()

        @pl.when(mine)
        def _():
            rows_in[dp] = sums[j]

    for slot in range(8):
        @pl.when(jnp.logical_not((dp // 2 == mp) & (dp == slot)))
        def _():
            sum_copy(0, 0, slot).wait_recv()

    for slot in range(8):
        joined[:, slot * half_out : (slot + 1) * half_out] = rows_in[slot].astype(FULL)
    embedding = joined[...]
    dots = lax.dot_general(
        embedding.astype(HALF), members[...], NT, preferred_element_type=FULL
    )
    inverse = lax.rsqrt(jnp.sum(embedding * embedding, axis=-1, keepdims=True) + 1e-06)
    found = (dots * inverse * scale).astype(HALF)
    row = lax.broadcasted_iota(jnp.int32, (128, 32), 0)
    column = lax.broadcasted_iota(jnp.int32, (128, 32), 1)
    value = jnp.zeros((128, 128), FULL)
    for q in range(4):
        spread = jnp.where(
            ((row % 16) // 4 == q) & (column == (row // 16) * 4 + row % 4), 1.0, 0.0
        ).astype(HALF)
        value = value + jnp.dot(
            spread, found[:, q * 128 : (q + 1) * 128], preferred_element_type=FULL
        )
    replies[...] = value.astype(HALF).reshape(replies.shape)

    def reply_copy(i, slot):
        to = (dp + i) % 8
        return remote(replies.at[to], arrived.at[slot], f_send.at[i], f_recv.at[slot], to, mp)

    for i in range(1, 8):
        reply_copy(i, dp).start()
    arrived[dp] = replies[dp]
    for i in range(1, 8):
        reply_copy(i, (dp + i) % 8).wait_recv()
    have = arrived[...].reshape(128, 128)
    column = lax.broadcasted_iota(jnp.int32, (dialogs, 128), 1).astype(FULL)
    for q in range(4):
        fetch = jnp.where(column == reply_place + 4.0 * q, flag_col, 0.0).astype(HALF)
        out[:, q * 128 : (q + 1) * 128] = jnp.dot(fetch, have, preferred_element_type=FULL)

    for r in range(chunks):
        y_copy(r, mp).wait_send()
        forward_copy(r, y_peer).wait_send()
    core_copy(mp).wait_send()
    own_out.wait_send()
    beside_out.wait_send()
    onward_out.wait_send()

    @at_end
    def _():
        for way, c, kind in sent["end"]:
            weight_copy(way, c, kind).wait_send()

    @at_mid
    def _():
        for way, c, kind in sent["mid"]:
            weight_copy(way, c, kind).wait_send()

    for j in range(2):
        for m in range(4):
            @pl.when(jnp.logical_not((2 * mp + j == dp) & (mp == m)))
            def _():
                pool_copy(j, m, dp).wait_send()

        @pl.when(2 * mp + j != dp)
        def _():
            sum_copy(j, 0, dp).wait_send()

        for i in range(1, 4):
            sum_copy(j, i, dp).wait_send()
    for i, j in partners:
        context_copy(i, j, mp, dp).wait_send()
    for i in range(1, 8):
        reply_copy(i, dp).wait_send()


def fused(
    tokens, norm_gain, w_query, w_keyval, w_out, residents, lengths, cluster, owner, counts, flags
):
    dialogs, seq_len, part = tokens.shape
    total = dialogs * seq_len
    depth, queries = w_query.shape
    width = norm_gain.shape[0]
    member_count = residents.shape[1]
    half_out = w_out.shape[1]
    half = HEAD_DIM // 2
    freqs = rope_base ** (-np.arange(half, dtype=np.float64) * 2.0 / HEAD_DIM)
    angles = np.arange(seq_len, dtype=np.float64)[:, None] * freqs[None, :]
    cosine, sine = np.cos(angles), np.sin(angles)
    cosine = np.tile(np.concatenate([cosine, cosine], axis=1), (CHUNK, 1)).astype(np.float32)
    sine = np.tile(np.concatenate([-sine, sine], axis=1), (CHUNK, 1)).astype(np.float32)
    vmem = pl.BlockSpec(memory_space=pltpu.VMEM)
    smem = pl.BlockSpec(memory_space=pltpu.SMEM)
    hbm = pl.BlockSpec(memory_space=pltpu.HBM)
    sem = pltpu.SemaphoreType.DMA
    return pl.pallas_call(
        fused_kernel,
        out_shape=jax.ShapeDtypeStruct((dialogs, member_count), FULL),
        in_specs=[smem] * 5 + [hbm, hbm, hbm, vmem, hbm, hbm, vmem, vmem],
        out_specs=vmem,
        scratch_shapes=[
            pltpu.VMEM((total, width), HALF),
            pltpu.VMEM((4, width, 256), HALF),
            pltpu.VMEM((width, 128), HALF),
            pltpu.VMEM((half_out, width), HALF),
            pltpu.VMEM((member_count, width), HALF),
            pltpu.VMEM((depth, queries), HALF),
            pltpu.VMEM((depth, 2, 128), HALF),
            pltpu.VMEM((512, 128), FULL),
            pltpu.VMEM((total, 128), FULL),
            pltpu.VMEM((total, 128), HALF),
            pltpu.VMEM((total, 128), HALF),
            pltpu.VMEM((2, GROUP * seq_len, 256), HALF),
            pltpu.VMEM((4, 4, 16, 128), FULL),
            pltpu.VMEM((dialogs, total), HALF),
            pltpu.VMEM((2, 4, 16, half_out), HALF),
            pltpu.VMEM((8, 16, half_out), HALF),
            pltpu.VMEM((4, 16, 512), HALF),
            pltpu.VMEM((4, 8, 16, 512), HALF),
            pltpu.VMEM((2, 32, half_out), HALF),
            pltpu.VMEM((8, 32, half_out), HALF),
            pltpu.VMEM((32, width), FULL),
            pltpu.VMEM((member_count, 128), FULL),
            pltpu.VMEM((8, 16, 128), HALF),
            pltpu.VMEM((8, 16, 128), HALF),
            sem((5,)),
            sem((8,)),
            sem((8,)),
            sem,
            sem,
            sem((8,)),
            sem((8,)),
            sem((3, 5, 8)),
            sem((5, 8)),
            sem((3,)),
            sem((3,)),
            sem((2, 4)),
            sem((8,)),
            sem((8, 4)),
            sem((4, 8)),
            sem((2, 4)),
            sem((8,)),
            sem((8,)),
            sem((8,)),
        ],
        compiler_params=pltpu.CompilerParams(
            collective_id=0, has_side_effects=True, vmem_limit_bytes=58 * 1024 * 1024
        ),
    )(
        lengths, cluster[:, 0], owner, counts, flags,
        tokens.reshape(total, part), w_query, w_keyval,
        norm_gain.reshape(-1, 128), w_out.T, residents[0], cosine, sine,
    )


def plain_project(tokens, norm_gain, w_query, w_keyval, lengths):
    gathered = lax.all_gather(tokens, "mp", axis=2, tiled=True)
    dialogs, seq_len, width = gathered.shape
    hidden = gathered.astype(jnp.float32)
    normed = (
        hidden * lax.rsqrt(jnp.mean(hidden * hidden, axis=-1, keepdims=True) + 1e-06) * norm_gain
    ).astype(jnp.bfloat16)
    normed_flat = normed.reshape(dialogs * seq_len, width)
    query_cols = w_query.shape[1]
    keyval_cols = w_keyval.shape[2]
    pieces = (
        lax.all_gather(w_query, "dp", axis=0, tiled=True),
        lax.all_gather(w_keyval, "dp", axis=0, tiled=True),
    )
    keyval_piece = pieces[1].reshape(pieces[1].shape[0], 2 * keyval_cols)
    query_sum = jnp.dot(normed_flat, pieces[0], preferred_element_type=jnp.float32)
    keyval_sum = jnp.dot(normed_flat, keyval_piece, preferred_element_type=jnp.float32)
    positions = jnp.arange(seq_len)
    local_heads = query_cols // HEAD_DIM
    local_kv = keyval_cols // HEAD_DIM
    query = jax.vmap(lambda block: rotate(block, positions))(
        query_sum.reshape(dialogs, seq_len, local_heads, HEAD_DIM)
    ).astype(jnp.bfloat16)
    keys = jax.vmap(lambda block: rotate(block, positions))(
        keyval_sum[:, :keyval_cols].reshape(dialogs, seq_len, local_kv, HEAD_DIM)
    ).astype(jnp.bfloat16)
    values = (
        keyval_sum[:, keyval_cols:]
        .reshape(dialogs, seq_len, local_kv, HEAD_DIM)
        .astype(jnp.bfloat16)
    )
    valid = (positions[None, :] < lengths[:, None]).astype(jnp.float32)
    pooled_input = (
        jnp.sum(hidden * valid[:, :, None], axis=1) / lengths.astype(jnp.float32)[:, None]
    )
    pooled_context = jax.vmap(attend)(query, keys, values, lengths).astype(jnp.bfloat16)
    return pooled_context, pooled_input


def plain_score(pooled_context, pooled_input, w_out, members, onehot, live):
    dialogs = pooled_context.shape[0]
    everyone = lax.all_gather(pooled_context, "dp", axis=0, tiled=True)
    slices = jnp.dot(everyone, w_out, preferred_element_type=jnp.float32).astype(jnp.bfloat16)
    slices = slices.reshape(-1, dialogs, w_out.shape[1])
    slices = lax.all_to_all(slices, "dp", split_axis=0, concat_axis=0, tiled=True)
    partial_out = slices.transpose(1, 0, 2).reshape(dialogs, -1)
    projected = lax.psum(partial_out, "mp").astype(jnp.float32)
    embedding = pooled_input + projected
    unit = embedding * lax.rsqrt(jnp.sum(embedding * embedding, axis=-1, keepdims=True) + 1e-06)
    unit = unit.astype(jnp.bfloat16)
    inverse_norm = lax.rsqrt(
        jnp.einsum("md,md->m", members, members, preferred_element_type=jnp.float32) + 1e-06
    )
    outgoing = jnp.einsum(
        "ocn,nd->ocd", onehot.astype(jnp.bfloat16), unit, preferred_element_type=jnp.float32
    ).astype(jnp.bfloat16)
    query_rows = lax.all_to_all(outgoing, "dp", split_axis=0, concat_axis=0, tiled=True)
    dots = lax.dot_general(
        query_rows,
        members,
        (((query_rows.ndim - 1,), (1,)), ((), ())),
        preferred_element_type=jnp.float32,
    )
    return lax.all_to_all(
        jnp.where(live[0] > 0, live[0] * dots * inverse_norm, 0.0).astype(jnp.bfloat16),
        "dp",
        split_axis=0,
        concat_axis=0,
        tiled=True,
    )


def general(
    tokens, norm_gain, w_query, w_keyval, w_out, residents, lengths, cluster, owner, counts, flags
):
    pooled_context, pooled_input = plain_project(tokens, norm_gain, w_query, w_keyval, lengths)
    dialogs = tokens.shape[0]
    my_index = lax.axis_index("dp")
    owner_count = lax.axis_size("dp")
    my_count = jnp.sum(jnp.where(owner == my_index, counts, 0))
    members = residents[0]
    member_count = members.shape[0]
    member_start = lax.axis_index("mp") * member_count
    live = jnp.where(member_start + jnp.arange(member_count) < my_count, logit_scale, 0.0)[None, :]
    table_size = owner.shape[0]
    cluster_ids = cluster[:, 0]
    destination = jnp.sum(
        jnp.where(jnp.arange(table_size)[None, :] == cluster_ids[:, None], owner[None, :], 0),
        axis=1,
    )
    capacity = max(1, -(-dialogs // owner_count))
    order = jnp.arange(dialogs)
    earlier = (destination[None, :] == destination[:, None]) & (order[None, :] < order[:, None])
    rank = jnp.sum(earlier.astype(jnp.int32), axis=1)
    onehot = (jnp.arange(owner_count)[:, None, None] == destination[None, None, :]) & (
        jnp.arange(capacity)[None, :, None] == rank[None, None, :]
    )
    returned = plain_score(pooled_context, pooled_input, w_out, members, onehot, live)
    similarity = jnp.einsum(
        "ocn,ocm->nm", onehot.astype(jnp.bfloat16), returned, preferred_element_type=jnp.float32
    )
    return similarity * flags.astype(jnp.float32)[:, None]


def local(*args):
    if lax.axis_size("dp") == 8 and lax.axis_size("mp") == 4:
        return fused(*args)
    return general(*args)


def solution(mesh):
    in_specs = (
        P("dp", None, "mp"),
        P(),
        P("dp", "mp"),
        P("dp", None, "mp"),
        P("mp", "dp"),
        P("dp", "mp"),
        P("dp"),
        P("dp"),
        P(),
        P(),
        P("dp"),
    )
    out_specs = P("dp", "mp")
    return jax.shard_map(local, mesh=mesh, in_specs=in_specs, out_specs=out_specs, check_vma=False)
```

```python
import math

import jax
import jax.numpy as jnp
import numpy as np
from jax import lax
from jax.experimental import pallas as pl
from jax.experimental.pallas import tpu as pltpu
from jax.sharding import PartitionSpec as P

HEAD_DIM = 128


rope_base = 1000000.0
logit_scale = 100.0


def rotate(values, positions):
    half = values.shape[-1] // 2
    freqs = rope_base ** (-jnp.arange(half, dtype=jnp.float32) * 2.0 / values.shape[-1])
    angles = positions.astype(jnp.float32)[:, None] * freqs[None, :]
    cosine = jnp.cos(angles)[:, None, :]
    sine = jnp.sin(angles)[:, None, :]
    first = values[..., :half]
    second = values[..., half:]
    return jnp.concatenate(
        [first * cosine - second * sine, second * cosine + first * sine], axis=-1
    )


def attend(query, keys, values, length):
    seq_len = query.shape[0]
    kv_count = keys.shape[1]
    group = query.shape[1] // kv_count
    grouped = query.reshape(seq_len, kv_count, group, query.shape[-1])
    scores = jnp.einsum(
        "qkgd,pkd->kgqp", grouped, keys, preferred_element_type=jnp.float32
    ) / math.sqrt(query.shape[-1])
    row_pos = jnp.arange(seq_len)[:, None]
    col_pos = jnp.arange(seq_len)[None, :]
    allowed = (col_pos <= row_pos) & (col_pos < length)
    scores = jnp.where(allowed, scores, -1e30)
    highest = jnp.max(scores, axis=-1, keepdims=True)
    expanded = jnp.exp(scores - highest)
    weights = (expanded / jnp.sum(expanded, axis=-1, keepdims=True)).astype(jnp.bfloat16)
    context = jnp.einsum("kgqp,pkd->qkgd", weights, values, preferred_element_type=jnp.float32)
    valid = (jnp.arange(seq_len) < length).astype(jnp.float32)
    pooled = jnp.sum(context * valid[:, None, None, None], axis=0) / length.astype(jnp.float32)
    return pooled.reshape(-1)


MESH = pl.DeviceIdType.MESH
HALF, FULL = jnp.bfloat16, jnp.float32
CHUNK = 4
GROUP = 8
NT = (((1,), (1,)), ((), ()))


def fused_kernel(
    lens, cluster, owner, counts, flags,
    tin, query_in, keyval_in, gain, w_out_in, members_in, cosine, sine,
    out,
    tok, wide, narrow, wot, members, qstage, kvstage, gcol, rs, kst, vst, qst, ctx, mask,
    pool_out, pool_in, cout, cin, sums, rows_in, joined, squares, replies, arrived,
    l_sem, ty_send, ty_recv, tc_send, tc_recv, tf_send, tf_recv, wsend, wrecv,
    o_send, o_recv, p_send, p_recv, a_send, a_recv, b_send, c_send, c_recv,
    d_send, d_recv, e_send, f_send, f_recv,
):
    dp = lax.axis_index("dp")
    mp = lax.axis_index("mp")
    z, x = dp // 2, dp % 2
    high = z // 2
    core_peer = mp + 1 - 2 * (mp % 2)
    y_peer = (mp + 2) % 4
    far = (core_peer + 2) % 4
    pair_z = z + 1 - 2 * (z % 2)
    x_peer = 2 * z + 1 - x
    total, part = tin.shape
    depth, queries = query_in.shape
    width = tok.shape[1]
    dialogs = lens.shape[0]
    seq_len = total // dialogs
    rows_each = CHUNK * seq_len
    chunks = total // rows_each
    end = (z == 0) | (z == 3)
    mid = (z == 1) | (z == 2)

    def across(k):
        return k + high * (3 - 2 * k)

    def slot_of(kind):
        k, prime = kind
        return 2 * across(k) + (1 - x if prime else x)

    def lanes_of(m):
        return pl.ds(pl.multiple_of(m * part, 128), part)

    def rows_of(r):
        return pl.ds(pl.multiple_of(r * rows_each, 64), rows_each)

    def remote(source, target, send, recv, dp_to, mp_to):
        return pltpu.make_async_remote_copy(
            src_ref=source, dst_ref=target, send_sem=send, recv_sem=recv,
            device_id={"dp": dp_to, "mp": mp_to}, device_id_type=MESH,
        )

    load_query = pltpu.make_async_copy(query_in, qstage, l_sem.at[0])
    load_keyval = pltpu.make_async_copy(keyval_in, kvstage, l_sem.at[1])
    load_tokens = pltpu.make_async_copy(tin, tok.at[:, lanes_of(mp)], l_sem.at[2])
    load_members = pltpu.make_async_copy(members_in, members, l_sem.at[3])
    load_out = pltpu.make_async_copy(w_out_in, wot.at[:, lanes_of(mp)], l_sem.at[4])
    load_keyval.start()
    load_query.start()

    barrier = pltpu.get_barrier_semaphore()

    def greet(dp_to, mp_to):
        pl.semaphore_signal(
            barrier, inc=1, device_id={"dp": dp_to, "mp": mp_to}, device_id_type=MESH
        )

    greet(dp, core_peer)
    greet(dp, y_peer)
    greet(x_peer, mp)
    greet(2 * pair_z + x, mp)

    @pl.when(mid)
    def _():
        greet(2 * across(2) + x, mp)

    load_tokens.start()
    load_members.start()
    load_out.start()

    first = (7 * dp) // 2
    for i in range(4):
        row = gain[pl.ds(first + i, 1), :]
        gcol[i * 128 : (i + 1) * 128, :] = jnp.broadcast_to(row, (128, 128)).T
    own_rows = pl.ds(pl.multiple_of(dp * depth, 64), depth)

    def gained(piece):
        factor = gcol[pl.ds(pl.multiple_of((dp % 2) * 64, 64), depth), :]
        return (piece.astype(FULL) * factor).astype(HALF)

    def fill_keyval():
        for i in range(2):
            wide[0, own_rows, i * 128 : (i + 1) * 128] = gained(kvstage[:, i, :])

    def fill_query(c):
        for h in range(2 * c - 2, min(2 * c, 7)):
            piece = gained(qstage[:, h * 128 : (h + 1) * 128])
            if h < 6:
                wide[c, own_rows, (h % 2) * 128 : (h % 2 + 1) * 128] = piece
            else:
                narrow[own_rows, :] = piece

    load_keyval.wait()
    fill_keyval()

    @pl.when(end)
    def _():
        pl.semaphore_wait(barrier, 4)

    @pl.when(mid)
    def _():
        pl.semaphore_wait(barrier, 5)

    def block_ref(c, slot):
        rows = pl.ds(pl.multiple_of(slot * depth, 64), depth)
        return wide.at[c, rows, :] if c < 4 else narrow.at[rows, :]

    ways = (x_peer, 2 * pair_z + x, 2 * across(2) + x)
    own_kind = {"end": (0, 0), "mid": (1, 0)}
    sent = {"end": [], "mid": []}
    waited = {"end": set(), "mid": set()}
    every = {
        "end": [(0, 1), (1, 0), (1, 1), (2, 0), (2, 1), (3, 0), (3, 1)],
        "mid": [(0, 0), (0, 1), (1, 1), (2, 0), (2, 1), (3, 0), (3, 1)],
    }

    def weight_copy(way, c, kind):
        slot = slot_of(kind)
        return remote(
            block_ref(c, slot), block_ref(c, slot), wsend.at[way, c, slot], wrecv.at[c, slot],
            ways[way], mp,
        )

    def send(role, way, c, kind):
        sent[role].append((way, c, kind))
        weight_copy(way, c, kind).start()

    def own(role, way, c):
        send(role, way, c, own_kind[role])

    def arrive(role, c, kind):
        if (c, kind) not in waited[role]:
            waited[role].add((c, kind))
            weight_copy(0, c, kind).wait_recv()

    def onward(role, c, kind, *to):
        arrive(role, c, kind)
        for way in to:
            send(role, way, c, kind)

    def at_end(f):
        pl.when(end)(f)

    def at_mid(f):
        pl.when(mid)(f)

    def rest(c):
        @at_end
        def _():
            for kind in every["end"]:
                arrive("end", c, kind)

        @at_mid
        def _():
            for kind in every["mid"]:
                arrive("mid", c, kind)

    def y_copy(r, m):
        return remote(
            tin.at[rows_of(r), :], tok.at[rows_of(r), lanes_of(m)], ty_send.at[r], ty_recv.at[r],
            dp, y_peer,
        )

    def forward_copy(r, m):
        return remote(
            tok.at[rows_of(r), lanes_of(m)], tok.at[rows_of(r), lanes_of(m)],
            tf_send.at[r], tf_recv.at[r], dp, core_peer,
        )

    def core_copy(m):
        return remote(tin, tok.at[:, lanes_of(m)], tc_send, tc_recv, dp, core_peer)

    def relay_tokens(r):
        y_copy(r, y_peer).wait_recv()
        forward_copy(r, y_peer).start()

    def out_copy(i, m, mp_to):
        return remote(
            wot.at[:, lanes_of(m)], wot.at[:, lanes_of(m)], o_send.at[i], o_recv.at[i], dp, mp_to
        )

    @at_end
    def _():
        own("end", 0, 0)
        own("end", 1, 0)

    @at_mid
    def _():
        own("mid", 1, 0)
        own("mid", 0, 0)
        own("mid", 2, 0)

    @pl.loop(0, chunks)
    def _(r):
        y_copy(r, mp).start()

    core_copy(mp).start()
    load_query.wait()
    fill_query(1)

    @at_end
    def _():
        own("end", 0, 1)
        own("end", 1, 1)

    @at_mid
    def _():
        own("mid", 1, 1)
        own("mid", 0, 1)
        own("mid", 2, 1)

    fill_query(2)
    fill_query(3)
    fill_query(4)

    @at_end
    def _():
        for c in (2, 3):
            own("end", 0, c)
            own("end", 1, c)

    @at_mid
    def _():
        for c in (2, 3):
            own("mid", 0, c)

    def owner_of(m, j):
        return 2 * (m % 2 + j * (3 - 2 * (m % 2))) + m // 2

    lane = lax.broadcasted_iota(jnp.int32, (dialogs, 128), 1)
    sub = lax.broadcasted_iota(jnp.int32, (dialogs, 128), 0)
    lane_dialog = GROUP * (lane // 16) + lane % GROUP
    to_col = jnp.zeros((dialogs, 128), jnp.int32)
    to_row = jnp.full((dialogs, 128), -64, jnp.int32)
    to_wide = jnp.full((dialogs, 128), -64, jnp.int32)
    len_col = jnp.zeros((dialogs, 128), jnp.int32)
    flag_col = jnp.zeros((dialogs, 128), jnp.int32)
    for d in range(dialogs):
        target = owner[cluster[d]]
        to_col = jnp.where(sub == d, target, to_col)
        to_row = jnp.where(lane == d, target, to_row)
        to_wide = jnp.where((lane_dialog == d) & (lane < 64), target, to_wide)
        len_col = jnp.where(sub == d, lens[d], len_col)
        flag_col = jnp.where(sub == d, flags[d], flag_col)
    len_col = len_col.astype(FULL)
    flag_col = flag_col.astype(FULL)
    rank_col = jnp.sum(
        jnp.where((to_col == to_row) & (lane < sub), 1.0, 0.0), axis=1, keepdims=True
    )
    rank_row = jnp.sum(
        jnp.where((to_col == to_row) & (sub < lane), 1.0, 0.0), axis=0, keepdims=True
    )
    rank_wide = jnp.sum(
        jnp.where((to_col == to_wide) & (sub < lane_dialog), 1.0, 0.0), axis=0, keepdims=True
    )
    slot_row = to_row[0:1].astype(FULL) * CHUNK + rank_row
    slot_wide = to_wide[0:1].astype(FULL) * CHUNK + rank_wide
    reply_place = to_col[:, 0:1].astype(FULL) * 16.0 + rank_col
    place = lax.broadcasted_iota(jnp.int32, (64, 128), 0)
    place_lane = lax.broadcasted_iota(jnp.int32, (64, 128), 1)
    upper = place % 16 < 8
    held = (owner_of(place // 16, (place % 8) // 4) * CHUNK + place % CHUNK).astype(FULL)
    part_row = lax.broadcasted_iota(jnp.int32, (16, 128), 0)
    part_held = (owner_of(mp, (part_row % 8) // 4) * CHUNK + part_row % CHUNK).astype(FULL)
    part_pick = jnp.where(part_held == slot_row, 1.0, 0.0)
    part_upper = jnp.where(part_row < 8, part_pick, 0.0).astype(HALF)[:, :dialogs]
    part_lower = jnp.where(part_row >= 8, part_pick, 0.0).astype(HALF)[:, :dialogs]

    index = lax.broadcasted_iota(jnp.int32, mask.shape, 1)
    start = lax.broadcasted_iota(jnp.int32, mask.shape, 0) * seq_len
    ahead = (index - start).astype(FULL)
    mask[...] = jnp.where((ahead >= 0.0) & (ahead < len_col[:, 0:1]), 1.0, 0.0).astype(HALF)
    load_tokens.wait()

    def pool_copy(i, source):
        to = (dp + i) % 8
        return remote(pool_out.at[to], pool_in.at[source], p_send.at[i], p_recv.at[source], to, mp)

    def pool():
        block = width // 8
        for m in range(4):
            some = tok[:, m * part : (m + 1) * part]
            mean = jnp.dot(mask[...], some, preferred_element_type=FULL)
            mean = (mean / len_col[:, 0:1]).astype(HALF)
            for j in range(2):
                lead = mean[:, j * block : j * block + 256]
                back = mean[:, j * block + 256 : (j + 1) * block]
                lower = jnp.dot(part_lower, back, preferred_element_type=FULL)
                pool_out[2 * m + j] = (
                    jnp.dot(part_upper, lead, preferred_element_type=FULL)
                    + jnp.concatenate([lower, jnp.zeros((16, 512 - block), FULL)], axis=1)
                ).astype(HALF)
        for i in range(1, 8):
            pool_copy(i, dp).start()
        pool_in[dp] = pool_out[dp]

    def normalize(r):
        for half in range(2):
            rows = pl.ds(pl.multiple_of(r * rows_each + half * (rows_each // 2), 32), rows_each // 2)
            values = tok[rows, :].astype(FULL)
            mean_square = jnp.sum(values * values, axis=-1, keepdims=True) * (1.0 / width)
            rs[rows, :] = jnp.broadcast_to(lax.rsqrt(mean_square + 1e-06), (rows_each // 2, 128))

    def turn(piece):
        return piece * cosine[...] + pltpu.roll(piece, HEAD_DIM // 2, 1) * sine[...]

    def keyval_rows(low, top):
        @pl.loop(low, top)
        def _(r):
            forward_copy(r, far).wait_recv()
            normalize(r)
            rows = rows_of(r)
            product = jnp.dot(tok[rows, :], wide[0], preferred_element_type=FULL)
            kst[rows, :] = turn(product[:, :HEAD_DIM] * rs[rows, :]).astype(HALF)
            vst[rows, :] = (product[:, HEAD_DIM:] * rs[rows, :]).astype(HALF)

    rows_group = GROUP * seq_len

    def query_rows(c, r, slot):
        rows = pl.ds(pl.multiple_of(r * rows_group, 128), rows_group)
        weights = wide[c] if c < 4 else narrow[...]
        product = jnp.dot(tok[rows, :], weights, preferred_element_type=FULL)
        for h in range(product.shape[1] // HEAD_DIM):
            span = slice(h * HEAD_DIM, (h + 1) * HEAD_DIM)
            for half in range(2):
                here = slice(half * rows_each, (half + 1) * rows_each)
                some = pl.ds(
                    pl.multiple_of(r * rows_group + half * rows_each, 64), rows_each
                )
                qst[slot, here, span] = turn(product[here, span] * rs[some, :]).astype(HALF)

    def attend_rows(c, r, slot):
        heads = 2 if c < 4 else 1
        lanes = heads * seq_len
        key_pos = lax.broadcasted_iota(jnp.int32, (seq_len, lanes), 0)
        query_pos = lax.broadcasted_iota(jnp.int32, (seq_len, lanes), 1) % seq_len
        causal = key_pos <= query_pos
        position = lax.broadcasted_iota(jnp.int32, (1, lanes), 1) % seq_len
        pieces = []
        for item in range(GROUP):
            here = slice(item * seq_len, (item + 1) * seq_len)
            keys = kst[pl.ds(pl.multiple_of(r * rows_group + item * seq_len, 16), seq_len), :]
            stacked = qst[slot, here, :HEAD_DIM]
            if heads == 2:
                stacked = jnp.concatenate([stacked, qst[slot, here, HEAD_DIM:]], axis=0)
            scores = lax.dot_general(keys, stacked, NT, preferred_element_type=FULL)
            scores = jnp.where(causal, scores * (1.0 / math.sqrt(HEAD_DIM)), -1e30)
            expanded = jnp.exp(scores - jnp.max(scores, axis=0, keepdims=True))
            length = lens[r * GROUP + item]
            share = jnp.where(position < length, 1.0, 0.0) / (
                jnp.sum(expanded, axis=0, keepdims=True)
                * jnp.full((1, lanes), length, jnp.int32).astype(FULL)
            )
            pieces.append((expanded * share).astype(HALF))
        weights = jnp.concatenate(pieces, axis=0)
        head_row = lax.broadcasted_iota(jnp.int32, (16, lanes), 0) // GROUP
        head_lane = lax.broadcasted_iota(jnp.int32, (16, lanes), 1) // seq_len
        chosen = jnp.where(head_row == head_lane, 1.0, 0.0).astype(HALF)
        sums_of = lax.dot_general(chosen, weights, NT, preferred_element_type=FULL)
        item_row = lax.broadcasted_iota(jnp.int32, sums_of.shape, 0) % GROUP
        item_lane = lax.broadcasted_iota(jnp.int32, sums_of.shape, 1) // seq_len
        sums_of = jnp.where(item_row == item_lane, sums_of, 0.0)
        coarse = sums_of.astype(HALF).astype(FULL)
        both = jnp.concatenate([coarse, sums_of - coarse], axis=0).astype(HALF)
        rows = pl.ds(pl.multiple_of(r * rows_group, 128), rows_group)
        mixed = jnp.dot(both, vst[rows, :], preferred_element_type=FULL)
        ctx[c - 1, r] = mixed[:16] + mixed[16:]

    def query_block(c, low, top):
        query_rows(c, low, low % 2)

        @pl.loop(low + 1, top)
        def _(r):
            attend_rows(c, r - 1, (r - 1) % 2)
            query_rows(c, r, r % 2)

        attend_rows(c, top - 1, (top - 1) % 2)

    def member_squares(low, top):
        @pl.loop(low, top)
        def _(step):
            rows = pl.ds(pl.multiple_of(step * 64, 64), 64)
            values = members[rows, :].astype(FULL)
            squares[rows, :] = jnp.broadcast_to(
                jnp.sum(values * values, axis=-1, keepdims=True), (64, 128)
            )

    @at_mid
    def _():
        onward("mid", 0, (2, 0), 1, 0)
        onward("mid", 0, (0, 0), 2)

    @at_end
    def _():
        onward("end", 0, (0, 1), 1)

    load_members.wait()
    member_squares(0, 4)
    relay_tokens(0)

    @at_mid
    def _():
        onward("mid", 1, (0, 0), 2)
        own("mid", 2, 2)
        onward("mid", 1, (2, 0), 0)
        own("mid", 0, 4)

    @at_end
    def _():
        onward("end", 1, (0, 1), 1)

    member_squares(4, 8)

    @at_mid
    def _():
        onward("mid", 0, (3, 0), 1, 0)
        onward("mid", 0, (1, 1), 1)
        send("mid", 1, 1, (2, 0))
        onward("mid", 2, (0, 0), 2)
        own("mid", 2, 3)

    @at_end
    def _():
        onward("end", 0, (2, 0), 0)
        onward("end", 2, (0, 1), 1)

    relay_tokens(1)

    @at_mid
    def _():
        onward("mid", 1, (3, 0), 1, 0)
        own("mid", 1, 2)
        onward("mid", 3, (0, 0), 2)
        own("mid", 2, 4)

    @at_end
    def _():
        onward("end", 0, (3, 0), 0)
        onward("end", 1, (1, 0), 0)
        own("end", 0, 4)
        onward("end", 3, (0, 1), 1)
        own("end", 1, 4)

    relay_tokens(2)

    @at_mid
    def _():
        onward("mid", 2, (2, 0), 1, 0)
        onward("mid", 4, (0, 0), 2)

    @at_end
    def _():
        onward("end", 1, (2, 0), 0)

    relay_tokens(3)

    @at_mid
    def _():
        onward("mid", 2, (3, 0), 1, 0)
        own("mid", 1, 3)
        onward("mid", 2, (1, 1), 1)
        onward("mid", 3, (2, 0), 1, 0)

    core_copy(core_peer).wait_recv()
    rest(0)
    keyval_rows(0, 4)

    @at_end
    def _():
        onward("end", 1, (3, 0), 0)
        onward("end", 4, (0, 1), 1)

    relay_tokens(4)

    @at_mid
    def _():
        onward("mid", 3, (3, 0), 1, 0)
        onward("mid", 4, (2, 0), 1, 0)

    relay_tokens(5)

    @at_end
    def _():
        onward("end", 2, (2, 0), 0)

    @at_mid
    def _():
        onward("mid", 4, (3, 0), 1, 0)
        own("mid", 1, 4)
        onward("mid", 4, (1, 1), 1)

    keyval_rows(4, 6)

    @at_end
    def _():
        onward("end", 2, (3, 0), 0)

    relay_tokens(6)
    load_out.wait()
    own_out = out_copy(0, mp, y_peer)
    own_out.start()
    beside_out = out_copy(1, mp, core_peer)
    beside_out.start()
    rest(1)
    query_block(1, 0, 3)

    @at_end
    def _():
        onward("end", 3, (1, 0), 0)

    relay_tokens(7)
    keyval_rows(6, 8)
    query_block(1, 3, 4)
    pool()

    @at_end
    def _():
        onward("end", 3, (2, 0), 0)

    rest(2)
    query_block(2, 0, 2)

    @at_end
    def _():
        onward("end", 3, (3, 0), 0)

    query_block(2, 2, 4)

    @at_end
    def _():
        onward("end", 4, (2, 0), 0)
        onward("end", 4, (3, 0), 0)

    limit = counts[0] * 0
    for c in range(counts.shape[0]):
        limit = limit + jnp.where(owner[c] == dp, counts[c], 0)
    member_count = members.shape[0]
    member = mp * member_count + lax.broadcasted_iota(jnp.int32, (1, member_count), 1)
    scale = jnp.where(member < limit, logit_scale, 0.0) * lax.rsqrt(squares[...].T[0:1, :] + 1e-06)
    rest(3)
    query_block(3, 0, 4)
    out_copy(0, y_peer, y_peer).wait_recv()
    onward_out = out_copy(2, y_peer, core_peer)
    onward_out.start()
    rest(4)
    query_block(4, 0, 4)

    lane_head = (place_lane // GROUP) % 2

    def pick(h):
        right = (upper if h < 4 else jnp.logical_not(upper)) & (lane_head == h % 2)
        return jnp.where(right & (held == slot_wide), 1.0, 0.0).astype(HALF)[:, :64]

    for block in range(4):
        value = jnp.zeros((64, 128), FULL)
        for h in (block, block + 4):
            if h < 7:
                rows = ctx[h // 2].reshape(64, 128).astype(HALF)
                value = value + jnp.dot(pick(h), rows, preferred_element_type=FULL)
        cout[:, :, block * 128 : (block + 1) * 128] = value.astype(HALF).reshape(4, 16, 128)

    def group_copy(j, m_slot):
        to = (mp + j) % 4
        return remote(
            cout.at[to], cin.at[dp, m_slot], a_send.at[j], a_recv.at[m_slot], dp, to
        )

    def context_copy(i, d_slot):
        to_z = (z + i) % 4
        return remote(
            cin.at[d_slot], cin.at[d_slot], c_send.at[i], c_recv.at[d_slot], 2 * to_z + x, mp
        )

    def beside_copy(k, d_slot):
        return remote(
            cin.at[d_slot], cin.at[d_slot], b_send.at[k], c_recv.at[d_slot], x_peer, mp
        )

    for j in range(1, 4):
        group_copy(j, mp).start()
    cin[dp, mp] = cout[mp]
    for j in range(1, 4):
        group_copy(j, (mp + j) % 4).wait_recv()
    beside_copy(0, dp).start()
    for i in (2, 1, 3):
        context_copy(i, dp).start()
    out_copy(1, core_peer, core_peer).wait_recv()
    out_copy(2, far, core_peer).wait_recv()
    for i in range(1, 8):
        pool_copy(i, (dp + i) % 8).wait_recv()
    for i in (1, 3, 2):
        slot = 2 * ((z + i) % 4) + x
        context_copy(i, slot).wait_recv()
        beside_copy(i, slot).start()
    for i in (0, 1, 3, 2):
        beside_copy(i, 2 * ((z + i) % 4) + 1 - x).wait_recv()

    half_out = wot.shape[0]
    total_a = jnp.zeros((128, half_out), FULL)
    total_b = jnp.zeros((128, half_out), FULL)
    for j in range(4):
        m = (mp + j) % 4
        have = cin[:, m].reshape(128, 512)
        total_a = total_a + lax.dot_general(
            have, wot[:, pl.ds(pl.multiple_of(m * part, 128), 512)], NT,
            preferred_element_type=FULL,
        )
        total_b = total_b + lax.dot_general(
            have[:, : part - 512],
            wot[:, pl.ds(pl.multiple_of(m * part + 512, 128), part - 512)], NT,
            preferred_element_type=FULL,
        )
    embedded = (
        total_a.reshape(8, 16, half_out)[:, :8]
        + total_b.reshape(8, 16, half_out)[:, 8:]
    ).reshape(64, half_out)
    pooled = pool_in[...].astype(FULL)
    embedded = embedded + jnp.concatenate(
        [pooled[:, :8].reshape(64, 256), pooled[:, 8:].reshape(64, 256)[:, : half_out - 256]],
        axis=1,
    )
    row = lax.broadcasted_iota(jnp.int32, (64, 64), 0)
    column = lax.broadcasted_iota(jnp.int32, (64, 64), 1)
    order = jnp.where(
        column == ((row // 4) % 8) * 8 + (row // 32) * 4 + row % 4, 1.0, 0.0
    ).astype(HALF)
    sums[...] = (
        jnp.dot(order, embedded.astype(HALF), preferred_element_type=FULL)
        .astype(HALF)
        .reshape(sums.shape)
    )

    core = mp % 2
    home = 2 * x + (z + 1) // 2 % 2

    def sum_copy(j, y):
        return remote(
            sums.at[j], rows_in.at[dp], d_send.at[j, y], d_recv.at[dp], owner_of(mp, j), 2 * y + x
        )

    def hand_copy(k, slot):
        return remote(
            rows_in.at[slot], rows_in.at[slot], e_send.at[k], d_recv.at[slot], dp, core_peer
        )

    for j in range(2):
        for y in range(2):
            mine = (owner_of(mp, j) == dp) & (2 * y + x == mp)

            @pl.when(jnp.logical_not(mine))
            def _():
                sum_copy(j, y).start()

            @pl.when(mine)
            def _():
                rows_in[dp] = sums[j]

    for k in range(4):
        slot = 2 * k + core

        @pl.when(jnp.logical_not((slot == dp) & (mp == home)))
        def _():
            hand_copy(k, slot).wait_recv()

        hand_copy(k, slot).start()
    for k in range(4):
        hand_copy(k, 2 * k + 1 - core).wait_recv()

    for slot in range(8):
        joined[:, slot * half_out : (slot + 1) * half_out] = rows_in[slot].astype(FULL)
    embedding = joined[...]
    dots = lax.dot_general(
        embedding.astype(HALF), members[...], NT, preferred_element_type=FULL
    )
    inverse = lax.rsqrt(jnp.sum(embedding * embedding, axis=-1, keepdims=True) + 1e-06)
    found = (dots * inverse * scale).astype(HALF)
    row = lax.broadcasted_iota(jnp.int32, (128, 32), 0)
    column = lax.broadcasted_iota(jnp.int32, (128, 32), 1)
    value = jnp.zeros((128, 128), FULL)
    for q in range(4):
        spread = jnp.where(
            ((row % 16) // 4 == q) & (column == (row // 16) * 4 + row % 4), 1.0, 0.0
        ).astype(HALF)
        value = value + jnp.dot(
            spread, found[:, q * 128 : (q + 1) * 128], preferred_element_type=FULL
        )
    replies[...] = value.astype(HALF).reshape(replies.shape)

    def reply_copy(i, slot):
        to = (dp + i) % 8
        return remote(replies.at[to], arrived.at[slot], f_send.at[i], f_recv.at[slot], to, mp)

    for i in range(1, 8):
        reply_copy(i, dp).start()
    arrived[dp] = replies[dp]
    for i in range(1, 8):
        reply_copy(i, (dp + i) % 8).wait_recv()
    have = arrived[...].reshape(128, 128)
    column = lax.broadcasted_iota(jnp.int32, (dialogs, 128), 1).astype(FULL)
    for q in range(4):
        fetch = jnp.where(column == reply_place + 4.0 * q, flag_col, 0.0).astype(HALF)
        out[:, q * 128 : (q + 1) * 128] = jnp.dot(fetch, have, preferred_element_type=FULL)

    for r in range(chunks):
        y_copy(r, mp).wait_send()
        forward_copy(r, y_peer).wait_send()
    core_copy(mp).wait_send()
    own_out.wait_send()
    beside_out.wait_send()
    onward_out.wait_send()

    @at_end
    def _():
        for way, c, kind in sent["end"]:
            weight_copy(way, c, kind).wait_send()

    @at_mid
    def _():
        for way, c, kind in sent["mid"]:
            weight_copy(way, c, kind).wait_send()

    for j in range(2):
        for y in range(2):
            @pl.when(jnp.logical_not((owner_of(mp, j) == dp) & (2 * y + x == mp)))
            def _():
                sum_copy(j, y).wait_send()

    for k in range(4):
        hand_copy(k, 2 * k + core).wait_send()
        beside_copy(k, dp).wait_send()
    for i in range(1, 4):
        group_copy(i, mp).wait_send()
        context_copy(i, dp).wait_send()
    for i in range(1, 8):
        reply_copy(i, dp).wait_send()
        pool_copy(i, dp).wait_send()


def fused(
    tokens, norm_gain, w_query, w_keyval, w_out, residents, lengths, cluster, owner, counts, flags
):
    dialogs, seq_len, part = tokens.shape
    total = dialogs * seq_len
    depth, queries = w_query.shape
    width = norm_gain.shape[0]
    member_count = residents.shape[1]
    half_out = w_out.shape[1]
    half = HEAD_DIM // 2
    freqs = rope_base ** (-np.arange(half, dtype=np.float64) * 2.0 / HEAD_DIM)
    angles = np.arange(seq_len, dtype=np.float64)[:, None] * freqs[None, :]
    cosine, sine = np.cos(angles), np.sin(angles)
    cosine = np.tile(np.concatenate([cosine, cosine], axis=1), (CHUNK, 1)).astype(np.float32)
    sine = np.tile(np.concatenate([-sine, sine], axis=1), (CHUNK, 1)).astype(np.float32)
    vmem = pl.BlockSpec(memory_space=pltpu.VMEM)
    smem = pl.BlockSpec(memory_space=pltpu.SMEM)
    hbm = pl.BlockSpec(memory_space=pltpu.HBM)
    sem = pltpu.SemaphoreType.DMA
    return pl.pallas_call(
        fused_kernel,
        out_shape=jax.ShapeDtypeStruct((dialogs, member_count), FULL),
        in_specs=[smem] * 5 + [hbm, hbm, hbm, vmem, hbm, hbm, vmem, vmem],
        out_specs=vmem,
        scratch_shapes=[
            pltpu.VMEM((total, width), HALF),
            pltpu.VMEM((4, width, 256), HALF),
            pltpu.VMEM((width, 128), HALF),
            pltpu.VMEM((half_out, width), HALF),
            pltpu.VMEM((member_count, width), HALF),
            pltpu.VMEM((depth, queries), HALF),
            pltpu.VMEM((depth, 2, 128), HALF),
            pltpu.VMEM((512, 128), FULL),
            pltpu.VMEM((total, 128), FULL),
            pltpu.VMEM((total, 128), HALF),
            pltpu.VMEM((total, 128), HALF),
            pltpu.VMEM((2, GROUP * seq_len, 256), HALF),
            pltpu.VMEM((4, 4, 16, 128), FULL),
            pltpu.VMEM((dialogs, total), HALF),
            pltpu.VMEM((8, 16, 256), HALF),
            pltpu.VMEM((8, 16, 256), HALF),
            pltpu.VMEM((4, 16, 512), HALF),
            pltpu.VMEM((8, 4, 16, 512), HALF),
            pltpu.VMEM((2, 32, half_out), HALF),
            pltpu.VMEM((8, 32, half_out), HALF),
            pltpu.VMEM((32, width), FULL),
            pltpu.VMEM((member_count, 128), FULL),
            pltpu.VMEM((8, 16, 128), HALF),
            pltpu.VMEM((8, 16, 128), HALF),
            sem((5,)),
            sem((8,)),
            sem((8,)),
            sem,
            sem,
            sem((8,)),
            sem((8,)),
            sem((3, 5, 8)),
            sem((5, 8)),
            sem((3,)),
            sem((3,)),
            sem((8,)),
            sem((8,)),
            sem((4,)),
            sem((4,)),
            sem((4,)),
            sem((4,)),
            sem((8,)),
            sem((2, 2)),
            sem((8,)),
            sem((4,)),
            sem((8,)),
            sem((8,)),
        ],
        compiler_params=pltpu.CompilerParams(
            collective_id=0, has_side_effects=True, vmem_limit_bytes=58 * 1024 * 1024
        ),
    )(
        lengths, cluster[:, 0], owner, counts, flags,
        tokens.reshape(total, part), w_query, w_keyval,
        norm_gain.reshape(-1, 128), w_out.T, residents[0], cosine, sine,
    )


def plain_project(tokens, norm_gain, w_query, w_keyval, lengths):
    gathered = lax.all_gather(tokens, "mp", axis=2, tiled=True)
    dialogs, seq_len, width = gathered.shape
    hidden = gathered.astype(jnp.float32)
    normed = (
        hidden * lax.rsqrt(jnp.mean(hidden * hidden, axis=-1, keepdims=True) + 1e-06) * norm_gain
    ).astype(jnp.bfloat16)
    normed_flat = normed.reshape(dialogs * seq_len, width)
    query_cols = w_query.shape[1]
    keyval_cols = w_keyval.shape[2]
    pieces = (
        lax.all_gather(w_query, "dp", axis=0, tiled=True),
        lax.all_gather(w_keyval, "dp", axis=0, tiled=True),
    )
    keyval_piece = pieces[1].reshape(pieces[1].shape[0], 2 * keyval_cols)
    query_sum = jnp.dot(normed_flat, pieces[0], preferred_element_type=jnp.float32)
    keyval_sum = jnp.dot(normed_flat, keyval_piece, preferred_element_type=jnp.float32)
    positions = jnp.arange(seq_len)
    local_heads = query_cols // HEAD_DIM
    local_kv = keyval_cols // HEAD_DIM
    query = jax.vmap(lambda block: rotate(block, positions))(
        query_sum.reshape(dialogs, seq_len, local_heads, HEAD_DIM)
    ).astype(jnp.bfloat16)
    keys = jax.vmap(lambda block: rotate(block, positions))(
        keyval_sum[:, :keyval_cols].reshape(dialogs, seq_len, local_kv, HEAD_DIM)
    ).astype(jnp.bfloat16)
    values = (
        keyval_sum[:, keyval_cols:]
        .reshape(dialogs, seq_len, local_kv, HEAD_DIM)
        .astype(jnp.bfloat16)
    )
    valid = (positions[None, :] < lengths[:, None]).astype(jnp.float32)
    pooled_input = (
        jnp.sum(hidden * valid[:, :, None], axis=1) / lengths.astype(jnp.float32)[:, None]
    )
    pooled_context = jax.vmap(attend)(query, keys, values, lengths).astype(jnp.bfloat16)
    return pooled_context, pooled_input


def plain_score(pooled_context, pooled_input, w_out, members, onehot, live):
    dialogs = pooled_context.shape[0]
    everyone = lax.all_gather(pooled_context, "dp", axis=0, tiled=True)
    slices = jnp.dot(everyone, w_out, preferred_element_type=jnp.float32).astype(jnp.bfloat16)
    slices = slices.reshape(-1, dialogs, w_out.shape[1])
    slices = lax.all_to_all(slices, "dp", split_axis=0, concat_axis=0, tiled=True)
    partial_out = slices.transpose(1, 0, 2).reshape(dialogs, -1)
    projected = lax.psum(partial_out, "mp").astype(jnp.float32)
    embedding = pooled_input + projected
    unit = embedding * lax.rsqrt(jnp.sum(embedding * embedding, axis=-1, keepdims=True) + 1e-06)
    unit = unit.astype(jnp.bfloat16)
    inverse_norm = lax.rsqrt(
        jnp.einsum("md,md->m", members, members, preferred_element_type=jnp.float32) + 1e-06
    )
    outgoing = jnp.einsum(
        "ocn,nd->ocd", onehot.astype(jnp.bfloat16), unit, preferred_element_type=jnp.float32
    ).astype(jnp.bfloat16)
    query_rows = lax.all_to_all(outgoing, "dp", split_axis=0, concat_axis=0, tiled=True)
    dots = lax.dot_general(
        query_rows,
        members,
        (((query_rows.ndim - 1,), (1,)), ((), ())),
        preferred_element_type=jnp.float32,
    )
    return lax.all_to_all(
        jnp.where(live[0] > 0, live[0] * dots * inverse_norm, 0.0).astype(jnp.bfloat16),
        "dp",
        split_axis=0,
        concat_axis=0,
        tiled=True,
    )


def general(
    tokens, norm_gain, w_query, w_keyval, w_out, residents, lengths, cluster, owner, counts, flags
):
    pooled_context, pooled_input = plain_project(tokens, norm_gain, w_query, w_keyval, lengths)
    dialogs = tokens.shape[0]
    my_index = lax.axis_index("dp")
    owner_count = lax.axis_size("dp")
    my_count = jnp.sum(jnp.where(owner == my_index, counts, 0))
    members = residents[0]
    member_count = members.shape[0]
    member_start = lax.axis_index("mp") * member_count
    live = jnp.where(member_start + jnp.arange(member_count) < my_count, logit_scale, 0.0)[None, :]
    table_size = owner.shape[0]
    cluster_ids = cluster[:, 0]
    destination = jnp.sum(
        jnp.where(jnp.arange(table_size)[None, :] == cluster_ids[:, None], owner[None, :], 0),
        axis=1,
    )
    capacity = max(1, -(-dialogs // owner_count))
    order = jnp.arange(dialogs)
    earlier = (destination[None, :] == destination[:, None]) & (order[None, :] < order[:, None])
    rank = jnp.sum(earlier.astype(jnp.int32), axis=1)
    onehot = (jnp.arange(owner_count)[:, None, None] == destination[None, None, :]) & (
        jnp.arange(capacity)[None, :, None] == rank[None, None, :]
    )
    returned = plain_score(pooled_context, pooled_input, w_out, members, onehot, live)
    similarity = jnp.einsum(
        "ocn,ocm->nm", onehot.astype(jnp.bfloat16), returned, preferred_element_type=jnp.float32
    )
    return similarity * flags.astype(jnp.float32)[:, None]


def local(*args):
    if lax.axis_size("dp") == 8 and lax.axis_size("mp") == 4:
        return fused(*args)
    return general(*args)


def solution(mesh):
    in_specs = (
        P("dp", None, "mp"),
        P(),
        P("dp", "mp"),
        P("dp", None, "mp"),
        P("mp", "dp"),
        P("dp", "mp"),
        P("dp"),
        P("dp"),
        P(),
        P(),
        P("dp"),
    )
    out_specs = P("dp", "mp")
    return jax.shard_map(local, mesh=mesh, in_specs=in_specs, out_specs=out_specs, check_vma=False)
```

```python
import math

import jax
import jax.numpy as jnp
import numpy as np
from jax import lax
from jax.experimental import pallas as pl
from jax.experimental.pallas import tpu as pltpu
from jax.sharding import PartitionSpec as P

HEAD_DIM = 128


rope_base = 1000000.0
logit_scale = 100.0


def rotate(values, positions):
    half = values.shape[-1] // 2
    freqs = rope_base ** (-jnp.arange(half, dtype=jnp.float32) * 2.0 / values.shape[-1])
    angles = positions.astype(jnp.float32)[:, None] * freqs[None, :]
    cosine = jnp.cos(angles)[:, None, :]
    sine = jnp.sin(angles)[:, None, :]
    first = values[..., :half]
    second = values[..., half:]
    return jnp.concatenate(
        [first * cosine - second * sine, second * cosine + first * sine], axis=-1
    )


def attend(query, keys, values, length):
    seq_len = query.shape[0]
    kv_count = keys.shape[1]
    group = query.shape[1] // kv_count
    grouped = query.reshape(seq_len, kv_count, group, query.shape[-1])
    scores = jnp.einsum(
        "qkgd,pkd->kgqp", grouped, keys, preferred_element_type=jnp.float32
    ) / math.sqrt(query.shape[-1])
    row_pos = jnp.arange(seq_len)[:, None]
    col_pos = jnp.arange(seq_len)[None, :]
    allowed = (col_pos <= row_pos) & (col_pos < length)
    scores = jnp.where(allowed, scores, -1e30)
    highest = jnp.max(scores, axis=-1, keepdims=True)
    expanded = jnp.exp(scores - highest)
    weights = (expanded / jnp.sum(expanded, axis=-1, keepdims=True)).astype(jnp.bfloat16)
    context = jnp.einsum("kgqp,pkd->qkgd", weights, values, preferred_element_type=jnp.float32)
    valid = (jnp.arange(seq_len) < length).astype(jnp.float32)
    pooled = jnp.sum(context * valid[:, None, None, None], axis=0) / length.astype(jnp.float32)
    return pooled.reshape(-1)


MESH = pl.DeviceIdType.MESH
HALF, FULL = jnp.bfloat16, jnp.float32
CHUNK = 4
GROUP = 8
NT = (((1,), (1,)), ((), ()))


def fused_kernel(
    lens, cluster, owner, counts, flags,
    tin, query_in, keyval_in, gain, w_out_in, members_in, cosine, sine,
    out,
    tok, wide, narrow, wot, members, qstage, kvstage, gcol, rs, kst, vst, qst, ctx, mask,
    acc_wide, acc_narrow, pool_out, pool_in, cout_a, cout_b, cout_c, cin_a, cin_b, cin_c, sums, rows_in, joined, squares, replies, arrived,
    l_sem, ty_send, ty_recv, tc_send, tc_recv, tf_send, tf_recv, wsend, wrecv,
    o_send, o_recv, p_send, p_recv, a_send, a_recv, c_send, c_recv,
    d_send, d_recv, e_send, f_send, f_recv,
):
    dp = lax.axis_index("dp")
    mp = lax.axis_index("mp")
    z, x = dp // 2, dp % 2
    high = z // 2
    core_peer = mp + 1 - 2 * (mp % 2)
    y_peer = (mp + 2) % 4
    far = (core_peer + 2) % 4
    pair_z = z + 1 - 2 * (z % 2)
    x_peer = 2 * z + 1 - x
    total, part = tin.shape
    depth, queries = query_in.shape
    width = tok.shape[1]
    dialogs = lens.shape[0]
    seq_len = total // dialogs
    rows_each = CHUNK * seq_len
    chunks = total // rows_each
    end = (z == 0) | (z == 3)
    mid = (z == 1) | (z == 2)

    def across(k):
        return k + high * (3 - 2 * k)

    def slot_of(kind):
        k, prime = kind
        return 2 * across(k) + (1 - x if prime else x)

    def lanes_of(m):
        return pl.ds(pl.multiple_of(m * part, 128), part)

    def rows_of(r):
        return pl.ds(pl.multiple_of(r * rows_each, 64), rows_each)

    def remote(source, target, send, recv, dp_to, mp_to):
        return pltpu.make_async_remote_copy(
            src_ref=source, dst_ref=target, send_sem=send, recv_sem=recv,
            device_id={"dp": dp_to, "mp": mp_to}, device_id_type=MESH,
        )

    load_query = pltpu.make_async_copy(query_in, qstage, l_sem.at[0])
    load_keyval = pltpu.make_async_copy(keyval_in, kvstage, l_sem.at[1])
    load_tokens = pltpu.make_async_copy(tin, tok.at[:, lanes_of(mp)], l_sem.at[2])
    load_members = pltpu.make_async_copy(members_in, members, l_sem.at[3])
    load_out = pltpu.make_async_copy(w_out_in, wot.at[:, lanes_of(mp)], l_sem.at[4])
    load_keyval.start()
    load_query.start()

    barrier = pltpu.get_barrier_semaphore()

    def greet(dp_to, mp_to):
        pl.semaphore_signal(
            barrier, inc=1, device_id={"dp": dp_to, "mp": mp_to}, device_id_type=MESH
        )

    greet(dp, core_peer)
    greet(dp, y_peer)
    greet(x_peer, mp)
    greet(2 * pair_z + x, mp)

    @pl.when(mid)
    def _():
        greet(2 * across(2) + x, mp)

    load_tokens.start()
    load_members.start()
    load_out.start()

    first = (7 * dp) // 2
    for i in range(4):
        row = gain[pl.ds(first + i, 1), :]
        gcol[i * 128 : (i + 1) * 128, :] = jnp.broadcast_to(row, (128, 128)).T
    own_rows = pl.ds(pl.multiple_of(dp * depth, 64), depth)

    def gained(piece):
        factor = gcol[pl.ds(pl.multiple_of((dp % 2) * 64, 64), depth), :]
        return (piece.astype(FULL) * factor).astype(HALF)

    def fill_keyval():
        for i in range(2):
            wide[0, own_rows, i * 128 : (i + 1) * 128] = gained(kvstage[:, i, :])

    def fill_query(c):
        for h in range(2 * c - 2, min(2 * c, 7)):
            piece = gained(qstage[:, h * 128 : (h + 1) * 128])
            if h < 6:
                wide[c, own_rows, (h % 2) * 128 : (h % 2 + 1) * 128] = piece
            else:
                narrow[own_rows, :] = piece

    load_keyval.wait()
    fill_keyval()

    @pl.when(end)
    def _():
        pl.semaphore_wait(barrier, 4)

    @pl.when(mid)
    def _():
        pl.semaphore_wait(barrier, 5)

    def block_ref(c, slot):
        rows = pl.ds(pl.multiple_of(slot * depth, 64), depth)
        return wide.at[c, rows, :] if c < 4 else narrow.at[rows, :]

    ways = (x_peer, 2 * pair_z + x, 2 * across(2) + x)
    own_kind = {"end": (0, 0), "mid": (1, 0)}
    sent = {"end": [], "mid": []}
    waited = {"end": set(), "mid": set()}
    every = {
        "end": [(0, 1), (1, 0), (1, 1), (2, 0), (2, 1), (3, 0), (3, 1)],
        "mid": [(0, 0), (0, 1), (1, 1), (2, 0), (2, 1), (3, 0), (3, 1)],
    }

    def weight_copy(way, c, kind):
        slot = slot_of(kind)
        return remote(
            block_ref(c, slot), block_ref(c, slot), wsend.at[way, c, slot], wrecv.at[c, slot],
            ways[way], mp,
        )

    def send(role, way, c, kind):
        sent[role].append((way, c, kind))
        weight_copy(way, c, kind).start()

    def own(role, way, c):
        send(role, way, c, own_kind[role])

    def arrive(role, c, kind):
        if (c, kind) not in waited[role]:
            waited[role].add((c, kind))
            weight_copy(0, c, kind).wait_recv()

    def onward(role, c, kind, *to):
        arrive(role, c, kind)
        for way in to:
            send(role, way, c, kind)

    def at_end(f):
        pl.when(end)(f)

    def at_mid(f):
        pl.when(mid)(f)

    def rest(c):
        @at_end
        def _():
            for kind in every["end"]:
                arrive("end", c, kind)

        @at_mid
        def _():
            for kind in every["mid"]:
                arrive("mid", c, kind)

    def need(c, *groups):
        @at_end
        def _():
            for kind in every["end"]:
                if kind[0] in groups:
                    arrive("end", c, kind)

        @at_mid
        def _():
            for kind in every["mid"]:
                if kind[0] in groups:
                    arrive("mid", c, kind)

    def y_copy(r, m):
        return remote(
            tin.at[rows_of(r), :], tok.at[rows_of(r), lanes_of(m)], ty_send.at[r], ty_recv.at[r],
            dp, y_peer,
        )

    def forward_copy(r, m):
        return remote(
            tok.at[rows_of(r), lanes_of(m)], tok.at[rows_of(r), lanes_of(m)],
            tf_send.at[r], tf_recv.at[r], dp, core_peer,
        )

    def core_copy(m):
        return remote(tin, tok.at[:, lanes_of(m)], tc_send, tc_recv, dp, core_peer)

    def relay_tokens(r):
        y_copy(r, y_peer).wait_recv()
        forward_copy(r, y_peer).start()

    def out_copy(i, m, mp_to):
        return remote(
            wot.at[:, lanes_of(m)], wot.at[:, lanes_of(m)], o_send.at[i], o_recv.at[i], dp, mp_to
        )

    @at_end
    def _():
        own("end", 0, 0)
        own("end", 1, 0)

    @at_mid
    def _():
        own("mid", 1, 0)
        own("mid", 0, 0)
        own("mid", 2, 0)

    @pl.loop(0, chunks)
    def _(r):
        y_copy(r, mp).start()

    core_copy(mp).start()
    load_query.wait()
    fill_query(1)

    @at_end
    def _():
        own("end", 0, 1)
        own("end", 1, 1)

    @at_mid
    def _():
        own("mid", 1, 1)
        own("mid", 0, 1)
        own("mid", 2, 1)

    fill_query(2)
    fill_query(3)
    fill_query(4)

    @at_end
    def _():
        for c in (2, 3):
            own("end", 0, c)
            own("end", 1, c)

    @at_mid
    def _():
        for c in (2, 3):
            own("mid", 0, c)

    def owner_of(m, j):
        return 2 * (m % 2 + j * (3 - 2 * (m % 2))) + m // 2

    lane = lax.broadcasted_iota(jnp.int32, (dialogs, 128), 1)
    sub = lax.broadcasted_iota(jnp.int32, (dialogs, 128), 0)
    lane_dialog = GROUP * (lane // 16) + lane % GROUP
    to_col = jnp.zeros((dialogs, 128), jnp.int32)
    to_row = jnp.full((dialogs, 128), -64, jnp.int32)
    to_wide = jnp.full((dialogs, 128), -64, jnp.int32)
    len_col = jnp.zeros((dialogs, 128), jnp.int32)
    flag_col = jnp.zeros((dialogs, 128), jnp.int32)
    for d in range(dialogs):
        target = owner[cluster[d]]
        to_col = jnp.where(sub == d, target, to_col)
        to_row = jnp.where(lane == d, target, to_row)
        to_wide = jnp.where((lane_dialog == d) & (lane < 64), target, to_wide)
        len_col = jnp.where(sub == d, lens[d], len_col)
        flag_col = jnp.where(sub == d, flags[d], flag_col)
    len_col = len_col.astype(FULL)
    flag_col = flag_col.astype(FULL)
    rank_col = jnp.sum(
        jnp.where((to_col == to_row) & (lane < sub), 1.0, 0.0), axis=1, keepdims=True
    )
    rank_row = jnp.sum(
        jnp.where((to_col == to_row) & (sub < lane), 1.0, 0.0), axis=0, keepdims=True
    )
    rank_wide = jnp.sum(
        jnp.where((to_col == to_wide) & (sub < lane_dialog), 1.0, 0.0), axis=0, keepdims=True
    )
    slot_row = to_row[0:1].astype(FULL) * CHUNK + rank_row
    slot_wide = to_wide[0:1].astype(FULL) * CHUNK + rank_wide
    reply_place = to_col[:, 0:1].astype(FULL) * 16.0 + rank_col
    place = lax.broadcasted_iota(jnp.int32, (64, 128), 0)
    place_lane = lax.broadcasted_iota(jnp.int32, (64, 128), 1)
    upper = place % 16 < 8
    held = (owner_of(place // 16, (place % 8) // 4) * CHUNK + place % CHUNK).astype(FULL)
    part_row = lax.broadcasted_iota(jnp.int32, (16, 128), 0)
    part_held = (owner_of(mp, (part_row % 8) // 4) * CHUNK + part_row % CHUNK).astype(FULL)
    part_pick = jnp.where(part_held == slot_row, 1.0, 0.0)
    part_upper = jnp.where(part_row < 8, part_pick, 0.0).astype(HALF)[:, :dialogs]
    part_lower = jnp.where(part_row >= 8, part_pick, 0.0).astype(HALF)[:, :dialogs]

    index = lax.broadcasted_iota(jnp.int32, mask.shape, 1)
    start = lax.broadcasted_iota(jnp.int32, mask.shape, 0) * seq_len
    ahead = (index - start).astype(FULL)
    mask[...] = jnp.where((ahead >= 0.0) & (ahead < len_col[:, 0:1]), 1.0, 0.0).astype(HALF)
    load_tokens.wait()

    def pool_copy(i, source):
        to = (dp + i) % 8
        return remote(pool_out.at[to], pool_in.at[source], p_send.at[i], p_recv.at[source], to, mp)

    def pool():
        block = width // 8
        for m in range(4):
            some = tok[:, m * part : (m + 1) * part]
            mean = jnp.dot(mask[...], some, preferred_element_type=FULL)
            mean = (mean / len_col[:, 0:1]).astype(HALF)
            for j in range(2):
                lead = mean[:, j * block : j * block + 256]
                back = mean[:, j * block + 256 : (j + 1) * block]
                lower = jnp.dot(part_lower, back, preferred_element_type=FULL)
                pool_out[2 * m + j] = (
                    jnp.dot(part_upper, lead, preferred_element_type=FULL)
                    + jnp.concatenate([lower, jnp.zeros((16, 512 - block), FULL)], axis=1)
                ).astype(HALF)
        for i in range(1, 8):
            pool_copy(i, dp).start()
        pool_in[dp] = pool_out[dp]

    def normalize(r):
        for half in range(2):
            rows = pl.ds(pl.multiple_of(r * rows_each + half * (rows_each // 2), 32), rows_each // 2)
            values = tok[rows, :].astype(FULL)
            mean_square = jnp.sum(values * values, axis=-1, keepdims=True) * (1.0 / width)
            rs[rows, :] = jnp.broadcast_to(lax.rsqrt(mean_square + 1e-06), (rows_each // 2, 128))

    def turn(piece):
        return piece * cosine[...] + pltpu.roll(piece, HEAD_DIM // 2, 1) * sine[...]

    def keyval_rows(low, top):
        @pl.loop(low, top)
        def _(r):
            forward_copy(r, far).wait_recv()
            normalize(r)
            rows = rows_of(r)
            product = jnp.dot(tok[rows, :], wide[0], preferred_element_type=FULL)
            kst[rows, :] = turn(product[:, :HEAD_DIM] * rs[rows, :]).astype(HALF)
            vst[rows, :] = (product[:, HEAD_DIM:] * rs[rows, :]).astype(HALF)

    rows_group = GROUP * seq_len

    def product_of(c, rows, first, length):
        depth_rows = pl.ds(first, length)
        weights = wide[c, depth_rows, :] if c < 4 else narrow[depth_rows, :]
        return jnp.dot(tok[rows, pl.ds(first, length)], weights, preferred_element_type=FULL)

    def total_of(c):
        return acc_wide if c < 4 else acc_narrow

    def partial_block(c, first, length, fresh):
        @pl.loop(0, total // rows_group)
        def _(r):
            rows = pl.ds(pl.multiple_of(r * rows_group, 128), rows_group)
            product = product_of(c, rows, pl.multiple_of(first, 128), length)
            if fresh:
                total_of(c)[rows, :] = product
            else:
                total_of(c)[rows, :] += product

    def query_rows(c, r, slot):
        rows = pl.ds(pl.multiple_of(r * rows_group, 128), rows_group)
        if c < 3:
            product = product_of(c, rows, 0, width)
        else:
            last = pl.multiple_of(across(3) * part, 128)
            product = total_of(c)[rows, :] + product_of(c, rows, last, part)
        for h in range(product.shape[1] // HEAD_DIM):
            span = slice(h * HEAD_DIM, (h + 1) * HEAD_DIM)
            for half in range(2):
                here = slice(half * rows_each, (half + 1) * rows_each)
                some = pl.ds(
                    pl.multiple_of(r * rows_group + half * rows_each, 64), rows_each
                )
                qst[slot, here, span] = turn(product[here, span] * rs[some, :]).astype(HALF)

    def attend_rows(c, r, slot):
        heads = 2 if c < 4 else 1
        lanes = heads * seq_len
        key_pos = lax.broadcasted_iota(jnp.int32, (seq_len, lanes), 0)
        query_pos = lax.broadcasted_iota(jnp.int32, (seq_len, lanes), 1) % seq_len
        causal = key_pos <= query_pos
        position = lax.broadcasted_iota(jnp.int32, (1, lanes), 1) % seq_len
        pieces = []
        for item in range(GROUP):
            here = slice(item * seq_len, (item + 1) * seq_len)
            keys = kst[pl.ds(pl.multiple_of(r * rows_group + item * seq_len, 16), seq_len), :]
            stacked = qst[slot, here, :HEAD_DIM]
            if heads == 2:
                stacked = jnp.concatenate([stacked, qst[slot, here, HEAD_DIM:]], axis=0)
            scores = lax.dot_general(keys, stacked, NT, preferred_element_type=FULL)
            scores = jnp.where(causal, scores * (1.0 / math.sqrt(HEAD_DIM)), -1e30)
            expanded = jnp.exp(scores - jnp.max(scores, axis=0, keepdims=True))
            length = lens[r * GROUP + item]
            share = jnp.where(position < length, 1.0, 0.0) / (
                jnp.sum(expanded, axis=0, keepdims=True)
                * jnp.full((1, lanes), length, jnp.int32).astype(FULL)
            )
            pieces.append((expanded * share).astype(HALF))
        weights = jnp.concatenate(pieces, axis=0)
        head_row = lax.broadcasted_iota(jnp.int32, (16, lanes), 0) // GROUP
        head_lane = lax.broadcasted_iota(jnp.int32, (16, lanes), 1) // seq_len
        chosen = jnp.where(head_row == head_lane, 1.0, 0.0).astype(HALF)
        sums_of = lax.dot_general(chosen, weights, NT, preferred_element_type=FULL)
        item_row = lax.broadcasted_iota(jnp.int32, sums_of.shape, 0) % GROUP
        item_lane = lax.broadcasted_iota(jnp.int32, sums_of.shape, 1) // seq_len
        sums_of = jnp.where(item_row == item_lane, sums_of, 0.0)
        coarse = sums_of.astype(HALF).astype(FULL)
        both = jnp.concatenate([coarse, sums_of - coarse], axis=0).astype(HALF)
        rows = pl.ds(pl.multiple_of(r * rows_group, 128), rows_group)
        mixed = jnp.dot(both, vst[rows, :], preferred_element_type=FULL)
        ctx[c - 1, r] = mixed[:16] + mixed[16:]

    def query_block(c, low, top):
        query_rows(c, low, low % 2)

        @pl.loop(low + 1, top)
        def _(r):
            attend_rows(c, r - 1, (r - 1) % 2)
            query_rows(c, r, r % 2)

        attend_rows(c, top - 1, (top - 1) % 2)

    def member_squares(low, top):
        @pl.loop(low, top)
        def _(step):
            rows = pl.ds(pl.multiple_of(step * 64, 64), 64)
            values = members[rows, :].astype(FULL)
            squares[rows, :] = jnp.broadcast_to(
                jnp.sum(values * values, axis=-1, keepdims=True), (64, 128)
            )

    @at_mid
    def _():
        onward("mid", 0, (2, 0), 1, 0)
        onward("mid", 0, (0, 0), 2)

    @at_end
    def _():
        onward("end", 0, (0, 1), 1)

    load_members.wait()
    member_squares(0, 4)
    relay_tokens(0)

    @at_mid
    def _():
        onward("mid", 1, (0, 0), 2)
        own("mid", 2, 2)
        onward("mid", 1, (2, 0), 0)
        own("mid", 0, 4)

    @at_end
    def _():
        onward("end", 1, (0, 1), 1)

    member_squares(4, 8)

    @at_mid
    def _():
        onward("mid", 0, (3, 0), 1, 0)
        onward("mid", 0, (1, 1), 1)
        send("mid", 1, 1, (2, 0))
        onward("mid", 2, (0, 0), 2)
        own("mid", 2, 3)

    @at_end
    def _():
        onward("end", 0, (2, 0), 0)
        onward("end", 2, (0, 1), 1)

    relay_tokens(1)

    @at_mid
    def _():
        onward("mid", 1, (3, 0), 1, 0)
        own("mid", 1, 2)
        onward("mid", 3, (0, 0), 2)
        own("mid", 2, 4)

    @at_end
    def _():
        onward("end", 0, (3, 0), 0)
        onward("end", 1, (1, 0), 0)
        own("end", 0, 4)
        onward("end", 3, (0, 1), 1)
        own("end", 1, 4)

    relay_tokens(2)

    @at_mid
    def _():
        onward("mid", 2, (2, 0), 1, 0)
        onward("mid", 4, (0, 0), 2)

    @at_end
    def _():
        onward("end", 1, (2, 0), 0)

    relay_tokens(3)

    @at_mid
    def _():
        onward("mid", 2, (3, 0), 1, 0)
        own("mid", 1, 3)
        onward("mid", 2, (1, 1), 1)
        onward("mid", 3, (2, 0), 1, 0)

    core_copy(core_peer).wait_recv()
    rest(0)
    keyval_rows(0, 4)

    @at_end
    def _():
        onward("end", 1, (3, 0), 0)
        onward("end", 4, (0, 1), 1)

    relay_tokens(4)

    @at_mid
    def _():
        onward("mid", 3, (3, 0), 1, 0)
        onward("mid", 4, (2, 0), 1, 0)

    relay_tokens(5)

    @at_end
    def _():
        onward("end", 2, (2, 0), 0)

    @at_mid
    def _():
        onward("mid", 4, (3, 0), 1, 0)
        own("mid", 1, 4)
        onward("mid", 4, (1, 1), 1)

    keyval_rows(4, 6)

    @at_end
    def _():
        onward("end", 2, (3, 0), 0)

    relay_tokens(6)
    load_out.wait()
    own_out = out_copy(0, mp, y_peer)
    own_out.start()
    beside_out = out_copy(1, mp, core_peer)
    beside_out.start()
    rest(1)
    query_block(1, 0, 3)

    @at_end
    def _():
        onward("end", 3, (1, 0), 0)

    relay_tokens(7)
    keyval_rows(6, 8)
    query_block(1, 3, 4)
    pool()

    @at_end
    def _():
        onward("end", 3, (2, 0), 0)

    rest(2)
    query_block(2, 0, 2)

    @at_end
    def _():
        onward("end", 3, (3, 0), 0)

    query_block(2, 2, 4)

    lane_head = (place_lane // GROUP) % 2
    heads_of = (((0, 2), (1, 3)), ((4, 5),), ((6, None),))
    couts, cins = (cout_a, cout_b, cout_c), (cin_a, cin_b, cin_c)

    def pick(h, right):
        right = right & (lane_head == h % 2)
        return jnp.where(right & (held == slot_wide), 1.0, 0.0).astype(HALF)[:, :64]

    def group_copy(p, j, m_slot):
        to = (mp + j) % 4
        return remote(
            couts[p].at[to], cins[p].at[dp, m_slot], a_send.at[p, j], a_recv.at[p, m_slot], dp, to
        )

    def context_copy(p, i, d_slot):
        return remote(
            cins[p].at[d_slot], cins[p].at[d_slot], c_send.at[p, i], c_recv.at[p, d_slot],
            (dp + i) % 8, mp,
        )

    def share_part(p):
        for block, (top, bottom) in enumerate(heads_of[p]):
            rows = ctx[top // 2].reshape(64, 128).astype(HALF)
            value = jnp.dot(pick(top, upper), rows, preferred_element_type=FULL)
            if bottom is not None:
                rows = ctx[bottom // 2].reshape(64, 128).astype(HALF)
                value = value + jnp.dot(
                    pick(bottom, jnp.logical_not(upper)), rows, preferred_element_type=FULL
                )
            couts[p][:, :, block * 128 : (block + 1) * 128] = value.astype(HALF).reshape(
                4, 16, 128
            )
        for j in range(1, 4):
            group_copy(p, j, mp).start()
        cins[p][dp, mp] = couts[p][mp]

    def spread_part(p):
        for j in range(1, 4):
            group_copy(p, j, (mp + j) % 4).wait_recv()
        for i in (4, 3, 5, 2, 6, 1, 7):
            context_copy(p, i, dp).start()

    share_part(0)

    @at_end
    def _():
        onward("end", 4, (2, 0), 0)

    need(3, 0, 1, 2)
    partial_block(3, high * part, 3 * part, True)

    @at_end
    def _():
        onward("end", 4, (3, 0), 0)

    spread_part(0)
    need(4, 0)
    partial_block(4, across(0) * part, part, True)

    limit = counts[0] * 0
    for c in range(counts.shape[0]):
        limit = limit + jnp.where(owner[c] == dp, counts[c], 0)
    member_count = members.shape[0]
    member = mp * member_count + lax.broadcasted_iota(jnp.int32, (1, member_count), 1)
    scale = jnp.where(member < limit, logit_scale, 0.0) * lax.rsqrt(squares[...].T[0:1, :] + 1e-06)
    rest(3)
    query_block(3, 0, 4)
    share_part(1)
    need(4, 2)
    partial_block(4, across(2) * part, part, False)
    spread_part(1)
    need(4, 1)
    partial_block(4, across(1) * part, part, False)
    out_copy(0, y_peer, y_peer).wait_recv()
    onward_out = out_copy(2, y_peer, core_peer)
    onward_out.start()
    rest(4)
    query_block(4, 0, 4)
    share_part(2)
    out_copy(1, core_peer, core_peer).wait_recv()
    out_copy(2, far, core_peer).wait_recv()
    for i in range(1, 8):
        pool_copy(i, (dp + i) % 8).wait_recv()
    spread_part(2)

    half_out = wot.shape[0]
    total_a = jnp.zeros((128, half_out), FULL)
    total_b = jnp.zeros((128, half_out), FULL)

    def lanes_from(m, first, length):
        return wot[:, m * part + first : m * part + first + length]

    for p in range(3):
        for i in range(1, 8):
            context_copy(p, i, (dp + i) % 8).wait_recv()
        length = cins[p].shape[3]
        for m in range(4):
            have = cins[p][:, m].reshape(128, length)
            first = (0, 512, 768)[p]
            total_a = total_a + lax.dot_general(
                have, lanes_from(m, first, length), NT, preferred_element_type=FULL
            )
            if p < 2:
                total_b = total_b + lax.dot_general(
                    have, lanes_from(m, first + length, length), NT, preferred_element_type=FULL
                )
    embedded = (
        total_a.reshape(8, 16, half_out)[:, :8]
        + total_b.reshape(8, 16, half_out)[:, 8:]
    ).reshape(64, half_out)
    pooled = pool_in[...].astype(FULL)
    embedded = embedded + jnp.concatenate(
        [pooled[:, :8].reshape(64, 256), pooled[:, 8:].reshape(64, 256)[:, : half_out - 256]],
        axis=1,
    )
    row = lax.broadcasted_iota(jnp.int32, (64, 64), 0)
    column = lax.broadcasted_iota(jnp.int32, (64, 64), 1)
    order = jnp.where(
        column == ((row // 4) % 8) * 8 + (row // 32) * 4 + row % 4, 1.0, 0.0
    ).astype(HALF)
    sums[...] = (
        jnp.dot(order, embedded.astype(HALF), preferred_element_type=FULL)
        .astype(HALF)
        .reshape(sums.shape)
    )

    core = mp % 2
    home = 2 * x + (z + 1) // 2 % 2

    def sum_copy(j, y):
        return remote(
            sums.at[j], rows_in.at[dp], d_send.at[j, y], d_recv.at[dp], owner_of(mp, j), 2 * y + x
        )

    def hand_copy(k, slot):
        return remote(
            rows_in.at[slot], rows_in.at[slot], e_send.at[k], d_recv.at[slot], dp, core_peer
        )

    for j in range(2):
        for y in range(2):
            mine = (owner_of(mp, j) == dp) & (2 * y + x == mp)

            @pl.when(jnp.logical_not(mine))
            def _():
                sum_copy(j, y).start()

            @pl.when(mine)
            def _():
                rows_in[dp] = sums[j]

    for k in range(4):
        slot = 2 * k + core

        @pl.when(jnp.logical_not((slot == dp) & (mp == home)))
        def _():
            hand_copy(k, slot).wait_recv()

        hand_copy(k, slot).start()
    for k in range(4):
        hand_copy(k, 2 * k + 1 - core).wait_recv()

    for slot in range(8):
        joined[:, slot * half_out : (slot + 1) * half_out] = rows_in[slot].astype(FULL)
    embedding = joined[...]
    dots = lax.dot_general(
        embedding.astype(HALF), members[...], NT, preferred_element_type=FULL
    )
    inverse = lax.rsqrt(jnp.sum(embedding * embedding, axis=-1, keepdims=True) + 1e-06)
    found = (dots * inverse * scale).astype(HALF)
    row = lax.broadcasted_iota(jnp.int32, (128, 32), 0)
    column = lax.broadcasted_iota(jnp.int32, (128, 32), 1)
    value = jnp.zeros((128, 128), FULL)
    for q in range(4):
        spread = jnp.where(
            ((row % 16) // 4 == q) & (column == (row // 16) * 4 + row % 4), 1.0, 0.0
        ).astype(HALF)
        value = value + jnp.dot(
            spread, found[:, q * 128 : (q + 1) * 128], preferred_element_type=FULL
        )
    replies[...] = value.astype(HALF).reshape(replies.shape)

    def reply_copy(i, slot):
        to = (dp + i) % 8
        return remote(replies.at[to], arrived.at[slot], f_send.at[i], f_recv.at[slot], to, mp)

    for i in range(1, 8):
        reply_copy(i, dp).start()
    arrived[dp] = replies[dp]
    for i in range(1, 8):
        reply_copy(i, (dp + i) % 8).wait_recv()
    have = arrived[...].reshape(128, 128)
    column = lax.broadcasted_iota(jnp.int32, (dialogs, 128), 1).astype(FULL)
    for q in range(4):
        fetch = jnp.where(column == reply_place + 4.0 * q, flag_col, 0.0).astype(HALF)
        out[:, q * 128 : (q + 1) * 128] = jnp.dot(fetch, have, preferred_element_type=FULL)

    for r in range(chunks):
        y_copy(r, mp).wait_send()
        forward_copy(r, y_peer).wait_send()
    core_copy(mp).wait_send()
    own_out.wait_send()
    beside_out.wait_send()
    onward_out.wait_send()

    @at_end
    def _():
        for way, c, kind in sent["end"]:
            weight_copy(way, c, kind).wait_send()

    @at_mid
    def _():
        for way, c, kind in sent["mid"]:
            weight_copy(way, c, kind).wait_send()

    for j in range(2):
        for y in range(2):
            @pl.when(jnp.logical_not((owner_of(mp, j) == dp) & (2 * y + x == mp)))
            def _():
                sum_copy(j, y).wait_send()

    for k in range(4):
        hand_copy(k, 2 * k + core).wait_send()
    for i in range(1, 4):
        for p in range(3):
            group_copy(p, i, mp).wait_send()
    for i in range(1, 8):
        for p in range(3):
            context_copy(p, i, dp).wait_send()
        reply_copy(i, dp).wait_send()
        pool_copy(i, dp).wait_send()


def fused(
    tokens, norm_gain, w_query, w_keyval, w_out, residents, lengths, cluster, owner, counts, flags
):
    dialogs, seq_len, part = tokens.shape
    total = dialogs * seq_len
    depth, queries = w_query.shape
    width = norm_gain.shape[0]
    member_count = residents.shape[1]
    half_out = w_out.shape[1]
    half = HEAD_DIM // 2
    freqs = rope_base ** (-np.arange(half, dtype=np.float64) * 2.0 / HEAD_DIM)
    angles = np.arange(seq_len, dtype=np.float64)[:, None] * freqs[None, :]
    cosine, sine = np.cos(angles), np.sin(angles)
    cosine = np.tile(np.concatenate([cosine, cosine], axis=1), (CHUNK, 1)).astype(np.float32)
    sine = np.tile(np.concatenate([-sine, sine], axis=1), (CHUNK, 1)).astype(np.float32)
    vmem = pl.BlockSpec(memory_space=pltpu.VMEM)
    smem = pl.BlockSpec(memory_space=pltpu.SMEM)
    hbm = pl.BlockSpec(memory_space=pltpu.HBM)
    sem = pltpu.SemaphoreType.DMA
    return pl.pallas_call(
        fused_kernel,
        out_shape=jax.ShapeDtypeStruct((dialogs, member_count), FULL),
        in_specs=[smem] * 5 + [hbm, hbm, hbm, vmem, hbm, hbm, vmem, vmem],
        out_specs=vmem,
        scratch_shapes=[
            pltpu.VMEM((total, width), HALF),
            pltpu.VMEM((4, width, 256), HALF),
            pltpu.VMEM((width, 128), HALF),
            pltpu.VMEM((half_out, width), HALF),
            pltpu.VMEM((member_count, width), HALF),
            pltpu.VMEM((depth, queries), HALF),
            pltpu.VMEM((depth, 2, 128), HALF),
            pltpu.VMEM((512, 128), FULL),
            pltpu.VMEM((total, 128), FULL),
            pltpu.VMEM((total, 128), HALF),
            pltpu.VMEM((total, 128), HALF),
            pltpu.VMEM((2, GROUP * seq_len, 256), HALF),
            pltpu.VMEM((4, 4, 16, 128), FULL),
            pltpu.VMEM((dialogs, total), HALF),
            pltpu.VMEM((total, 256), FULL),
            pltpu.VMEM((total, 128), FULL),
            pltpu.VMEM((8, 16, 256), HALF),
            pltpu.VMEM((8, 16, 256), HALF),
            pltpu.VMEM((4, 16, 256), HALF),
            pltpu.VMEM((4, 16, 128), HALF),
            pltpu.VMEM((4, 16, 128), HALF),
            pltpu.VMEM((8, 4, 16, 256), HALF),
            pltpu.VMEM((8, 4, 16, 128), HALF),
            pltpu.VMEM((8, 4, 16, 128), HALF),
            pltpu.VMEM((2, 32, half_out), HALF),
            pltpu.VMEM((8, 32, half_out), HALF),
            pltpu.VMEM((32, width), FULL),
            pltpu.VMEM((member_count, 128), FULL),
            pltpu.VMEM((8, 16, 128), HALF),
            pltpu.VMEM((8, 16, 128), HALF),
            sem((5,)),
            sem((8,)),
            sem((8,)),
            sem,
            sem,
            sem((8,)),
            sem((8,)),
            sem((3, 5, 8)),
            sem((5, 8)),
            sem((3,)),
            sem((3,)),
            sem((8,)),
            sem((8,)),
            sem((3, 4)),
            sem((3, 4)),
            sem((3, 8)),
            sem((3, 8)),
            sem((2, 2)),
            sem((8,)),
            sem((4,)),
            sem((8,)),
            sem((8,)),
        ],
        compiler_params=pltpu.CompilerParams(
            collective_id=0, has_side_effects=True, vmem_limit_bytes=58 * 1024 * 1024
        ),
    )(
        lengths, cluster[:, 0], owner, counts, flags,
        tokens.reshape(total, part), w_query, w_keyval,
        norm_gain.reshape(-1, 128), w_out.T, residents[0], cosine, sine,
    )


def plain_project(tokens, norm_gain, w_query, w_keyval, lengths):
    gathered = lax.all_gather(tokens, "mp", axis=2, tiled=True)
    dialogs, seq_len, width = gathered.shape
    hidden = gathered.astype(jnp.float32)
    normed = (
        hidden * lax.rsqrt(jnp.mean(hidden * hidden, axis=-1, keepdims=True) + 1e-06) * norm_gain
    ).astype(jnp.bfloat16)
    normed_flat = normed.reshape(dialogs * seq_len, width)
    query_cols = w_query.shape[1]
    keyval_cols = w_keyval.shape[2]
    pieces = (
        lax.all_gather(w_query, "dp", axis=0, tiled=True),
        lax.all_gather(w_keyval, "dp", axis=0, tiled=True),
    )
    keyval_piece = pieces[1].reshape(pieces[1].shape[0], 2 * keyval_cols)
    query_sum = jnp.dot(normed_flat, pieces[0], preferred_element_type=jnp.float32)
    keyval_sum = jnp.dot(normed_flat, keyval_piece, preferred_element_type=jnp.float32)
    positions = jnp.arange(seq_len)
    local_heads = query_cols // HEAD_DIM
    local_kv = keyval_cols // HEAD_DIM
    query = jax.vmap(lambda block: rotate(block, positions))(
        query_sum.reshape(dialogs, seq_len, local_heads, HEAD_DIM)
    ).astype(jnp.bfloat16)
    keys = jax.vmap(lambda block: rotate(block, positions))(
        keyval_sum[:, :keyval_cols].reshape(dialogs, seq_len, local_kv, HEAD_DIM)
    ).astype(jnp.bfloat16)
    values = (
        keyval_sum[:, keyval_cols:]
        .reshape(dialogs, seq_len, local_kv, HEAD_DIM)
        .astype(jnp.bfloat16)
    )
    valid = (positions[None, :] < lengths[:, None]).astype(jnp.float32)
    pooled_input = (
        jnp.sum(hidden * valid[:, :, None], axis=1) / lengths.astype(jnp.float32)[:, None]
    )
    pooled_context = jax.vmap(attend)(query, keys, values, lengths).astype(jnp.bfloat16)
    return pooled_context, pooled_input


def plain_score(pooled_context, pooled_input, w_out, members, onehot, live):
    dialogs = pooled_context.shape[0]
    everyone = lax.all_gather(pooled_context, "dp", axis=0, tiled=True)
    slices = jnp.dot(everyone, w_out, preferred_element_type=jnp.float32).astype(jnp.bfloat16)
    slices = slices.reshape(-1, dialogs, w_out.shape[1])
    slices = lax.all_to_all(slices, "dp", split_axis=0, concat_axis=0, tiled=True)
    partial_out = slices.transpose(1, 0, 2).reshape(dialogs, -1)
    projected = lax.psum(partial_out, "mp").astype(jnp.float32)
    embedding = pooled_input + projected
    unit = embedding * lax.rsqrt(jnp.sum(embedding * embedding, axis=-1, keepdims=True) + 1e-06)
    unit = unit.astype(jnp.bfloat16)
    inverse_norm = lax.rsqrt(
        jnp.einsum("md,md->m", members, members, preferred_element_type=jnp.float32) + 1e-06
    )
    outgoing = jnp.einsum(
        "ocn,nd->ocd", onehot.astype(jnp.bfloat16), unit, preferred_element_type=jnp.float32
    ).astype(jnp.bfloat16)
    query_rows = lax.all_to_all(outgoing, "dp", split_axis=0, concat_axis=0, tiled=True)
    dots = lax.dot_general(
        query_rows,
        members,
        (((query_rows.ndim - 1,), (1,)), ((), ())),
        preferred_element_type=jnp.float32,
    )
    return lax.all_to_all(
        jnp.where(live[0] > 0, live[0] * dots * inverse_norm, 0.0).astype(jnp.bfloat16),
        "dp",
        split_axis=0,
        concat_axis=0,
        tiled=True,
    )


def general(
    tokens, norm_gain, w_query, w_keyval, w_out, residents, lengths, cluster, owner, counts, flags
):
    pooled_context, pooled_input = plain_project(tokens, norm_gain, w_query, w_keyval, lengths)
    dialogs = tokens.shape[0]
    my_index = lax.axis_index("dp")
    owner_count = lax.axis_size("dp")
    my_count = jnp.sum(jnp.where(owner == my_index, counts, 0))
    members = residents[0]
    member_count = members.shape[0]
    member_start = lax.axis_index("mp") * member_count
    live = jnp.where(member_start + jnp.arange(member_count) < my_count, logit_scale, 0.0)[None, :]
    table_size = owner.shape[0]
    cluster_ids = cluster[:, 0]
    destination = jnp.sum(
        jnp.where(jnp.arange(table_size)[None, :] == cluster_ids[:, None], owner[None, :], 0),
        axis=1,
    )
    capacity = max(1, -(-dialogs // owner_count))
    order = jnp.arange(dialogs)
    earlier = (destination[None, :] == destination[:, None]) & (order[None, :] < order[:, None])
    rank = jnp.sum(earlier.astype(jnp.int32), axis=1)
    onehot = (jnp.arange(owner_count)[:, None, None] == destination[None, None, :]) & (
        jnp.arange(capacity)[None, :, None] == rank[None, None, :]
    )
    returned = plain_score(pooled_context, pooled_input, w_out, members, onehot, live)
    similarity = jnp.einsum(
        "ocn,ocm->nm", onehot.astype(jnp.bfloat16), returned, preferred_element_type=jnp.float32
    )
    return similarity * flags.astype(jnp.float32)[:, None]


def local(*args):
    if lax.axis_size("dp") == 8 and lax.axis_size("mp") == 4:
        return fused(*args)
    return general(*args)


def solution(mesh):
    in_specs = (
        P("dp", None, "mp"),
        P(),
        P("dp", "mp"),
        P("dp", None, "mp"),
        P("mp", "dp"),
        P("dp", "mp"),
        P("dp"),
        P("dp"),
        P(),
        P(),
        P("dp"),
    )
    out_specs = P("dp", "mp")
    return jax.shard_map(local, mesh=mesh, in_specs=in_specs, out_specs=out_specs, check_vma=False)
```

```python
import math

import jax
import jax.numpy as jnp
import numpy as np
from jax import lax
from jax.experimental import pallas as pl
from jax.experimental.pallas import tpu as pltpu
from jax.sharding import PartitionSpec as P

HEAD_DIM = 128


rope_base = 1000000.0
logit_scale = 100.0


def rotate(values, positions):
    half = values.shape[-1] // 2
    freqs = rope_base ** (-jnp.arange(half, dtype=jnp.float32) * 2.0 / values.shape[-1])
    angles = positions.astype(jnp.float32)[:, None] * freqs[None, :]
    cosine = jnp.cos(angles)[:, None, :]
    sine = jnp.sin(angles)[:, None, :]
    first = values[..., :half]
    second = values[..., half:]
    return jnp.concatenate(
        [first * cosine - second * sine, second * cosine + first * sine], axis=-1
    )


def attend(query, keys, values, length):
    seq_len = query.shape[0]
    kv_count = keys.shape[1]
    group = query.shape[1] // kv_count
    grouped = query.reshape(seq_len, kv_count, group, query.shape[-1])
    scores = jnp.einsum(
        "qkgd,pkd->kgqp", grouped, keys, preferred_element_type=jnp.float32
    ) / math.sqrt(query.shape[-1])
    row_pos = jnp.arange(seq_len)[:, None]
    col_pos = jnp.arange(seq_len)[None, :]
    allowed = (col_pos <= row_pos) & (col_pos < length)
    scores = jnp.where(allowed, scores, -1e30)
    highest = jnp.max(scores, axis=-1, keepdims=True)
    expanded = jnp.exp(scores - highest)
    weights = (expanded / jnp.sum(expanded, axis=-1, keepdims=True)).astype(jnp.bfloat16)
    context = jnp.einsum("kgqp,pkd->qkgd", weights, values, preferred_element_type=jnp.float32)
    valid = (jnp.arange(seq_len) < length).astype(jnp.float32)
    pooled = jnp.sum(context * valid[:, None, None, None], axis=0) / length.astype(jnp.float32)
    return pooled.reshape(-1)


MESH = pl.DeviceIdType.MESH
HALF, FULL = jnp.bfloat16, jnp.float32
CHUNK = 4
GROUP = 8
NT = (((1,), (1,)), ((), ()))


def fused_kernel(
    lens, cluster, owner, counts, flags,
    tin, query_in, keyval_in, gain, w_out_in, members_in, cosine, sine,
    out,
    tok, wide, narrow, wot, members, qstage, kvstage, gcol, rs, kst, vst, qst, ctx, mask,
    acc_wide, acc_narrow, pool_mine, pool_out, pool_in, cout_a, cout_b, cout_c, cin_a, cin_b, cin_c, sums, rows_in, joined, squares, replies, arrived,
    l_sem, ty_send, ty_recv, tc_send, tc_recv, tf_send, tf_recv, wsend, wrecv,
    o_send, o_recv, g_send, g_recv, p_send, p_recv, a_send, a_recv, c_send, c_recv,
    d_send, d_recv, e_send, f_send, f_recv,
):
    dp = lax.axis_index("dp")
    mp = lax.axis_index("mp")
    z, x = dp // 2, dp % 2
    high = z // 2
    core_peer = mp + 1 - 2 * (mp % 2)
    y_peer = (mp + 2) % 4
    far = (core_peer + 2) % 4
    pair_z = z + 1 - 2 * (z % 2)
    x_peer = 2 * z + 1 - x
    total, part = tin.shape
    depth, queries = query_in.shape
    width = tok.shape[1]
    dialogs = lens.shape[0]
    seq_len = total // dialogs
    rows_each = CHUNK * seq_len
    chunks = total // rows_each
    end = (z == 0) | (z == 3)
    mid = (z == 1) | (z == 2)

    def across(k):
        return k + high * (3 - 2 * k)

    def slot_of(kind):
        k, prime = kind
        return 2 * across(k) + (1 - x if prime else x)

    def lanes_of(m):
        return pl.ds(pl.multiple_of(m * part, 128), part)

    def rows_of(r):
        return pl.ds(pl.multiple_of(r * rows_each, 64), rows_each)

    def remote(source, target, send, recv, dp_to, mp_to):
        return pltpu.make_async_remote_copy(
            src_ref=source, dst_ref=target, send_sem=send, recv_sem=recv,
            device_id={"dp": dp_to, "mp": mp_to}, device_id_type=MESH,
        )

    load_query = pltpu.make_async_copy(query_in, qstage, l_sem.at[0])
    load_keyval = pltpu.make_async_copy(keyval_in, kvstage, l_sem.at[1])
    load_tokens = pltpu.make_async_copy(tin, tok.at[:, lanes_of(mp)], l_sem.at[2])
    load_members = pltpu.make_async_copy(members_in, members, l_sem.at[3])
    load_out = pltpu.make_async_copy(w_out_in, wot.at[:, lanes_of(mp)], l_sem.at[4])
    load_keyval.start()
    load_query.start()

    barrier = pltpu.get_barrier_semaphore()

    def greet(dp_to, mp_to):
        pl.semaphore_signal(
            barrier, inc=1, device_id={"dp": dp_to, "mp": mp_to}, device_id_type=MESH
        )

    greet(dp, core_peer)
    greet(dp, y_peer)
    greet(x_peer, mp)
    greet(2 * pair_z + x, mp)

    @pl.when(mid)
    def _():
        greet(2 * across(2) + x, mp)

    load_tokens.start()
    load_members.start()
    load_out.start()

    first = (7 * dp) // 2
    for i in range(4):
        row = gain[pl.ds(first + i, 1), :]
        gcol[i * 128 : (i + 1) * 128, :] = jnp.broadcast_to(row, (128, 128)).T
    own_rows = pl.ds(pl.multiple_of(dp * depth, 64), depth)

    def gained(piece):
        factor = gcol[pl.ds(pl.multiple_of((dp % 2) * 64, 64), depth), :]
        return (piece.astype(FULL) * factor).astype(HALF)

    def fill_keyval():
        for i in range(2):
            wide[0, own_rows, i * 128 : (i + 1) * 128] = gained(kvstage[:, i, :])

    def fill_query(c):
        for h in range(2 * c - 2, min(2 * c, 7)):
            piece = gained(qstage[:, h * 128 : (h + 1) * 128])
            if h < 6:
                wide[c, own_rows, (h % 2) * 128 : (h % 2 + 1) * 128] = piece
            else:
                narrow[own_rows, :] = piece

    load_keyval.wait()
    fill_keyval()

    @pl.when(end)
    def _():
        pl.semaphore_wait(barrier, 4)

    @pl.when(mid)
    def _():
        pl.semaphore_wait(barrier, 5)

    def block_ref(c, slot):
        rows = pl.ds(pl.multiple_of(slot * depth, 64), depth)
        return wide.at[c, rows, :] if c < 4 else narrow.at[rows, :]

    ways = (x_peer, 2 * pair_z + x, 2 * across(2) + x)
    own_kind = {"end": (0, 0), "mid": (1, 0)}
    sent = {"end": [], "mid": []}
    waited = {"end": set(), "mid": set()}
    every = {
        "end": [(0, 1), (1, 0), (1, 1), (2, 0), (2, 1), (3, 0), (3, 1)],
        "mid": [(0, 0), (0, 1), (1, 1), (2, 0), (2, 1), (3, 0), (3, 1)],
    }

    def weight_copy(way, c, kind):
        slot = slot_of(kind)
        return remote(
            block_ref(c, slot), block_ref(c, slot), wsend.at[way, c, slot], wrecv.at[c, slot],
            ways[way], mp,
        )

    def send(role, way, c, kind):
        sent[role].append((way, c, kind))
        weight_copy(way, c, kind).start()

    def own(role, way, c):
        send(role, way, c, own_kind[role])

    def arrive(role, c, kind):
        if (c, kind) not in waited[role]:
            waited[role].add((c, kind))
            weight_copy(0, c, kind).wait_recv()

    def onward(role, c, kind, *to):
        arrive(role, c, kind)
        for way in to:
            send(role, way, c, kind)

    def at_end(f):
        pl.when(end)(f)

    def at_mid(f):
        pl.when(mid)(f)

    def rest(c):
        @at_end
        def _():
            for kind in every["end"]:
                arrive("end", c, kind)

        @at_mid
        def _():
            for kind in every["mid"]:
                arrive("mid", c, kind)

    def need(c, *groups):
        @at_end
        def _():
            for kind in every["end"]:
                if kind[0] in groups:
                    arrive("end", c, kind)

        @at_mid
        def _():
            for kind in every["mid"]:
                if kind[0] in groups:
                    arrive("mid", c, kind)

    def y_copy(r, m):
        return remote(
            tin.at[rows_of(r), :], tok.at[rows_of(r), lanes_of(m)], ty_send.at[r], ty_recv.at[r],
            dp, y_peer,
        )

    def forward_copy(r, m):
        return remote(
            tok.at[rows_of(r), lanes_of(m)], tok.at[rows_of(r), lanes_of(m)],
            tf_send.at[r], tf_recv.at[r], dp, core_peer,
        )

    def core_copy(m):
        return remote(tin, tok.at[:, lanes_of(m)], tc_send, tc_recv, dp, core_peer)

    def relay_tokens(r):
        y_copy(r, y_peer).wait_recv()
        forward_copy(r, y_peer).start()

    def out_copy(i, m, mp_to):
        return remote(
            wot.at[:, lanes_of(m)], wot.at[:, lanes_of(m)], o_send.at[i], o_recv.at[i], dp, mp_to
        )

    @at_end
    def _():
        own("end", 0, 0)
        own("end", 1, 0)

    @at_mid
    def _():
        own("mid", 1, 0)
        own("mid", 0, 0)
        own("mid", 2, 0)

    @pl.loop(0, chunks)
    def _(r):
        y_copy(r, mp).start()

    core_copy(mp).start()
    load_query.wait()
    fill_query(1)

    @at_end
    def _():
        own("end", 0, 1)
        own("end", 1, 1)

    @at_mid
    def _():
        own("mid", 1, 1)
        own("mid", 0, 1)
        own("mid", 2, 1)

    fill_query(2)
    fill_query(3)
    fill_query(4)

    @at_end
    def _():
        for c in (2, 3):
            own("end", 0, c)
            own("end", 1, c)

    @at_mid
    def _():
        for c in (2, 3):
            own("mid", 0, c)

    def owner_of(m, j):
        return 2 * (m % 2 + j * (3 - 2 * (m % 2))) + m // 2

    lane = lax.broadcasted_iota(jnp.int32, (dialogs, 128), 1)
    sub = lax.broadcasted_iota(jnp.int32, (dialogs, 128), 0)
    lane_dialog = GROUP * (lane // 16) + lane % GROUP
    to_col = jnp.zeros((dialogs, 128), jnp.int32)
    to_row = jnp.full((dialogs, 128), -64, jnp.int32)
    to_wide = jnp.full((dialogs, 128), -64, jnp.int32)
    len_col = jnp.zeros((dialogs, 128), jnp.int32)
    flag_col = jnp.zeros((dialogs, 128), jnp.int32)
    for d in range(dialogs):
        target = owner[cluster[d]]
        to_col = jnp.where(sub == d, target, to_col)
        to_row = jnp.where(lane == d, target, to_row)
        to_wide = jnp.where((lane_dialog == d) & (lane < 64), target, to_wide)
        len_col = jnp.where(sub == d, lens[d], len_col)
        flag_col = jnp.where(sub == d, flags[d], flag_col)
    len_col = len_col.astype(FULL)
    flag_col = flag_col.astype(FULL)
    rank_col = jnp.sum(
        jnp.where((to_col == to_row) & (lane < sub), 1.0, 0.0), axis=1, keepdims=True
    )
    rank_row = jnp.sum(
        jnp.where((to_col == to_row) & (sub < lane), 1.0, 0.0), axis=0, keepdims=True
    )
    rank_wide = jnp.sum(
        jnp.where((to_col == to_wide) & (sub < lane_dialog), 1.0, 0.0), axis=0, keepdims=True
    )
    slot_row = to_row[0:1].astype(FULL) * CHUNK + rank_row
    slot_wide = to_wide[0:1].astype(FULL) * CHUNK + rank_wide
    reply_place = to_col[:, 0:1].astype(FULL) * 16.0 + rank_col
    place = lax.broadcasted_iota(jnp.int32, (64, 128), 0)
    place_lane = lax.broadcasted_iota(jnp.int32, (64, 128), 1)
    upper = place % 16 < 8
    held = (owner_of(place // 16, (place % 8) // 4) * CHUNK + place % CHUNK).astype(FULL)
    slot_match = jnp.where(held == slot_row, 1.0, 0.0)
    upper_pick = jnp.where(upper, slot_match, 0.0).astype(HALF)[:, :dialogs]
    lower_pick = jnp.where(upper, 0.0, slot_match).astype(HALF)[:, :dialogs]

    index = lax.broadcasted_iota(jnp.int32, mask.shape, 1)
    start = lax.broadcasted_iota(jnp.int32, mask.shape, 0) * seq_len
    ahead = (index - start).astype(FULL)
    mask[...] = jnp.where((ahead >= 0.0) & (ahead < len_col[:, 0:1]), 1.0, 0.0).astype(HALF)
    load_tokens.wait()

    def pool_copy(i, source):
        to = (dp + i) % 8
        return remote(pool_out.at[to], pool_in.at[source], p_send.at[i], p_recv.at[source], to, mp)

    def pool_group(j, m_slot):
        to = (mp + j) % 4
        return remote(
            pool_mine.at[to], pool_out.at[pl.ds(2 * m_slot, 2)], g_send.at[j], g_recv.at[m_slot],
            dp, to,
        )

    def pool():
        mean = jnp.dot(mask[...], tok[:, lanes_of(mp)], preferred_element_type=FULL)
        mean = (mean / len_col[:, 0:1]).astype(HALF)
        block = width // 8
        for j in range(2):
            lead = mean[:, j * block : j * block + 256]
            back = mean[:, j * block + 256 : (j + 1) * block]
            lower = jnp.dot(lower_pick, back, preferred_element_type=FULL)
            pool_mine[:, j] = (
                (
                    jnp.dot(upper_pick, lead, preferred_element_type=FULL)
                    + jnp.concatenate([lower, jnp.zeros((64, 512 - block), FULL)], axis=1)
                )
                .astype(HALF)
                .reshape(4, 16, 256)
            )
        for j in range(1, 4):
            pool_group(j, mp).start()
        pool_out[pl.ds(2 * mp, 2)] = pool_mine[mp]

    def spread_pool():
        for j in range(1, 4):
            pool_group(j, (mp + j) % 4).wait_recv()
        for i in range(1, 8):
            pool_copy(i, dp).start()
        pool_in[dp] = pool_out[dp]

    def normalize(r):
        for half in range(2):
            rows = pl.ds(pl.multiple_of(r * rows_each + half * (rows_each // 2), 32), rows_each // 2)
            values = tok[rows, :].astype(FULL)
            mean_square = jnp.sum(values * values, axis=-1, keepdims=True) * (1.0 / width)
            rs[rows, :] = jnp.broadcast_to(lax.rsqrt(mean_square + 1e-06), (rows_each // 2, 128))

    def turn(piece):
        return piece * cosine[...] + pltpu.roll(piece, HEAD_DIM // 2, 1) * sine[...]

    def keyval_rows(low, top):
        @pl.loop(low, top)
        def _(r):
            forward_copy(r, far).wait_recv()
            normalize(r)
            rows = rows_of(r)
            product = jnp.dot(tok[rows, :], wide[0], preferred_element_type=FULL)
            kst[rows, :] = turn(product[:, :HEAD_DIM] * rs[rows, :]).astype(HALF)
            vst[rows, :] = (product[:, HEAD_DIM:] * rs[rows, :]).astype(HALF)

    rows_group = GROUP * seq_len

    def product_of(c, rows, first, length):
        depth_rows = pl.ds(first, length)
        weights = wide[c, depth_rows, :] if c < 4 else narrow[depth_rows, :]
        return jnp.dot(tok[rows, pl.ds(first, length)], weights, preferred_element_type=FULL)

    def total_of(c):
        return acc_wide if c < 4 else acc_narrow

    def partial_block(c, first, length, fresh, low=0, top=total // GROUP // seq_len):
        @pl.loop(low, top)
        def _(r):
            rows = pl.ds(pl.multiple_of(r * rows_group, 128), rows_group)
            product = product_of(c, rows, pl.multiple_of(first, 128), length)
            if fresh:
                total_of(c)[rows, :] = product
            else:
                total_of(c)[rows, :] += product

    def query_rows(c, r, slot):
        rows = pl.ds(pl.multiple_of(r * rows_group, 128), rows_group)
        if c < 2:
            product = product_of(c, rows, 0, width)
        else:
            last = pl.multiple_of(across(3 if c > 2 else 1) * part, 128)
            product = total_of(c)[rows, :] + product_of(c, rows, last, part)
        for h in range(product.shape[1] // HEAD_DIM):
            span = slice(h * HEAD_DIM, (h + 1) * HEAD_DIM)
            for half in range(2):
                here = slice(half * rows_each, (half + 1) * rows_each)
                some = pl.ds(
                    pl.multiple_of(r * rows_group + half * rows_each, 64), rows_each
                )
                qst[slot, here, span] = turn(product[here, span] * rs[some, :]).astype(HALF)

    def attend_rows(c, r, slot):
        heads = 2 if c < 4 else 1
        lanes = heads * seq_len
        key_pos = lax.broadcasted_iota(jnp.int32, (seq_len, lanes), 0)
        query_pos = lax.broadcasted_iota(jnp.int32, (seq_len, lanes), 1) % seq_len
        causal = key_pos <= query_pos
        position = lax.broadcasted_iota(jnp.int32, (1, lanes), 1) % seq_len
        pieces = []
        for item in range(GROUP):
            here = slice(item * seq_len, (item + 1) * seq_len)
            keys = kst[pl.ds(pl.multiple_of(r * rows_group + item * seq_len, 16), seq_len), :]
            stacked = qst[slot, here, :HEAD_DIM]
            if heads == 2:
                stacked = jnp.concatenate([stacked, qst[slot, here, HEAD_DIM:]], axis=0)
            scores = lax.dot_general(keys, stacked, NT, preferred_element_type=FULL)
            scores = jnp.where(causal, scores * (1.0 / math.sqrt(HEAD_DIM)), -1e30)
            expanded = jnp.exp(scores - jnp.max(scores, axis=0, keepdims=True))
            length = lens[r * GROUP + item]
            share = jnp.where(position < length, 1.0, 0.0) / (
                jnp.sum(expanded, axis=0, keepdims=True)
                * jnp.full((1, lanes), length, jnp.int32).astype(FULL)
            )
            pieces.append((expanded * share).astype(HALF))
        weights = jnp.concatenate(pieces, axis=0)
        head_row = lax.broadcasted_iota(jnp.int32, (16, lanes), 0) // GROUP
        head_lane = lax.broadcasted_iota(jnp.int32, (16, lanes), 1) // seq_len
        chosen = jnp.where(head_row == head_lane, 1.0, 0.0).astype(HALF)
        sums_of = lax.dot_general(chosen, weights, NT, preferred_element_type=FULL)
        item_row = lax.broadcasted_iota(jnp.int32, sums_of.shape, 0) % GROUP
        item_lane = lax.broadcasted_iota(jnp.int32, sums_of.shape, 1) // seq_len
        sums_of = jnp.where(item_row == item_lane, sums_of, 0.0)
        coarse = sums_of.astype(HALF).astype(FULL)
        both = jnp.concatenate([coarse, sums_of - coarse], axis=0).astype(HALF)
        rows = pl.ds(pl.multiple_of(r * rows_group, 128), rows_group)
        mixed = jnp.dot(both, vst[rows, :], preferred_element_type=FULL)
        ctx[c - 1, r] = mixed[:16] + mixed[16:]

    def query_block(c, low, top):
        query_rows(c, low, low % 2)

        @pl.loop(low + 1, top)
        def _(r):
            attend_rows(c, r - 1, (r - 1) % 2)
            query_rows(c, r, r % 2)

        attend_rows(c, top - 1, (top - 1) % 2)

    def member_squares(low, top):
        @pl.loop(low, top)
        def _(step):
            rows = pl.ds(pl.multiple_of(step * 64, 64), 64)
            values = members[rows, :].astype(FULL)
            squares[rows, :] = jnp.broadcast_to(
                jnp.sum(values * values, axis=-1, keepdims=True), (64, 128)
            )

    @at_mid
    def _():
        onward("mid", 0, (2, 0), 1, 0)
        onward("mid", 0, (0, 0), 2)

    @at_end
    def _():
        onward("end", 0, (0, 1), 1)

    load_members.wait()
    member_squares(0, 4)
    relay_tokens(0)

    @at_mid
    def _():
        onward("mid", 1, (0, 0), 2)
        own("mid", 2, 2)
        onward("mid", 1, (2, 0), 0)
        own("mid", 0, 4)

    @at_end
    def _():
        onward("end", 1, (0, 1), 1)

    pool()

    @at_mid
    def _():
        onward("mid", 0, (3, 0), 1, 0)
        onward("mid", 0, (1, 1), 1)
        send("mid", 1, 1, (2, 0))
        onward("mid", 2, (0, 0), 2)
        own("mid", 2, 3)

    @at_end
    def _():
        onward("end", 0, (2, 0), 0)
        onward("end", 2, (0, 1), 1)

    relay_tokens(1)

    @at_mid
    def _():
        onward("mid", 1, (3, 0), 1, 0)
        own("mid", 1, 2)
        onward("mid", 3, (0, 0), 2)
        own("mid", 2, 4)

    @at_end
    def _():
        onward("end", 0, (3, 0), 0)
        onward("end", 1, (1, 0), 0)
        own("end", 0, 4)
        onward("end", 3, (0, 1), 1)
        own("end", 1, 4)

    relay_tokens(2)

    @at_mid
    def _():
        onward("mid", 2, (2, 0), 1, 0)
        onward("mid", 4, (0, 0), 2)

    @at_end
    def _():
        onward("end", 1, (2, 0), 0)

    member_squares(4, 8)
    relay_tokens(3)

    @at_mid
    def _():
        onward("mid", 2, (3, 0), 1, 0)
        own("mid", 1, 3)
        onward("mid", 2, (1, 1), 1)
        onward("mid", 3, (2, 0), 1, 0)

    core_copy(core_peer).wait_recv()
    rest(0)
    keyval_rows(0, 4)

    @at_end
    def _():
        onward("end", 1, (3, 0), 0)
        onward("end", 4, (0, 1), 1)

    spread_pool()

    relay_tokens(4)

    @at_mid
    def _():
        onward("mid", 3, (3, 0), 1, 0)
        onward("mid", 4, (2, 0), 1, 0)

    relay_tokens(5)

    @at_end
    def _():
        onward("end", 2, (2, 0), 0)

    @at_mid
    def _():
        onward("mid", 4, (3, 0), 1, 0)
        own("mid", 1, 4)
        onward("mid", 4, (1, 1), 1)

    keyval_rows(4, 6)
    rest(1)
    query_block(1, 0, 1)

    @at_end
    def _():
        onward("end", 2, (3, 0), 0)

    query_block(1, 1, 3)
    relay_tokens(6)
    load_out.wait()
    own_out = out_copy(0, mp, y_peer)
    own_out.start()
    beside_out = out_copy(1, mp, core_peer)
    beside_out.start()
    need(2, 0, 2)
    partial_block(2, across(0) * part, part, True, 0, 3)
    partial_block(2, across(2) * part, part, False, 0, 3)

    @at_end
    def _():
        onward("end", 3, (1, 0), 0)

    need(2, 3)
    partial_block(2, across(3) * part, part, False, 0, 3)
    relay_tokens(7)
    keyval_rows(6, 8)
    query_block(1, 3, 4)
    partial_block(2, across(0) * part, part, True, 3, 4)
    partial_block(2, across(2) * part, part, False, 3, 4)
    partial_block(2, across(3) * part, part, False, 3, 4)
    rest(2)
    query_block(2, 0, 2)

    @at_end
    def _():
        onward("end", 3, (2, 0), 0)

    query_block(2, 2, 4)

    lane_head = (place_lane // GROUP) % 2
    heads_of = (((0, 2), (1, 3)), ((4, 5),), ((6, None),))
    couts, cins = (cout_a, cout_b, cout_c), (cin_a, cin_b, cin_c)

    def pick(h, right):
        right = right & (lane_head == h % 2)
        return jnp.where(right & (held == slot_wide), 1.0, 0.0).astype(HALF)[:, :64]

    def group_copy(p, j, m_slot):
        to = (mp + j) % 4
        return remote(
            couts[p].at[to], cins[p].at[dp, m_slot], a_send.at[p, j], a_recv.at[p, m_slot], dp, to
        )

    def context_copy(p, i, d_slot):
        return remote(
            cins[p].at[d_slot], cins[p].at[d_slot], c_send.at[p, i], c_recv.at[p, d_slot],
            (dp + i) % 8, mp,
        )

    def share_part(p):
        for block, (top, bottom) in enumerate(heads_of[p]):
            rows = ctx[top // 2].reshape(64, 128).astype(HALF)
            value = jnp.dot(pick(top, upper), rows, preferred_element_type=FULL)
            if bottom is not None:
                rows = ctx[bottom // 2].reshape(64, 128).astype(HALF)
                value = value + jnp.dot(
                    pick(bottom, jnp.logical_not(upper)), rows, preferred_element_type=FULL
                )
            couts[p][:, :, block * 128 : (block + 1) * 128] = value.astype(HALF).reshape(
                4, 16, 128
            )
        for j in range(1, 4):
            group_copy(p, j, mp).start()
        cins[p][dp, mp] = couts[p][mp]

    def spread_part(p):
        for j in range(1, 4):
            group_copy(p, j, (mp + j) % 4).wait_recv()
        for i in (4, 3, 5, 2, 6, 1, 7):
            context_copy(p, i, dp).start()

    share_part(0)
    need(3, 0, 1)
    partial_block(3, high * 2 * part, 2 * part, True)

    @at_end
    def _():
        onward("end", 3, (3, 0), 0)

    need(3, 2)
    partial_block(3, across(2) * part, part, False)

    @at_end
    def _():
        onward("end", 4, (2, 0), 0)

    need(4, 0)
    partial_block(4, across(0) * part, part, True)

    @at_end
    def _():
        onward("end", 4, (3, 0), 0)

    spread_part(0)

    limit = counts[0] * 0
    for c in range(counts.shape[0]):
        limit = limit + jnp.where(owner[c] == dp, counts[c], 0)
    member_count = members.shape[0]
    member = mp * member_count + lax.broadcasted_iota(jnp.int32, (1, member_count), 1)
    scale = jnp.where(member < limit, logit_scale, 0.0) * lax.rsqrt(squares[...].T[0:1, :] + 1e-06)
    rest(3)
    query_block(3, 0, 4)
    share_part(1)
    need(4, 2)
    partial_block(4, across(2) * part, part, False)
    spread_part(1)
    need(4, 1)
    partial_block(4, across(1) * part, part, False)
    out_copy(0, y_peer, y_peer).wait_recv()
    onward_out = out_copy(2, y_peer, core_peer)
    onward_out.start()
    rest(4)
    query_block(4, 0, 4)
    share_part(2)
    out_copy(1, core_peer, core_peer).wait_recv()
    out_copy(2, far, core_peer).wait_recv()
    for i in range(1, 8):
        pool_copy(i, (dp + i) % 8).wait_recv()
    spread_part(2)

    half_out = wot.shape[0]
    total_a = jnp.zeros((128, half_out), FULL)
    total_b = jnp.zeros((128, half_out), FULL)

    def lanes_from(m, first, length):
        return wot[:, m * part + first : m * part + first + length]

    for p in range(3):
        for i in range(1, 8):
            context_copy(p, i, (dp + i) % 8).wait_recv()
        length = cins[p].shape[3]
        for m in range(4):
            have = cins[p][:, m].reshape(128, length)
            first = (0, 512, 768)[p]
            total_a = total_a + lax.dot_general(
                have, lanes_from(m, first, length), NT, preferred_element_type=FULL
            )
            if p < 2:
                total_b = total_b + lax.dot_general(
                    have, lanes_from(m, first + length, length), NT, preferred_element_type=FULL
                )
    embedded = (
        total_a.reshape(8, 16, half_out)[:, :8]
        + total_b.reshape(8, 16, half_out)[:, 8:]
    ).reshape(64, half_out)
    pooled = pool_in[...].astype(FULL)
    embedded = embedded + jnp.concatenate(
        [pooled[:, :8].reshape(64, 256), pooled[:, 8:].reshape(64, 256)[:, : half_out - 256]],
        axis=1,
    )
    row = lax.broadcasted_iota(jnp.int32, (64, 64), 0)
    column = lax.broadcasted_iota(jnp.int32, (64, 64), 1)
    order = jnp.where(
        column == ((row // 4) % 8) * 8 + (row // 32) * 4 + row % 4, 1.0, 0.0
    ).astype(HALF)
    sums[...] = (
        jnp.dot(order, embedded.astype(HALF), preferred_element_type=FULL)
        .astype(HALF)
        .reshape(sums.shape)
    )

    core = mp % 2
    home = 2 * x + (z + 1) // 2 % 2

    def sum_copy(j, y):
        return remote(
            sums.at[j], rows_in.at[dp], d_send.at[j, y], d_recv.at[dp], owner_of(mp, j), 2 * y + x
        )

    def hand_copy(k, slot):
        return remote(
            rows_in.at[slot], rows_in.at[slot], e_send.at[k], d_recv.at[slot], dp, core_peer
        )

    for j in range(2):
        for y in range(2):
            mine = (owner_of(mp, j) == dp) & (2 * y + x == mp)

            @pl.when(jnp.logical_not(mine))
            def _():
                sum_copy(j, y).start()

            @pl.when(mine)
            def _():
                rows_in[dp] = sums[j]

    for k in range(4):
        slot = 2 * k + core

        @pl.when(jnp.logical_not((slot == dp) & (mp == home)))
        def _():
            hand_copy(k, slot).wait_recv()

        hand_copy(k, slot).start()
    for k in range(4):
        hand_copy(k, 2 * k + 1 - core).wait_recv()

    for slot in range(8):
        joined[:, slot * half_out : (slot + 1) * half_out] = rows_in[slot].astype(FULL)
    embedding = joined[...]
    dots = lax.dot_general(
        embedding.astype(HALF), members[...], NT, preferred_element_type=FULL
    )
    inverse = lax.rsqrt(jnp.sum(embedding * embedding, axis=-1, keepdims=True) + 1e-06)
    found = (dots * inverse * scale).astype(HALF)
    row = lax.broadcasted_iota(jnp.int32, (128, 32), 0)
    column = lax.broadcasted_iota(jnp.int32, (128, 32), 1)
    value = jnp.zeros((128, 128), FULL)
    for q in range(4):
        spread = jnp.where(
            ((row % 16) // 4 == q) & (column == (row // 16) * 4 + row % 4), 1.0, 0.0
        ).astype(HALF)
        value = value + jnp.dot(
            spread, found[:, q * 128 : (q + 1) * 128], preferred_element_type=FULL
        )
    replies[...] = value.astype(HALF).reshape(replies.shape)

    def reply_copy(i, slot):
        to = (dp + i) % 8
        return remote(replies.at[to], arrived.at[slot], f_send.at[i], f_recv.at[slot], to, mp)

    for i in range(1, 8):
        reply_copy(i, dp).start()
    arrived[dp] = replies[dp]
    for i in range(1, 8):
        reply_copy(i, (dp + i) % 8).wait_recv()
    have = arrived[...].reshape(128, 128)
    column = lax.broadcasted_iota(jnp.int32, (dialogs, 128), 1).astype(FULL)
    for q in range(4):
        fetch = jnp.where(column == reply_place + 4.0 * q, flag_col, 0.0).astype(HALF)
        out[:, q * 128 : (q + 1) * 128] = jnp.dot(fetch, have, preferred_element_type=FULL)

    for r in range(chunks):
        y_copy(r, mp).wait_send()
        forward_copy(r, y_peer).wait_send()
    core_copy(mp).wait_send()
    own_out.wait_send()
    beside_out.wait_send()
    onward_out.wait_send()

    @at_end
    def _():
        for way, c, kind in sent["end"]:
            weight_copy(way, c, kind).wait_send()

    @at_mid
    def _():
        for way, c, kind in sent["mid"]:
            weight_copy(way, c, kind).wait_send()

    for j in range(2):
        for y in range(2):
            @pl.when(jnp.logical_not((owner_of(mp, j) == dp) & (2 * y + x == mp)))
            def _():
                sum_copy(j, y).wait_send()

    for k in range(4):
        hand_copy(k, 2 * k + core).wait_send()
    for i in range(1, 4):
        pool_group(i, mp).wait_send()
        for p in range(3):
            group_copy(p, i, mp).wait_send()
    for i in range(1, 8):
        for p in range(3):
            context_copy(p, i, dp).wait_send()
        reply_copy(i, dp).wait_send()
        pool_copy(i, dp).wait_send()


def fused(
    tokens, norm_gain, w_query, w_keyval, w_out, residents, lengths, cluster, owner, counts, flags
):
    dialogs, seq_len, part = tokens.shape
    total = dialogs * seq_len
    depth, queries = w_query.shape
    width = norm_gain.shape[0]
    member_count = residents.shape[1]
    half_out = w_out.shape[1]
    half = HEAD_DIM // 2
    freqs = rope_base ** (-np.arange(half, dtype=np.float64) * 2.0 / HEAD_DIM)
    angles = np.arange(seq_len, dtype=np.float64)[:, None] * freqs[None, :]
    cosine, sine = np.cos(angles), np.sin(angles)
    cosine = np.tile(np.concatenate([cosine, cosine], axis=1), (CHUNK, 1)).astype(np.float32)
    sine = np.tile(np.concatenate([-sine, sine], axis=1), (CHUNK, 1)).astype(np.float32)
    vmem = pl.BlockSpec(memory_space=pltpu.VMEM)
    smem = pl.BlockSpec(memory_space=pltpu.SMEM)
    hbm = pl.BlockSpec(memory_space=pltpu.HBM)
    sem = pltpu.SemaphoreType.DMA
    return pl.pallas_call(
        fused_kernel,
        out_shape=jax.ShapeDtypeStruct((dialogs, member_count), FULL),
        in_specs=[smem] * 5 + [hbm, hbm, hbm, vmem, hbm, hbm, vmem, vmem],
        out_specs=vmem,
        scratch_shapes=[
            pltpu.VMEM((total, width), HALF),
            pltpu.VMEM((4, width, 256), HALF),
            pltpu.VMEM((width, 128), HALF),
            pltpu.VMEM((half_out, width), HALF),
            pltpu.VMEM((member_count, width), HALF),
            pltpu.VMEM((depth, queries), HALF),
            pltpu.VMEM((depth, 2, 128), HALF),
            pltpu.VMEM((512, 128), FULL),
            pltpu.VMEM((total, 128), FULL),
            pltpu.VMEM((total, 128), HALF),
            pltpu.VMEM((total, 128), HALF),
            pltpu.VMEM((2, GROUP * seq_len, 256), HALF),
            pltpu.VMEM((4, 4, 16, 128), FULL),
            pltpu.VMEM((dialogs, total), HALF),
            pltpu.VMEM((total, 256), FULL),
            pltpu.VMEM((total, 128), FULL),
            pltpu.VMEM((4, 2, 16, 256), HALF),
            pltpu.VMEM((8, 16, 256), HALF),
            pltpu.VMEM((8, 16, 256), HALF),
            pltpu.VMEM((4, 16, 256), HALF),
            pltpu.VMEM((4, 16, 128), HALF),
            pltpu.VMEM((4, 16, 128), HALF),
            pltpu.VMEM((8, 4, 16, 256), HALF),
            pltpu.VMEM((8, 4, 16, 128), HALF),
            pltpu.VMEM((8, 4, 16, 128), HALF),
            pltpu.VMEM((2, 32, half_out), HALF),
            pltpu.VMEM((8, 32, half_out), HALF),
            pltpu.VMEM((32, width), FULL),
            pltpu.VMEM((member_count, 128), FULL),
            pltpu.VMEM((8, 16, 128), HALF),
            pltpu.VMEM((8, 16, 128), HALF),
            sem((5,)),
            sem((8,)),
            sem((8,)),
            sem,
            sem,
            sem((8,)),
            sem((8,)),
            sem((3, 5, 8)),
            sem((5, 8)),
            sem((3,)),
            sem((3,)),
            sem((4,)),
            sem((4,)),
            sem((8,)),
            sem((8,)),
            sem((3, 4)),
            sem((3, 4)),
            sem((3, 8)),
            sem((3, 8)),
            sem((2, 2)),
            sem((8,)),
            sem((4,)),
            sem((8,)),
            sem((8,)),
        ],
        compiler_params=pltpu.CompilerParams(
            collective_id=0, has_side_effects=True, vmem_limit_bytes=58 * 1024 * 1024
        ),
    )(
        lengths, cluster[:, 0], owner, counts, flags,
        tokens.reshape(total, part), w_query, w_keyval,
        norm_gain.reshape(-1, 128), w_out.T, residents[0], cosine, sine,
    )


def plain_project(tokens, norm_gain, w_query, w_keyval, lengths):
    gathered = lax.all_gather(tokens, "mp", axis=2, tiled=True)
    dialogs, seq_len, width = gathered.shape
    hidden = gathered.astype(jnp.float32)
    normed = (
        hidden * lax.rsqrt(jnp.mean(hidden * hidden, axis=-1, keepdims=True) + 1e-06) * norm_gain
    ).astype(jnp.bfloat16)
    normed_flat = normed.reshape(dialogs * seq_len, width)
    query_cols = w_query.shape[1]
    keyval_cols = w_keyval.shape[2]
    pieces = (
        lax.all_gather(w_query, "dp", axis=0, tiled=True),
        lax.all_gather(w_keyval, "dp", axis=0, tiled=True),
    )
    keyval_piece = pieces[1].reshape(pieces[1].shape[0], 2 * keyval_cols)
    query_sum = jnp.dot(normed_flat, pieces[0], preferred_element_type=jnp.float32)
    keyval_sum = jnp.dot(normed_flat, keyval_piece, preferred_element_type=jnp.float32)
    positions = jnp.arange(seq_len)
    local_heads = query_cols // HEAD_DIM
    local_kv = keyval_cols // HEAD_DIM
    query = jax.vmap(lambda block: rotate(block, positions))(
        query_sum.reshape(dialogs, seq_len, local_heads, HEAD_DIM)
    ).astype(jnp.bfloat16)
    keys = jax.vmap(lambda block: rotate(block, positions))(
        keyval_sum[:, :keyval_cols].reshape(dialogs, seq_len, local_kv, HEAD_DIM)
    ).astype(jnp.bfloat16)
    values = (
        keyval_sum[:, keyval_cols:]
        .reshape(dialogs, seq_len, local_kv, HEAD_DIM)
        .astype(jnp.bfloat16)
    )
    valid = (positions[None, :] < lengths[:, None]).astype(jnp.float32)
    pooled_input = (
        jnp.sum(hidden * valid[:, :, None], axis=1) / lengths.astype(jnp.float32)[:, None]
    )
    pooled_context = jax.vmap(attend)(query, keys, values, lengths).astype(jnp.bfloat16)
    return pooled_context, pooled_input


def plain_score(pooled_context, pooled_input, w_out, members, onehot, live):
    dialogs = pooled_context.shape[0]
    everyone = lax.all_gather(pooled_context, "dp", axis=0, tiled=True)
    slices = jnp.dot(everyone, w_out, preferred_element_type=jnp.float32).astype(jnp.bfloat16)
    slices = slices.reshape(-1, dialogs, w_out.shape[1])
    slices = lax.all_to_all(slices, "dp", split_axis=0, concat_axis=0, tiled=True)
    partial_out = slices.transpose(1, 0, 2).reshape(dialogs, -1)
    projected = lax.psum(partial_out, "mp").astype(jnp.float32)
    embedding = pooled_input + projected
    unit = embedding * lax.rsqrt(jnp.sum(embedding * embedding, axis=-1, keepdims=True) + 1e-06)
    unit = unit.astype(jnp.bfloat16)
    inverse_norm = lax.rsqrt(
        jnp.einsum("md,md->m", members, members, preferred_element_type=jnp.float32) + 1e-06
    )
    outgoing = jnp.einsum(
        "ocn,nd->ocd", onehot.astype(jnp.bfloat16), unit, preferred_element_type=jnp.float32
    ).astype(jnp.bfloat16)
    query_rows = lax.all_to_all(outgoing, "dp", split_axis=0, concat_axis=0, tiled=True)
    dots = lax.dot_general(
        query_rows,
        members,
        (((query_rows.ndim - 1,), (1,)), ((), ())),
        preferred_element_type=jnp.float32,
    )
    return lax.all_to_all(
        jnp.where(live[0] > 0, live[0] * dots * inverse_norm, 0.0).astype(jnp.bfloat16),
        "dp",
        split_axis=0,
        concat_axis=0,
        tiled=True,
    )


def general(
    tokens, norm_gain, w_query, w_keyval, w_out, residents, lengths, cluster, owner, counts, flags
):
    pooled_context, pooled_input = plain_project(tokens, norm_gain, w_query, w_keyval, lengths)
    dialogs = tokens.shape[0]
    my_index = lax.axis_index("dp")
    owner_count = lax.axis_size("dp")
    my_count = jnp.sum(jnp.where(owner == my_index, counts, 0))
    members = residents[0]
    member_count = members.shape[0]
    member_start = lax.axis_index("mp") * member_count
    live = jnp.where(member_start + jnp.arange(member_count) < my_count, logit_scale, 0.0)[None, :]
    table_size = owner.shape[0]
    cluster_ids = cluster[:, 0]
    destination = jnp.sum(
        jnp.where(jnp.arange(table_size)[None, :] == cluster_ids[:, None], owner[None, :], 0),
        axis=1,
    )
    capacity = max(1, -(-dialogs // owner_count))
    order = jnp.arange(dialogs)
    earlier = (destination[None, :] == destination[:, None]) & (order[None, :] < order[:, None])
    rank = jnp.sum(earlier.astype(jnp.int32), axis=1)
    onehot = (jnp.arange(owner_count)[:, None, None] == destination[None, None, :]) & (
        jnp.arange(capacity)[None, :, None] == rank[None, None, :]
    )
    returned = plain_score(pooled_context, pooled_input, w_out, members, onehot, live)
    similarity = jnp.einsum(
        "ocn,ocm->nm", onehot.astype(jnp.bfloat16), returned, preferred_element_type=jnp.float32
    )
    return similarity * flags.astype(jnp.float32)[:, None]


def local(*args):
    if lax.axis_size("dp") == 8 and lax.axis_size("mp") == 4:
        return fused(*args)
    return general(*args)


def solution(mesh):
    in_specs = (
        P("dp", None, "mp"),
        P(),
        P("dp", "mp"),
        P("dp", None, "mp"),
        P("mp", "dp"),
        P("dp", "mp"),
        P("dp"),
        P("dp"),
        P(),
        P(),
        P("dp"),
    )
    out_specs = P("dp", "mp")
    return jax.shard_map(local, mesh=mesh, in_specs=in_specs, out_specs=out_specs, check_vma=False)
```

```python
import math

import jax
import jax.numpy as jnp
import numpy as np
from jax import lax
from jax.experimental import pallas as pl
from jax.experimental.pallas import tpu as pltpu
from jax.sharding import PartitionSpec as P

HEAD_DIM = 128


rope_base = 1000000.0
logit_scale = 100.0


def rotate(values, positions):
    half = values.shape[-1] // 2
    freqs = rope_base ** (-jnp.arange(half, dtype=jnp.float32) * 2.0 / values.shape[-1])
    angles = positions.astype(jnp.float32)[:, None] * freqs[None, :]
    cosine = jnp.cos(angles)[:, None, :]
    sine = jnp.sin(angles)[:, None, :]
    first = values[..., :half]
    second = values[..., half:]
    return jnp.concatenate(
        [first * cosine - second * sine, second * cosine + first * sine], axis=-1
    )


def attend(query, keys, values, length):
    seq_len = query.shape[0]
    kv_count = keys.shape[1]
    group = query.shape[1] // kv_count
    grouped = query.reshape(seq_len, kv_count, group, query.shape[-1])
    scores = jnp.einsum(
        "qkgd,pkd->kgqp", grouped, keys, preferred_element_type=jnp.float32
    ) / math.sqrt(query.shape[-1])
    row_pos = jnp.arange(seq_len)[:, None]
    col_pos = jnp.arange(seq_len)[None, :]
    allowed = (col_pos <= row_pos) & (col_pos < length)
    scores = jnp.where(allowed, scores, -1e30)
    highest = jnp.max(scores, axis=-1, keepdims=True)
    expanded = jnp.exp(scores - highest)
    weights = (expanded / jnp.sum(expanded, axis=-1, keepdims=True)).astype(jnp.bfloat16)
    context = jnp.einsum("kgqp,pkd->qkgd", weights, values, preferred_element_type=jnp.float32)
    valid = (jnp.arange(seq_len) < length).astype(jnp.float32)
    pooled = jnp.sum(context * valid[:, None, None, None], axis=0) / length.astype(jnp.float32)
    return pooled.reshape(-1)


MESH = pl.DeviceIdType.MESH
HALF, FULL = jnp.bfloat16, jnp.float32
CHUNK = 4
GROUP = 8
NT = (((1,), (1,)), ((), ()))


def fused_kernel(
    lens, cluster, owner, counts, flags,
    tin, query_in, keyval_in, gain, w_out_in, members_in, cosine, sine,
    out,
    tok, wide, narrow, wot, members, qstage, kvstage, gcol, rs, kst, vst, qst, ctx, mask,
    acc_wide, acc_narrow, pool_mine, pool_out, pool_in, cout_a, cout_b, cout_c, cin_a, cin_b, cin_c, sums, rows_in, joined, squares, replies, arrived,
    l_sem, ty_send, ty_recv, tc_send, tc_recv, tf_send, tf_recv, wsend, wrecv,
    o_send, o_recv, g_send, g_recv, p_send, p_recv, a_send, a_recv, c_send, c_recv,
    d_send, d_recv, e_send, f_send, f_recv,
):
    dp = lax.axis_index("dp")
    mp = lax.axis_index("mp")
    z, x = dp // 2, dp % 2
    high = z // 2
    core_peer = mp + 1 - 2 * (mp % 2)
    y_peer = (mp + 2) % 4
    far = (core_peer + 2) % 4
    pair_z = z + 1 - 2 * (z % 2)
    x_peer = 2 * z + 1 - x
    total, part = tin.shape
    depth, queries = query_in.shape
    width = tok.shape[1]
    dialogs = lens.shape[0]
    seq_len = total // dialogs
    rows_each = CHUNK * seq_len
    chunks = total // rows_each
    end = (z == 0) | (z == 3)
    mid = (z == 1) | (z == 2)

    def across(k):
        return k + high * (3 - 2 * k)

    def slot_of(kind):
        k, prime = kind
        return 2 * across(k) + (1 - x if prime else x)

    def lanes_of(m):
        return pl.ds(pl.multiple_of(m * part, 128), part)

    def rows_of(r):
        return pl.ds(pl.multiple_of(r * rows_each, 64), rows_each)

    def remote(source, target, send, recv, dp_to, mp_to):
        return pltpu.make_async_remote_copy(
            src_ref=source, dst_ref=target, send_sem=send, recv_sem=recv,
            device_id={"dp": dp_to, "mp": mp_to}, device_id_type=MESH,
        )

    load_query = pltpu.make_async_copy(query_in, qstage, l_sem.at[0])
    load_keyval = pltpu.make_async_copy(keyval_in, kvstage, l_sem.at[1])
    load_tokens = pltpu.make_async_copy(tin, tok.at[:, lanes_of(mp)], l_sem.at[2])
    load_members = pltpu.make_async_copy(members_in, members, l_sem.at[3])
    load_out = pltpu.make_async_copy(w_out_in, wot.at[:, lanes_of(mp)], l_sem.at[4])
    load_keyval.start()
    load_query.start()

    barrier = pltpu.get_barrier_semaphore()

    def greet(dp_to, mp_to):
        pl.semaphore_signal(
            barrier, inc=1, device_id={"dp": dp_to, "mp": mp_to}, device_id_type=MESH
        )

    greet(dp, core_peer)
    greet(dp, y_peer)
    greet(x_peer, mp)
    greet(2 * pair_z + x, mp)

    @pl.when(mid)
    def _():
        greet(2 * across(2) + x, mp)

    load_tokens.start()
    load_members.start()
    load_out.start()

    first = (7 * dp) // 2
    for i in range(4):
        row = gain[pl.ds(first + i, 1), :]
        gcol[i * 128 : (i + 1) * 128, :] = jnp.broadcast_to(row, (128, 128)).T
    own_rows = pl.ds(pl.multiple_of(dp * depth, 64), depth)

    def gained(piece):
        factor = gcol[pl.ds(pl.multiple_of((dp % 2) * 64, 64), depth), :]
        return (piece.astype(FULL) * factor).astype(HALF)

    def fill_keyval():
        for i in range(2):
            wide[0, own_rows, i * 128 : (i + 1) * 128] = gained(kvstage[:, i, :])

    def fill_query(c):
        for h in range(2 * c - 2, min(2 * c, 7)):
            piece = gained(qstage[:, h * 128 : (h + 1) * 128])
            if h < 6:
                wide[c, own_rows, (h % 2) * 128 : (h % 2 + 1) * 128] = piece
            else:
                narrow[own_rows, :] = piece

    load_keyval.wait()
    fill_keyval()

    @pl.when(end)
    def _():
        pl.semaphore_wait(barrier, 4)

    @pl.when(mid)
    def _():
        pl.semaphore_wait(barrier, 5)

    def block_ref(c, slot):
        rows = pl.ds(pl.multiple_of(slot * depth, 64), depth)
        return wide.at[c, rows, :] if c < 4 else narrow.at[rows, :]

    ways = (x_peer, 2 * pair_z + x, 2 * across(2) + x)
    own_kind = {"end": (0, 0), "mid": (1, 0)}
    sent = {"end": [], "mid": []}
    waited = {"end": set(), "mid": set()}
    every = {
        "end": [(0, 1), (1, 0), (1, 1), (2, 0), (2, 1), (3, 0), (3, 1)],
        "mid": [(0, 0), (0, 1), (1, 1), (2, 0), (2, 1), (3, 0), (3, 1)],
    }

    def weight_copy(way, c, kind):
        slot = slot_of(kind)
        return remote(
            block_ref(c, slot), block_ref(c, slot), wsend.at[way, c, slot], wrecv.at[c, slot],
            ways[way], mp,
        )

    def send(role, way, c, kind):
        sent[role].append((way, c, kind))
        weight_copy(way, c, kind).start()

    def own(role, way, c):
        send(role, way, c, own_kind[role])

    def arrive(role, c, kind):
        if (c, kind) not in waited[role]:
            waited[role].add((c, kind))
            weight_copy(0, c, kind).wait_recv()

    def onward(role, c, kind, *to):
        arrive(role, c, kind)
        for way in to:
            send(role, way, c, kind)

    def at_end(f):
        pl.when(end)(f)

    def at_mid(f):
        pl.when(mid)(f)

    def rest(c):
        @at_end
        def _():
            for kind in every["end"]:
                arrive("end", c, kind)

        @at_mid
        def _():
            for kind in every["mid"]:
                arrive("mid", c, kind)

    def need(c, *groups):
        @at_end
        def _():
            for kind in every["end"]:
                if kind[0] in groups:
                    arrive("end", c, kind)

        @at_mid
        def _():
            for kind in every["mid"]:
                if kind[0] in groups:
                    arrive("mid", c, kind)

    def y_copy(r, m):
        return remote(
            tin.at[rows_of(r), :], tok.at[rows_of(r), lanes_of(m)], ty_send.at[r], ty_recv.at[r],
            dp, y_peer,
        )

    def forward_copy(r, m):
        return remote(
            tok.at[rows_of(r), lanes_of(m)], tok.at[rows_of(r), lanes_of(m)],
            tf_send.at[r], tf_recv.at[r], dp, core_peer,
        )

    def core_copy(m):
        return remote(tin, tok.at[:, lanes_of(m)], tc_send, tc_recv, dp, core_peer)

    def relay_tokens(r):
        y_copy(r, y_peer).wait_recv()
        forward_copy(r, y_peer).start()

    def out_copy(i, m, mp_to):
        return remote(
            wot.at[:, lanes_of(m)], wot.at[:, lanes_of(m)], o_send.at[i], o_recv.at[i], dp, mp_to
        )

    @at_end
    def _():
        own("end", 0, 0)
        own("end", 1, 0)

    @at_mid
    def _():
        own("mid", 1, 0)
        own("mid", 0, 0)
        own("mid", 2, 0)

    @pl.loop(0, chunks)
    def _(r):
        y_copy(r, mp).start()

    core_copy(mp).start()
    load_query.wait()
    fill_query(1)

    @at_end
    def _():
        own("end", 0, 1)
        own("end", 1, 1)

    @at_mid
    def _():
        own("mid", 1, 1)
        own("mid", 0, 1)
        own("mid", 2, 1)

    fill_query(2)
    fill_query(3)
    fill_query(4)

    @at_end
    def _():
        for c in (2, 3):
            own("end", 0, c)
            own("end", 1, c)

    @at_mid
    def _():
        for c in (2, 3):
            own("mid", 0, c)

    def owner_of(m, j):
        return 2 * (m % 2 + j * (3 - 2 * (m % 2))) + m // 2

    lane = lax.broadcasted_iota(jnp.int32, (dialogs, 128), 1)
    sub = lax.broadcasted_iota(jnp.int32, (dialogs, 128), 0)
    lane_dialog = GROUP * (lane // 16) + lane % GROUP
    to_col = jnp.zeros((dialogs, 128), jnp.int32)
    to_row = jnp.full((dialogs, 128), -64, jnp.int32)
    to_wide = jnp.full((dialogs, 128), -64, jnp.int32)
    len_col = jnp.zeros((dialogs, 128), jnp.int32)
    flag_col = jnp.zeros((dialogs, 128), jnp.int32)
    for d in range(dialogs):
        target = owner[cluster[d]]
        to_col = jnp.where(sub == d, target, to_col)
        to_row = jnp.where(lane == d, target, to_row)
        to_wide = jnp.where((lane_dialog == d) & (lane < 64), target, to_wide)
        len_col = jnp.where(sub == d, lens[d], len_col)
        flag_col = jnp.where(sub == d, flags[d], flag_col)
    len_col = len_col.astype(FULL)
    flag_col = flag_col.astype(FULL)
    rank_col = jnp.sum(
        jnp.where((to_col == to_row) & (lane < sub), 1.0, 0.0), axis=1, keepdims=True
    )
    rank_row = jnp.sum(
        jnp.where((to_col == to_row) & (sub < lane), 1.0, 0.0), axis=0, keepdims=True
    )
    rank_wide = jnp.sum(
        jnp.where((to_col == to_wide) & (sub < lane_dialog), 1.0, 0.0), axis=0, keepdims=True
    )
    slot_row = to_row[0:1].astype(FULL) * CHUNK + rank_row
    slot_wide = to_wide[0:1].astype(FULL) * CHUNK + rank_wide
    reply_place = to_col[:, 0:1].astype(FULL) * 16.0 + rank_col
    place = lax.broadcasted_iota(jnp.int32, (64, 128), 0)
    place_lane = lax.broadcasted_iota(jnp.int32, (64, 128), 1)
    upper = place % 16 < 8
    held = (owner_of(place // 16, (place % 8) // 4) * CHUNK + place % CHUNK).astype(FULL)
    slot_match = jnp.where(held == slot_row, 1.0, 0.0)
    upper_pick = jnp.where(upper, slot_match, 0.0).astype(HALF)[:, :dialogs]
    lower_pick = jnp.where(upper, 0.0, slot_match).astype(HALF)[:, :dialogs]

    index = lax.broadcasted_iota(jnp.int32, mask.shape, 1)
    start = lax.broadcasted_iota(jnp.int32, mask.shape, 0) * seq_len
    ahead = (index - start).astype(FULL)
    mask[...] = jnp.where((ahead >= 0.0) & (ahead < len_col[:, 0:1]), 1.0, 0.0).astype(HALF)
    load_tokens.wait()

    def pool_copy(i, source):
        to = (dp + i) % 8
        return remote(pool_out.at[to], pool_in.at[source], p_send.at[i], p_recv.at[source], to, mp)

    def pool_group(j, m_slot):
        to = (mp + j) % 4
        return remote(
            pool_mine.at[to], pool_out.at[pl.ds(2 * m_slot, 2)], g_send.at[j], g_recv.at[m_slot],
            dp, to,
        )

    def pool():
        mean = jnp.dot(mask[...], tok[:, lanes_of(mp)], preferred_element_type=FULL)
        mean = (mean / len_col[:, 0:1]).astype(HALF)
        block = width // 8
        for j in range(2):
            lead = mean[:, j * block : j * block + 256]
            back = mean[:, j * block + 256 : (j + 1) * block]
            lower = jnp.dot(lower_pick, back, preferred_element_type=FULL)
            pool_mine[:, j] = (
                (
                    jnp.dot(upper_pick, lead, preferred_element_type=FULL)
                    + jnp.concatenate([lower, jnp.zeros((64, 512 - block), FULL)], axis=1)
                )
                .astype(HALF)
                .reshape(4, 16, 256)
            )
        for j in range(1, 4):
            pool_group(j, mp).start()
        pool_out[pl.ds(2 * mp, 2)] = pool_mine[mp]

    def spread_pool():
        for j in range(1, 4):
            pool_group(j, (mp + j) % 4).wait_recv()
        for i in range(1, 8):
            pool_copy(i, dp).start()
        pool_in[dp] = pool_out[dp]

    def normalize(r):
        for half in range(2):
            rows = pl.ds(pl.multiple_of(r * rows_each + half * (rows_each // 2), 32), rows_each // 2)
            values = tok[rows, :].astype(FULL)
            mean_square = jnp.sum(values * values, axis=-1, keepdims=True) * (1.0 / width)
            rs[rows, :] = jnp.broadcast_to(lax.rsqrt(mean_square + 1e-06), (rows_each // 2, 128))

    def turn(piece):
        return piece * cosine[...] + pltpu.roll(piece, HEAD_DIM // 2, 1) * sine[...]

    def keyval_rows(low, top):
        @pl.loop(low, top)
        def _(r):
            forward_copy(r, far).wait_recv()
            normalize(r)
            rows = rows_of(r)
            product = jnp.dot(tok[rows, :], wide[0], preferred_element_type=FULL)
            kst[rows, :] = turn(product[:, :HEAD_DIM] * rs[rows, :]).astype(HALF)
            vst[rows, :] = (product[:, HEAD_DIM:] * rs[rows, :]).astype(HALF)

    rows_group = GROUP * seq_len

    def product_of(c, rows, first, length):
        depth_rows = pl.ds(first, length)
        weights = wide[c, depth_rows, :] if c < 4 else narrow[depth_rows, :]
        return jnp.dot(tok[rows, pl.ds(first, length)], weights, preferred_element_type=FULL)

    def total_of(c):
        return acc_wide if c < 4 else acc_narrow

    def partial_block(c, first, length, fresh, low=0, top=total // GROUP // seq_len):
        @pl.loop(low, top)
        def _(r):
            rows = pl.ds(pl.multiple_of(r * rows_group, 128), rows_group)
            product = product_of(c, rows, pl.multiple_of(first, 128), length)
            if fresh:
                total_of(c)[rows, :] = product
            else:
                total_of(c)[rows, :] += product

    def query_rows(c, r, slot):
        rows = pl.ds(pl.multiple_of(r * rows_group, 128), rows_group)
        if c < 2:
            product = product_of(c, rows, 0, width)
        else:
            last = pl.multiple_of(across(3 if c > 2 else 1) * part, 128)
            product = total_of(c)[rows, :] + product_of(c, rows, last, part)
        for h in range(product.shape[1] // HEAD_DIM):
            span = slice(h * HEAD_DIM, (h + 1) * HEAD_DIM)
            for half in range(2):
                here = slice(half * rows_each, (half + 1) * rows_each)
                some = pl.ds(
                    pl.multiple_of(r * rows_group + half * rows_each, 64), rows_each
                )
                qst[slot, here, span] = turn(product[here, span] * rs[some, :]).astype(HALF)

    def attend_rows(c, r, slot):
        heads = 2 if c < 4 else 1
        lanes = heads * seq_len
        key_pos = lax.broadcasted_iota(jnp.int32, (seq_len, lanes), 0)
        query_pos = lax.broadcasted_iota(jnp.int32, (seq_len, lanes), 1) % seq_len
        causal = key_pos <= query_pos
        position = lax.broadcasted_iota(jnp.int32, (1, lanes), 1) % seq_len
        pieces = []
        for item in range(GROUP):
            here = slice(item * seq_len, (item + 1) * seq_len)
            keys = kst[pl.ds(pl.multiple_of(r * rows_group + item * seq_len, 16), seq_len), :]
            stacked = qst[slot, here, :HEAD_DIM]
            if heads == 2:
                stacked = jnp.concatenate([stacked, qst[slot, here, HEAD_DIM:]], axis=0)
            scores = lax.dot_general(keys, stacked, NT, preferred_element_type=FULL)
            scores = jnp.where(causal, scores * (1.0 / math.sqrt(HEAD_DIM)), -1e30)
            expanded = jnp.exp(scores - jnp.max(scores, axis=0, keepdims=True))
            length = lens[r * GROUP + item]
            share = jnp.where(position < length, 1.0, 0.0) / (
                jnp.sum(expanded, axis=0, keepdims=True)
                * jnp.full((1, lanes), length, jnp.int32).astype(FULL)
            )
            pieces.append((expanded * share).astype(HALF))
        weights = jnp.concatenate(pieces, axis=0)
        head_row = lax.broadcasted_iota(jnp.int32, (16, lanes), 0) // GROUP
        head_lane = lax.broadcasted_iota(jnp.int32, (16, lanes), 1) // seq_len
        chosen = jnp.where(head_row == head_lane, 1.0, 0.0).astype(HALF)
        sums_of = lax.dot_general(chosen, weights, NT, preferred_element_type=FULL)
        item_row = lax.broadcasted_iota(jnp.int32, sums_of.shape, 0) % GROUP
        item_lane = lax.broadcasted_iota(jnp.int32, sums_of.shape, 1) // seq_len
        sums_of = jnp.where(item_row == item_lane, sums_of, 0.0)
        coarse = sums_of.astype(HALF).astype(FULL)
        both = jnp.concatenate([coarse, sums_of - coarse], axis=0).astype(HALF)
        rows = pl.ds(pl.multiple_of(r * rows_group, 128), rows_group)
        mixed = jnp.dot(both, vst[rows, :], preferred_element_type=FULL)
        ctx[c - 1, r] = mixed[:16] + mixed[16:]

    def query_block(c, low, top):
        query_rows(c, low, low % 2)

        @pl.loop(low + 1, top)
        def _(r):
            attend_rows(c, r - 1, (r - 1) % 2)
            query_rows(c, r, r % 2)

        attend_rows(c, top - 1, (top - 1) % 2)

    def member_squares(low, top):
        @pl.loop(low, top)
        def _(step):
            rows = pl.ds(pl.multiple_of(step * 64, 64), 64)
            values = members[rows, :].astype(FULL)
            squares[rows, :] = jnp.broadcast_to(
                jnp.sum(values * values, axis=-1, keepdims=True), (64, 128)
            )

    @at_mid
    def _():
        onward("mid", 0, (2, 0), 1, 0)
        onward("mid", 0, (0, 0), 2)

    @at_end
    def _():
        onward("end", 0, (0, 1), 1)

    load_members.wait()
    member_squares(0, 4)
    relay_tokens(0)

    @at_mid
    def _():
        onward("mid", 1, (0, 0), 2)
        own("mid", 2, 2)
        onward("mid", 1, (2, 0), 0)
        own("mid", 0, 4)

    @at_end
    def _():
        onward("end", 1, (0, 1), 1)

    pool()

    @at_mid
    def _():
        onward("mid", 0, (3, 0), 1, 0)
        onward("mid", 0, (1, 1), 1)
        send("mid", 1, 1, (2, 0))
        onward("mid", 2, (0, 0), 2)
        own("mid", 2, 3)

    @at_end
    def _():
        onward("end", 0, (2, 0), 0)
        onward("end", 2, (0, 1), 1)

    relay_tokens(1)

    @at_mid
    def _():
        onward("mid", 1, (3, 0), 1, 0)
        own("mid", 1, 2)
        onward("mid", 3, (0, 0), 2)
        own("mid", 2, 4)

    @at_end
    def _():
        onward("end", 0, (3, 0), 0)
        onward("end", 1, (1, 0), 0)
        own("end", 0, 4)
        onward("end", 3, (0, 1), 1)
        own("end", 1, 4)

    relay_tokens(2)

    @at_mid
    def _():
        onward("mid", 2, (2, 0), 1, 0)
        onward("mid", 4, (0, 0), 2)

    @at_end
    def _():
        onward("end", 1, (2, 0), 0)

    member_squares(4, 8)
    relay_tokens(3)

    @at_mid
    def _():
        onward("mid", 2, (3, 0), 1, 0)
        own("mid", 1, 3)
        onward("mid", 2, (1, 1), 1)
        onward("mid", 3, (2, 0), 1, 0)

    core_copy(core_peer).wait_recv()
    rest(0)
    keyval_rows(0, 4)

    @at_end
    def _():
        onward("end", 1, (3, 0), 0)
        onward("end", 4, (0, 1), 1)

    relay_tokens(4)

    @at_mid
    def _():
        onward("mid", 3, (3, 0), 1, 0)
        onward("mid", 4, (2, 0), 1, 0)

    relay_tokens(5)

    @at_end
    def _():
        onward("end", 2, (2, 0), 0)

    @at_mid
    def _():
        onward("mid", 4, (3, 0), 1, 0)
        own("mid", 1, 4)
        onward("mid", 4, (1, 1), 1)

    keyval_rows(4, 6)
    rest(1)
    query_block(1, 0, 1)

    @at_end
    def _():
        onward("end", 2, (3, 0), 0)

    query_block(1, 1, 3)
    relay_tokens(6)
    load_out.wait()
    own_out = out_copy(0, mp, y_peer)
    own_out.start()
    beside_out = out_copy(1, mp, core_peer)
    beside_out.start()
    need(2, 0, 2)
    partial_block(2, across(0) * part, part, True, 0, 3)
    partial_block(2, across(2) * part, part, False, 0, 3)

    @at_end
    def _():
        onward("end", 3, (1, 0), 0)

    need(2, 3)
    partial_block(2, across(3) * part, part, False, 0, 3)
    relay_tokens(7)
    keyval_rows(6, 8)
    query_block(1, 3, 4)
    partial_block(2, across(0) * part, part, True, 3, 4)
    partial_block(2, across(2) * part, part, False, 3, 4)
    partial_block(2, across(3) * part, part, False, 3, 4)
    rest(2)
    query_block(2, 0, 2)

    @at_end
    def _():
        onward("end", 3, (2, 0), 0)

    query_block(2, 2, 4)

    lane_head = (place_lane // GROUP) % 2
    heads_of = (((0, 2), (1, 3)), ((4, 5),), ((6, None),))
    couts, cins = (cout_a, cout_b, cout_c), (cin_a, cin_b, cin_c)

    def pick(h, right):
        right = right & (lane_head == h % 2)
        return jnp.where(right & (held == slot_wide), 1.0, 0.0).astype(HALF)[:, :64]

    def group_copy(p, j, m_slot):
        to = (mp + j) % 4
        return remote(
            couts[p].at[to], cins[p].at[dp, m_slot], a_send.at[p, j], a_recv.at[p, m_slot], dp, to
        )

    def context_copy(p, i, d_slot):
        return remote(
            cins[p].at[d_slot], cins[p].at[d_slot], c_send.at[p, i], c_recv.at[p, d_slot],
            (dp + i) % 8, mp,
        )

    def share_part(p):
        for block, (top, bottom) in enumerate(heads_of[p]):
            rows = ctx[top // 2].reshape(64, 128).astype(HALF)
            value = jnp.dot(pick(top, upper), rows, preferred_element_type=FULL)
            if bottom is not None:
                rows = ctx[bottom // 2].reshape(64, 128).astype(HALF)
                value = value + jnp.dot(
                    pick(bottom, jnp.logical_not(upper)), rows, preferred_element_type=FULL
                )
            couts[p][:, :, block * 128 : (block + 1) * 128] = value.astype(HALF).reshape(
                4, 16, 128
            )
        for j in range(1, 4):
            group_copy(p, j, mp).start()
        cins[p][dp, mp] = couts[p][mp]

    def spread_part(p):
        for j in range(1, 4):
            group_copy(p, j, (mp + j) % 4).wait_recv()
        for i in (4, 3, 5, 2, 6, 1, 7):
            context_copy(p, i, dp).start()

    share_part(0)
    need(3, 0, 1)
    partial_block(3, high * 2 * part, 2 * part, True)

    @at_end
    def _():
        onward("end", 3, (3, 0), 0)

    need(3, 2)
    partial_block(3, across(2) * part, part, False)

    @at_end
    def _():
        onward("end", 4, (2, 0), 0)

    need(4, 0)
    partial_block(4, across(0) * part, part, True)

    @at_end
    def _():
        onward("end", 4, (3, 0), 0)

    spread_part(0)

    limit = counts[0] * 0
    for c in range(counts.shape[0]):
        limit = limit + jnp.where(owner[c] == dp, counts[c], 0)
    member_count = members.shape[0]
    member = mp * member_count + lax.broadcasted_iota(jnp.int32, (1, member_count), 1)
    scale = jnp.where(member < limit, logit_scale, 0.0) * lax.rsqrt(squares[...].T[0:1, :] + 1e-06)
    rest(3)
    query_block(3, 0, 4)
    share_part(1)
    spread_pool()
    need(4, 2)
    partial_block(4, across(2) * part, part, False)
    spread_part(1)
    need(4, 1)
    partial_block(4, across(1) * part, part, False)
    out_copy(0, y_peer, y_peer).wait_recv()
    onward_out = out_copy(2, y_peer, core_peer)
    onward_out.start()
    rest(4)
    query_block(4, 0, 4)
    share_part(2)
    out_copy(1, core_peer, core_peer).wait_recv()
    out_copy(2, far, core_peer).wait_recv()
    for i in range(1, 8):
        pool_copy(i, (dp + i) % 8).wait_recv()
    spread_part(2)

    half_out = wot.shape[0]
    total_a = jnp.zeros((128, half_out), FULL)
    total_b = jnp.zeros((128, half_out), FULL)

    def lanes_from(m, first, length):
        return wot[:, m * part + first : m * part + first + length]

    for p in range(3):
        for i in range(1, 8):
            context_copy(p, i, (dp + i) % 8).wait_recv()
        length = cins[p].shape[3]
        for m in range(4):
            have = cins[p][:, m].reshape(128, length)
            first = (0, 512, 768)[p]
            total_a = total_a + lax.dot_general(
                have, lanes_from(m, first, length), NT, preferred_element_type=FULL
            )
            if p < 2:
                total_b = total_b + lax.dot_general(
                    have, lanes_from(m, first + length, length), NT, preferred_element_type=FULL
                )
    embedded = (
        total_a.reshape(8, 16, half_out)[:, :8]
        + total_b.reshape(8, 16, half_out)[:, 8:]
    ).reshape(64, half_out)
    pooled = pool_in[...].astype(FULL)
    embedded = embedded + jnp.concatenate(
        [pooled[:, :8].reshape(64, 256), pooled[:, 8:].reshape(64, 256)[:, : half_out - 256]],
        axis=1,
    )
    row = lax.broadcasted_iota(jnp.int32, (64, 64), 0)
    column = lax.broadcasted_iota(jnp.int32, (64, 64), 1)
    order = jnp.where(
        column == ((row // 4) % 8) * 8 + (row // 32) * 4 + row % 4, 1.0, 0.0
    ).astype(HALF)
    sums[...] = (
        jnp.dot(order, embedded.astype(HALF), preferred_element_type=FULL)
        .astype(HALF)
        .reshape(sums.shape)
    )

    core = mp % 2
    home = 2 * x + (z + 1) // 2 % 2

    def sum_copy(j, y):
        return remote(
            sums.at[j], rows_in.at[dp], d_send.at[j, y], d_recv.at[dp], owner_of(mp, j), 2 * y + x
        )

    def hand_copy(k, slot):
        return remote(
            rows_in.at[slot], rows_in.at[slot], e_send.at[k], d_recv.at[slot], dp, core_peer
        )

    for j in range(2):
        for y in range(2):
            mine = (owner_of(mp, j) == dp) & (2 * y + x == mp)

            @pl.when(jnp.logical_not(mine))
            def _():
                sum_copy(j, y).start()

            @pl.when(mine)
            def _():
                rows_in[dp] = sums[j]

    for k in range(4):
        slot = 2 * k + core

        @pl.when(jnp.logical_not((slot == dp) & (mp == home)))
        def _():
            hand_copy(k, slot).wait_recv()

        hand_copy(k, slot).start()
    for k in range(4):
        hand_copy(k, 2 * k + 1 - core).wait_recv()

    for slot in range(8):
        joined[:, slot * half_out : (slot + 1) * half_out] = rows_in[slot].astype(FULL)
    embedding = joined[...]
    dots = lax.dot_general(
        embedding.astype(HALF), members[...], NT, preferred_element_type=FULL
    )
    inverse = lax.rsqrt(jnp.sum(embedding * embedding, axis=-1, keepdims=True) + 1e-06)
    found = (dots * inverse * scale).astype(HALF)
    row = lax.broadcasted_iota(jnp.int32, (128, 32), 0)
    column = lax.broadcasted_iota(jnp.int32, (128, 32), 1)
    value = jnp.zeros((128, 128), FULL)
    for q in range(4):
        spread = jnp.where(
            ((row % 16) // 4 == q) & (column == (row // 16) * 4 + row % 4), 1.0, 0.0
        ).astype(HALF)
        value = value + jnp.dot(
            spread, found[:, q * 128 : (q + 1) * 128], preferred_element_type=FULL
        )
    replies[...] = value.astype(HALF).reshape(replies.shape)

    def reply_copy(i, slot):
        to = (dp + i) % 8
        return remote(replies.at[to], arrived.at[slot], f_send.at[i], f_recv.at[slot], to, mp)

    for i in range(1, 8):
        reply_copy(i, dp).start()
    arrived[dp] = replies[dp]
    for i in range(1, 8):
        reply_copy(i, (dp + i) % 8).wait_recv()
    have = arrived[...].reshape(128, 128)
    column = lax.broadcasted_iota(jnp.int32, (dialogs, 128), 1).astype(FULL)
    for q in range(4):
        fetch = jnp.where(column == reply_place + 4.0 * q, flag_col, 0.0).astype(HALF)
        out[:, q * 128 : (q + 1) * 128] = jnp.dot(fetch, have, preferred_element_type=FULL)

    for r in range(chunks):
        y_copy(r, mp).wait_send()
        forward_copy(r, y_peer).wait_send()
    core_copy(mp).wait_send()
    own_out.wait_send()
    beside_out.wait_send()
    onward_out.wait_send()

    @at_end
    def _():
        for way, c, kind in sent["end"]:
            weight_copy(way, c, kind).wait_send()

    @at_mid
    def _():
        for way, c, kind in sent["mid"]:
            weight_copy(way, c, kind).wait_send()

    for j in range(2):
        for y in range(2):
            @pl.when(jnp.logical_not((owner_of(mp, j) == dp) & (2 * y + x == mp)))
            def _():
                sum_copy(j, y).wait_send()

    for k in range(4):
        hand_copy(k, 2 * k + core).wait_send()
    for i in range(1, 4):
        pool_group(i, mp).wait_send()
        for p in range(3):
            group_copy(p, i, mp).wait_send()
    for i in range(1, 8):
        for p in range(3):
            context_copy(p, i, dp).wait_send()
        reply_copy(i, dp).wait_send()
        pool_copy(i, dp).wait_send()


def fused(
    tokens, norm_gain, w_query, w_keyval, w_out, residents, lengths, cluster, owner, counts, flags
):
    dialogs, seq_len, part = tokens.shape
    total = dialogs * seq_len
    depth, queries = w_query.shape
    width = norm_gain.shape[0]
    member_count = residents.shape[1]
    half_out = w_out.shape[1]
    half = HEAD_DIM // 2
    freqs = rope_base ** (-np.arange(half, dtype=np.float64) * 2.0 / HEAD_DIM)
    angles = np.arange(seq_len, dtype=np.float64)[:, None] * freqs[None, :]
    cosine, sine = np.cos(angles), np.sin(angles)
    cosine = np.tile(np.concatenate([cosine, cosine], axis=1), (CHUNK, 1)).astype(np.float32)
    sine = np.tile(np.concatenate([-sine, sine], axis=1), (CHUNK, 1)).astype(np.float32)
    vmem = pl.BlockSpec(memory_space=pltpu.VMEM)
    smem = pl.BlockSpec(memory_space=pltpu.SMEM)
    hbm = pl.BlockSpec(memory_space=pltpu.HBM)
    sem = pltpu.SemaphoreType.DMA
    return pl.pallas_call(
        fused_kernel,
        out_shape=jax.ShapeDtypeStruct((dialogs, member_count), FULL),
        in_specs=[smem] * 5 + [hbm, hbm, hbm, vmem, hbm, hbm, vmem, vmem],
        out_specs=vmem,
        scratch_shapes=[
            pltpu.VMEM((total, width), HALF),
            pltpu.VMEM((4, width, 256), HALF),
            pltpu.VMEM((width, 128), HALF),
            pltpu.VMEM((half_out, width), HALF),
            pltpu.VMEM((member_count, width), HALF),
            pltpu.VMEM((depth, queries), HALF),
            pltpu.VMEM((depth, 2, 128), HALF),
            pltpu.VMEM((512, 128), FULL),
            pltpu.VMEM((total, 128), FULL),
            pltpu.VMEM((total, 128), HALF),
            pltpu.VMEM((total, 128), HALF),
            pltpu.VMEM((2, GROUP * seq_len, 256), HALF),
            pltpu.VMEM((4, 4, 16, 128), FULL),
            pltpu.VMEM((dialogs, total), HALF),
            pltpu.VMEM((total, 256), FULL),
            pltpu.VMEM((total, 128), FULL),
            pltpu.VMEM((4, 2, 16, 256), HALF),
            pltpu.VMEM((8, 16, 256), HALF),
            pltpu.VMEM((8, 16, 256), HALF),
            pltpu.VMEM((4, 16, 256), HALF),
            pltpu.VMEM((4, 16, 128), HALF),
            pltpu.VMEM((4, 16, 128), HALF),
            pltpu.VMEM((8, 4, 16, 256), HALF),
            pltpu.VMEM((8, 4, 16, 128), HALF),
            pltpu.VMEM((8, 4, 16, 128), HALF),
            pltpu.VMEM((2, 32, half_out), HALF),
            pltpu.VMEM((8, 32, half_out), HALF),
            pltpu.VMEM((32, width), FULL),
            pltpu.VMEM((member_count, 128), FULL),
            pltpu.VMEM((8, 16, 128), HALF),
            pltpu.VMEM((8, 16, 128), HALF),
            sem((5,)),
            sem((8,)),
            sem((8,)),
            sem,
            sem,
            sem((8,)),
            sem((8,)),
            sem((3, 5, 8)),
            sem((5, 8)),
            sem((3,)),
            sem((3,)),
            sem((4,)),
            sem((4,)),
            sem((8,)),
            sem((8,)),
            sem((3, 4)),
            sem((3, 4)),
            sem((3, 8)),
            sem((3, 8)),
            sem((2, 2)),
            sem((8,)),
            sem((4,)),
            sem((8,)),
            sem((8,)),
        ],
        compiler_params=pltpu.CompilerParams(
            collective_id=0, has_side_effects=True, vmem_limit_bytes=58 * 1024 * 1024
        ),
    )(
        lengths, cluster[:, 0], owner, counts, flags,
        tokens.reshape(total, part), w_query, w_keyval,
        norm_gain.reshape(-1, 128), w_out.T, residents[0], cosine, sine,
    )


def plain_project(tokens, norm_gain, w_query, w_keyval, lengths):
    gathered = lax.all_gather(tokens, "mp", axis=2, tiled=True)
    dialogs, seq_len, width = gathered.shape
    hidden = gathered.astype(jnp.float32)
    normed = (
        hidden * lax.rsqrt(jnp.mean(hidden * hidden, axis=-1, keepdims=True) + 1e-06) * norm_gain
    ).astype(jnp.bfloat16)
    normed_flat = normed.reshape(dialogs * seq_len, width)
    query_cols = w_query.shape[1]
    keyval_cols = w_keyval.shape[2]
    pieces = (
        lax.all_gather(w_query, "dp", axis=0, tiled=True),
        lax.all_gather(w_keyval, "dp", axis=0, tiled=True),
    )
    keyval_piece = pieces[1].reshape(pieces[1].shape[0], 2 * keyval_cols)
    query_sum = jnp.dot(normed_flat, pieces[0], preferred_element_type=jnp.float32)
    keyval_sum = jnp.dot(normed_flat, keyval_piece, preferred_element_type=jnp.float32)
    positions = jnp.arange(seq_len)
    local_heads = query_cols // HEAD_DIM
    local_kv = keyval_cols // HEAD_DIM
    query = jax.vmap(lambda block: rotate(block, positions))(
        query_sum.reshape(dialogs, seq_len, local_heads, HEAD_DIM)
    ).astype(jnp.bfloat16)
    keys = jax.vmap(lambda block: rotate(block, positions))(
        keyval_sum[:, :keyval_cols].reshape(dialogs, seq_len, local_kv, HEAD_DIM)
    ).astype(jnp.bfloat16)
    values = (
        keyval_sum[:, keyval_cols:]
        .reshape(dialogs, seq_len, local_kv, HEAD_DIM)
        .astype(jnp.bfloat16)
    )
    valid = (positions[None, :] < lengths[:, None]).astype(jnp.float32)
    pooled_input = (
        jnp.sum(hidden * valid[:, :, None], axis=1) / lengths.astype(jnp.float32)[:, None]
    )
    pooled_context = jax.vmap(attend)(query, keys, values, lengths).astype(jnp.bfloat16)
    return pooled_context, pooled_input


def plain_score(pooled_context, pooled_input, w_out, members, onehot, live):
    dialogs = pooled_context.shape[0]
    everyone = lax.all_gather(pooled_context, "dp", axis=0, tiled=True)
    slices = jnp.dot(everyone, w_out, preferred_element_type=jnp.float32).astype(jnp.bfloat16)
    slices = slices.reshape(-1, dialogs, w_out.shape[1])
    slices = lax.all_to_all(slices, "dp", split_axis=0, concat_axis=0, tiled=True)
    partial_out = slices.transpose(1, 0, 2).reshape(dialogs, -1)
    projected = lax.psum(partial_out, "mp").astype(jnp.float32)
    embedding = pooled_input + projected
    unit = embedding * lax.rsqrt(jnp.sum(embedding * embedding, axis=-1, keepdims=True) + 1e-06)
    unit = unit.astype(jnp.bfloat16)
    inverse_norm = lax.rsqrt(
        jnp.einsum("md,md->m", members, members, preferred_element_type=jnp.float32) + 1e-06
    )
    outgoing = jnp.einsum(
        "ocn,nd->ocd", onehot.astype(jnp.bfloat16), unit, preferred_element_type=jnp.float32
    ).astype(jnp.bfloat16)
    query_rows = lax.all_to_all(outgoing, "dp", split_axis=0, concat_axis=0, tiled=True)
    dots = lax.dot_general(
        query_rows,
        members,
        (((query_rows.ndim - 1,), (1,)), ((), ())),
        preferred_element_type=jnp.float32,
    )
    return lax.all_to_all(
        jnp.where(live[0] > 0, live[0] * dots * inverse_norm, 0.0).astype(jnp.bfloat16),
        "dp",
        split_axis=0,
        concat_axis=0,
        tiled=True,
    )


def general(
    tokens, norm_gain, w_query, w_keyval, w_out, residents, lengths, cluster, owner, counts, flags
):
    pooled_context, pooled_input = plain_project(tokens, norm_gain, w_query, w_keyval, lengths)
    dialogs = tokens.shape[0]
    my_index = lax.axis_index("dp")
    owner_count = lax.axis_size("dp")
    my_count = jnp.sum(jnp.where(owner == my_index, counts, 0))
    members = residents[0]
    member_count = members.shape[0]
    member_start = lax.axis_index("mp") * member_count
    live = jnp.where(member_start + jnp.arange(member_count) < my_count, logit_scale, 0.0)[None, :]
    table_size = owner.shape[0]
    cluster_ids = cluster[:, 0]
    destination = jnp.sum(
        jnp.where(jnp.arange(table_size)[None, :] == cluster_ids[:, None], owner[None, :], 0),
        axis=1,
    )
    capacity = max(1, -(-dialogs // owner_count))
    order = jnp.arange(dialogs)
    earlier = (destination[None, :] == destination[:, None]) & (order[None, :] < order[:, None])
    rank = jnp.sum(earlier.astype(jnp.int32), axis=1)
    onehot = (jnp.arange(owner_count)[:, None, None] == destination[None, None, :]) & (
        jnp.arange(capacity)[None, :, None] == rank[None, None, :]
    )
    returned = plain_score(pooled_context, pooled_input, w_out, members, onehot, live)
    similarity = jnp.einsum(
        "ocn,ocm->nm", onehot.astype(jnp.bfloat16), returned, preferred_element_type=jnp.float32
    )
    return similarity * flags.astype(jnp.float32)[:, None]


def local(*args):
    if lax.axis_size("dp") == 8 and lax.axis_size("mp") == 4:
        return fused(*args)
    return general(*args)


def solution(mesh):
    in_specs = (
        P("dp", None, "mp"),
        P(),
        P("dp", "mp"),
        P("dp", None, "mp"),
        P("mp", "dp"),
        P("dp", "mp"),
        P("dp"),
        P("dp"),
        P(),
        P(),
        P("dp"),
    )
    out_specs = P("dp", "mp")
    return jax.shard_map(local, mesh=mesh, in_specs=in_specs, out_specs=out_specs, check_vma=False)
```

```python
import math

import jax
import jax.numpy as jnp
import numpy as np
from jax import lax
from jax.experimental import pallas as pl
from jax.experimental.pallas import tpu as pltpu
from jax.sharding import PartitionSpec as P

HEAD_DIM = 128


rope_base = 1000000.0
logit_scale = 100.0


def rotate(values, positions):
    half = values.shape[-1] // 2
    freqs = rope_base ** (-jnp.arange(half, dtype=jnp.float32) * 2.0 / values.shape[-1])
    angles = positions.astype(jnp.float32)[:, None] * freqs[None, :]
    cosine = jnp.cos(angles)[:, None, :]
    sine = jnp.sin(angles)[:, None, :]
    first = values[..., :half]
    second = values[..., half:]
    return jnp.concatenate(
        [first * cosine - second * sine, second * cosine + first * sine], axis=-1
    )


def attend(query, keys, values, length):
    seq_len = query.shape[0]
    kv_count = keys.shape[1]
    group = query.shape[1] // kv_count
    grouped = query.reshape(seq_len, kv_count, group, query.shape[-1])
    scores = jnp.einsum(
        "qkgd,pkd->kgqp", grouped, keys, preferred_element_type=jnp.float32
    ) / math.sqrt(query.shape[-1])
    row_pos = jnp.arange(seq_len)[:, None]
    col_pos = jnp.arange(seq_len)[None, :]
    allowed = (col_pos <= row_pos) & (col_pos < length)
    scores = jnp.where(allowed, scores, -1e30)
    highest = jnp.max(scores, axis=-1, keepdims=True)
    expanded = jnp.exp(scores - highest)
    weights = (expanded / jnp.sum(expanded, axis=-1, keepdims=True)).astype(jnp.bfloat16)
    context = jnp.einsum("kgqp,pkd->qkgd", weights, values, preferred_element_type=jnp.float32)
    valid = (jnp.arange(seq_len) < length).astype(jnp.float32)
    pooled = jnp.sum(context * valid[:, None, None, None], axis=0) / length.astype(jnp.float32)
    return pooled.reshape(-1)


MESH = pl.DeviceIdType.MESH
HALF, FULL = jnp.bfloat16, jnp.float32
CHUNK = 4
GROUP = 8
NT = (((1,), (1,)), ((), ()))


def fused_kernel(
    lens, cluster, owner, counts, flags,
    tin, query_in, keyval_in, gain, w_out_in, members_in, cosine, sine,
    out,
    tok, wide, narrow, wot, members, qstage, kvstage, gcol, rs, kst, vst, qst, ctx, mask,
    acc_wide, acc_narrow, pool_mine, pool_out, pool_in, cout_a, cout_b, cout_c, cin_a, cin_b, cin_c, sums, rows_in, joined, squares, replies, arrived,
    l_sem, ty_send, ty_recv, tc_send, tc_recv, tf_send, tf_recv, wsend, wrecv,
    o_send, o_recv, g_send, g_recv, p_send, p_recv, a_send, a_recv, c_send, c_recv,
    d_send, d_recv, e_send, f_send, f_recv, e_out, e_in,
):
    dp = lax.axis_index("dp")
    mp = lax.axis_index("mp")
    z, x = dp // 2, dp % 2
    high = z // 2
    core_peer = mp + 1 - 2 * (mp % 2)
    y_peer = (mp + 2) % 4
    far = (core_peer + 2) % 4
    pair_z = z + 1 - 2 * (z % 2)
    x_peer = 2 * z + 1 - x
    total, part = tin.shape
    depth, queries = query_in.shape
    width = tok.shape[1]
    dialogs = lens.shape[0]
    seq_len = total // dialogs
    rows_each = CHUNK * seq_len
    chunks = total // rows_each
    end = (z == 0) | (z == 3)
    mid = (z == 1) | (z == 2)

    def across(k):
        return k + high * (3 - 2 * k)

    def slot_of(kind):
        k, prime = kind
        return 2 * across(k) + (1 - x if prime else x)

    def lanes_of(m):
        return pl.ds(pl.multiple_of(m * part, 128), part)

    def rows_of(r):
        return pl.ds(pl.multiple_of(r * rows_each, 64), rows_each)

    def remote(source, target, send, recv, dp_to, mp_to):
        return pltpu.make_async_remote_copy(
            src_ref=source, dst_ref=target, send_sem=send, recv_sem=recv,
            device_id={"dp": dp_to, "mp": mp_to}, device_id_type=MESH,
        )

    load_query = pltpu.make_async_copy(query_in, qstage, l_sem.at[0])
    load_keyval = pltpu.make_async_copy(keyval_in, kvstage, l_sem.at[1])
    load_tokens = pltpu.make_async_copy(tin, tok.at[:, lanes_of(mp)], l_sem.at[2])
    load_members = pltpu.make_async_copy(members_in, members, l_sem.at[3])
    load_out = pltpu.make_async_copy(w_out_in, wot.at[:, lanes_of(mp)], l_sem.at[4])
    load_keyval.start()
    load_query.start()

    barrier = pltpu.get_barrier_semaphore()

    def greet(dp_to, mp_to):
        pl.semaphore_signal(
            barrier, inc=1, device_id={"dp": dp_to, "mp": mp_to}, device_id_type=MESH
        )

    greet(dp, core_peer)
    greet(dp, y_peer)
    greet(x_peer, mp)
    greet(2 * pair_z + x, mp)

    @pl.when(mid)
    def _():
        greet(2 * across(2) + x, mp)

    load_tokens.start()
    load_members.start()
    load_out.start()

    first = (7 * dp) // 2
    for i in range(4):
        row = gain[pl.ds(first + i, 1), :]
        gcol[i * 128 : (i + 1) * 128, :] = jnp.broadcast_to(row, (128, 128)).T
    own_rows = pl.ds(pl.multiple_of(dp * depth, 64), depth)

    def gained(piece):
        factor = gcol[pl.ds(pl.multiple_of((dp % 2) * 64, 64), depth), :]
        return (piece.astype(FULL) * factor).astype(HALF)

    def fill_keyval():
        for i in range(2):
            wide[0, own_rows, i * 128 : (i + 1) * 128] = gained(kvstage[:, i, :])

    def fill_query(c):
        for h in range(2 * c - 2, min(2 * c, 7)):
            piece = gained(qstage[:, h * 128 : (h + 1) * 128])
            if h < 6:
                wide[c, own_rows, (h % 2) * 128 : (h % 2 + 1) * 128] = piece
            else:
                narrow[own_rows, :] = piece

    load_keyval.wait()
    fill_keyval()

    @pl.when(end)
    def _():
        pl.semaphore_wait(barrier, 4)

    @pl.when(mid)
    def _():
        pl.semaphore_wait(barrier, 5)

    def block_ref(c, slot):
        rows = pl.ds(pl.multiple_of(slot * depth, 64), depth)
        return wide.at[c, rows, :] if c < 4 else narrow.at[rows, :]

    ways = (x_peer, 2 * pair_z + x, 2 * across(2) + x)
    own_kind = {"end": (0, 0), "mid": (1, 0)}
    sent = {"end": [], "mid": []}
    waited = {"end": set(), "mid": set()}
    every = {
        "end": [(0, 1), (1, 0), (1, 1), (2, 0), (2, 1), (3, 0), (3, 1)],
        "mid": [(0, 0), (0, 1), (1, 1), (2, 0), (2, 1), (3, 0), (3, 1)],
    }

    def weight_copy(way, c, kind):
        slot = slot_of(kind)
        return remote(
            block_ref(c, slot), block_ref(c, slot), wsend.at[way, c, slot], wrecv.at[c, slot],
            ways[way], mp,
        )

    def send(role, way, c, kind):
        sent[role].append((way, c, kind))
        weight_copy(way, c, kind).start()

    def own(role, way, c):
        send(role, way, c, own_kind[role])

    def arrive(role, c, kind):
        if (c, kind) not in waited[role]:
            waited[role].add((c, kind))
            weight_copy(0, c, kind).wait_recv()

    def onward(role, c, kind, *to):
        arrive(role, c, kind)
        for way in to:
            send(role, way, c, kind)

    def at_end(f):
        pl.when(end)(f)

    def at_mid(f):
        pl.when(mid)(f)

    def rest(c):
        @at_end
        def _():
            for kind in every["end"]:
                arrive("end", c, kind)

        @at_mid
        def _():
            for kind in every["mid"]:
                arrive("mid", c, kind)

    def need(c, *groups):
        @at_end
        def _():
            for kind in every["end"]:
                if kind[0] in groups:
                    arrive("end", c, kind)

        @at_mid
        def _():
            for kind in every["mid"]:
                if kind[0] in groups:
                    arrive("mid", c, kind)

    def y_copy(r, m):
        return remote(
            tin.at[rows_of(r), :], tok.at[rows_of(r), lanes_of(m)], ty_send.at[r], ty_recv.at[r],
            dp, y_peer,
        )

    def forward_copy(r, m):
        return remote(
            tok.at[rows_of(r), lanes_of(m)], tok.at[rows_of(r), lanes_of(m)],
            tf_send.at[r], tf_recv.at[r], dp, core_peer,
        )

    def core_copy(m):
        return remote(tin, tok.at[:, lanes_of(m)], tc_send, tc_recv, dp, core_peer)

    def relay_tokens(r):
        y_copy(r, y_peer).wait_recv()
        forward_copy(r, y_peer).start()

    def out_copy(i, m, mp_to):
        return remote(
            wot.at[:, lanes_of(m)], wot.at[:, lanes_of(m)], o_send.at[i], o_recv.at[i], dp, mp_to
        )

    @at_end
    def _():
        own("end", 0, 0)
        own("end", 1, 0)

    @at_mid
    def _():
        own("mid", 1, 0)
        own("mid", 0, 0)
        own("mid", 2, 0)

    @pl.loop(0, chunks)
    def _(r):
        y_copy(r, mp).start()

    core_copy(mp).start()
    load_query.wait()
    fill_query(1)

    @at_end
    def _():
        own("end", 0, 1)
        own("end", 1, 1)

    @at_mid
    def _():
        own("mid", 1, 1)
        own("mid", 0, 1)
        own("mid", 2, 1)

    fill_query(2)
    fill_query(3)
    fill_query(4)

    @at_end
    def _():
        for c in (2, 3):
            own("end", 0, c)
            own("end", 1, c)

    @at_mid
    def _():
        for c in (2, 3):
            own("mid", 0, c)

    def owner_of(m, j):
        return 2 * (m % 2 + j * (3 - 2 * (m % 2))) + m // 2

    lane = lax.broadcasted_iota(jnp.int32, (dialogs, 128), 1)
    sub = lax.broadcasted_iota(jnp.int32, (dialogs, 128), 0)
    lane_dialog = GROUP * (lane // 16) + lane % GROUP
    to_col = jnp.zeros((dialogs, 128), jnp.int32)
    to_row = jnp.full((dialogs, 128), -64, jnp.int32)
    to_wide = jnp.full((dialogs, 128), -64, jnp.int32)
    len_col = jnp.zeros((dialogs, 128), jnp.int32)
    flag_col = jnp.zeros((dialogs, 128), jnp.int32)
    for d in range(dialogs):
        target = owner[cluster[d]]
        to_col = jnp.where(sub == d, target, to_col)
        to_row = jnp.where(lane == d, target, to_row)
        to_wide = jnp.where((lane_dialog == d) & (lane < 64), target, to_wide)
        len_col = jnp.where(sub == d, lens[d], len_col)
        flag_col = jnp.where(sub == d, flags[d], flag_col)
    len_col = len_col.astype(FULL)
    flag_col = flag_col.astype(FULL)
    rank_col = jnp.sum(
        jnp.where((to_col == to_row) & (lane < sub), 1.0, 0.0), axis=1, keepdims=True
    )
    rank_row = jnp.sum(
        jnp.where((to_col == to_row) & (sub < lane), 1.0, 0.0), axis=0, keepdims=True
    )
    rank_wide = jnp.sum(
        jnp.where((to_col == to_wide) & (sub < lane_dialog), 1.0, 0.0), axis=0, keepdims=True
    )
    slot_row = to_row[0:1].astype(FULL) * CHUNK + rank_row
    slot_wide = to_wide[0:1].astype(FULL) * CHUNK + rank_wide
    reply_place = to_col[:, 0:1].astype(FULL) * 16.0 + rank_col
    place = lax.broadcasted_iota(jnp.int32, (64, 128), 0)
    place_lane = lax.broadcasted_iota(jnp.int32, (64, 128), 1)
    upper = place % 16 < 8
    held = (owner_of(place // 16, (place % 8) // 4) * CHUNK + place % CHUNK).astype(FULL)
    slot_match = jnp.where(held == slot_row, 1.0, 0.0)
    upper_pick = jnp.where(upper, slot_match, 0.0).astype(HALF)[:, :dialogs]
    lower_pick = jnp.where(upper, 0.0, slot_match).astype(HALF)[:, :dialogs]

    index = lax.broadcasted_iota(jnp.int32, mask.shape, 1)
    start = lax.broadcasted_iota(jnp.int32, mask.shape, 0) * seq_len
    ahead = (index - start).astype(FULL)
    mask[...] = jnp.where((ahead >= 0.0) & (ahead < len_col[:, 0:1]), 1.0, 0.0).astype(HALF)
    load_tokens.wait()

    def pool_copy(i, source):
        to = (dp + i) % 8
        return remote(pool_out.at[to], pool_in.at[source], p_send.at[i], p_recv.at[source], to, mp)

    def pool_group(j, m_slot):
        to = (mp + j) % 4
        return remote(
            pool_mine.at[to], pool_out.at[pl.ds(2 * m_slot, 2)], g_send.at[j], g_recv.at[m_slot],
            dp, to,
        )

    def pool():
        mean = jnp.dot(mask[...], tok[:, lanes_of(mp)], preferred_element_type=FULL)
        mean = (mean / len_col[:, 0:1]).astype(HALF)
        block = width // 8
        for j in range(2):
            lead = mean[:, j * block : j * block + 256]
            back = mean[:, j * block + 256 : (j + 1) * block]
            lower = jnp.dot(lower_pick, back, preferred_element_type=FULL)
            pool_mine[:, j] = (
                (
                    jnp.dot(upper_pick, lead, preferred_element_type=FULL)
                    + jnp.concatenate([lower, jnp.zeros((64, 512 - block), FULL)], axis=1)
                )
                .astype(HALF)
                .reshape(4, 16, 256)
            )
        for j in range(1, 4):
            pool_group(j, mp).start()
        pool_out[pl.ds(2 * mp, 2)] = pool_mine[mp]

    def spread_pool():
        for j in range(1, 4):
            pool_group(j, (mp + j) % 4).wait_recv()
        for i in range(1, 8):
            pool_copy(i, dp).start()
        pool_in[dp] = pool_out[dp]

    def normalize(r):
        for half in range(2):
            rows = pl.ds(pl.multiple_of(r * rows_each + half * (rows_each // 2), 32), rows_each // 2)
            values = tok[rows, :].astype(FULL)
            mean_square = jnp.sum(values * values, axis=-1, keepdims=True) * (1.0 / width)
            rs[rows, :] = jnp.broadcast_to(lax.rsqrt(mean_square + 1e-06), (rows_each // 2, 128))

    def turn(piece):
        return piece * cosine[...] + pltpu.roll(piece, HEAD_DIM // 2, 1) * sine[...]

    def keyval_rows(low, top):
        @pl.loop(low, top)
        def _(r):
            forward_copy(r, far).wait_recv()
            normalize(r)
            rows = rows_of(r)
            product = jnp.dot(tok[rows, :], wide[0], preferred_element_type=FULL)
            kst[rows, :] = turn(product[:, :HEAD_DIM] * rs[rows, :]).astype(HALF)
            vst[rows, :] = (product[:, HEAD_DIM:] * rs[rows, :]).astype(HALF)

    rows_group = GROUP * seq_len

    def product_of(c, rows, first, length):
        depth_rows = pl.ds(first, length)
        weights = wide[c, depth_rows, :] if c < 4 else narrow[depth_rows, :]
        return jnp.dot(tok[rows, pl.ds(first, length)], weights, preferred_element_type=FULL)

    def total_of(c):
        return acc_wide if c < 4 else acc_narrow

    def partial_block(c, first, length, fresh, low=0, top=total // GROUP // seq_len):
        @pl.loop(low, top)
        def _(r):
            rows = pl.ds(pl.multiple_of(r * rows_group, 128), rows_group)
            product = product_of(c, rows, pl.multiple_of(first, 128), length)
            if fresh:
                total_of(c)[rows, :] = product
            else:
                total_of(c)[rows, :] += product

    def query_rows(c, r, slot):
        rows = pl.ds(pl.multiple_of(r * rows_group, 128), rows_group)
        if c < 2:
            product = product_of(c, rows, 0, width)
        else:
            last = pl.multiple_of(across(3 if c > 2 else 1) * part, 128)
            product = total_of(c)[rows, :] + product_of(c, rows, last, part)
        for h in range(product.shape[1] // HEAD_DIM):
            span = slice(h * HEAD_DIM, (h + 1) * HEAD_DIM)
            for half in range(2):
                here = slice(half * rows_each, (half + 1) * rows_each)
                some = pl.ds(
                    pl.multiple_of(r * rows_group + half * rows_each, 64), rows_each
                )
                qst[slot, here, span] = turn(product[here, span] * rs[some, :]).astype(HALF)

    def attend_rows(c, r, slot):
        heads = 2 if c < 4 else 1
        lanes = heads * seq_len
        key_pos = lax.broadcasted_iota(jnp.int32, (seq_len, lanes), 0)
        query_pos = lax.broadcasted_iota(jnp.int32, (seq_len, lanes), 1) % seq_len
        causal = key_pos <= query_pos
        position = lax.broadcasted_iota(jnp.int32, (1, lanes), 1) % seq_len
        pieces = []
        for item in range(GROUP):
            here = slice(item * seq_len, (item + 1) * seq_len)
            keys = kst[pl.ds(pl.multiple_of(r * rows_group + item * seq_len, 16), seq_len), :]
            stacked = qst[slot, here, :HEAD_DIM]
            if heads == 2:
                stacked = jnp.concatenate([stacked, qst[slot, here, HEAD_DIM:]], axis=0)
            scores = lax.dot_general(keys, stacked, NT, preferred_element_type=FULL)
            scores = jnp.where(causal, scores * (1.0 / math.sqrt(HEAD_DIM)), -1e30)
            expanded = jnp.exp(scores - jnp.max(scores, axis=0, keepdims=True))
            length = lens[r * GROUP + item]
            share = jnp.where(position < length, 1.0, 0.0) / (
                jnp.sum(expanded, axis=0, keepdims=True)
                * jnp.full((1, lanes), length, jnp.int32).astype(FULL)
            )
            pieces.append((expanded * share).astype(HALF))
        weights = jnp.concatenate(pieces, axis=0)
        head_row = lax.broadcasted_iota(jnp.int32, (16, lanes), 0) // GROUP
        head_lane = lax.broadcasted_iota(jnp.int32, (16, lanes), 1) // seq_len
        chosen = jnp.where(head_row == head_lane, 1.0, 0.0).astype(HALF)
        sums_of = lax.dot_general(chosen, weights, NT, preferred_element_type=FULL)
        item_row = lax.broadcasted_iota(jnp.int32, sums_of.shape, 0) % GROUP
        item_lane = lax.broadcasted_iota(jnp.int32, sums_of.shape, 1) // seq_len
        sums_of = jnp.where(item_row == item_lane, sums_of, 0.0)
        coarse = sums_of.astype(HALF).astype(FULL)
        both = jnp.concatenate([coarse, sums_of - coarse], axis=0).astype(HALF)
        rows = pl.ds(pl.multiple_of(r * rows_group, 128), rows_group)
        mixed = jnp.dot(both, vst[rows, :], preferred_element_type=FULL)
        ctx[c - 1, r] = mixed[:16] + mixed[16:]

    def query_block(c, low, top):
        query_rows(c, low, low % 2)

        @pl.loop(low + 1, top)
        def _(r):
            attend_rows(c, r - 1, (r - 1) % 2)
            query_rows(c, r, r % 2)

        attend_rows(c, top - 1, (top - 1) % 2)

    def member_squares(low, top):
        @pl.loop(low, top)
        def _(step):
            rows = pl.ds(pl.multiple_of(step * 64, 64), 64)
            values = members[rows, :].astype(FULL)
            squares[rows, :] = jnp.broadcast_to(
                jnp.sum(values * values, axis=-1, keepdims=True), (64, 128)
            )

    @at_mid
    def _():
        onward("mid", 0, (2, 0), 1, 0)
        onward("mid", 0, (0, 0), 2)

    @at_end
    def _():
        onward("end", 0, (0, 1), 1)

    load_members.wait()
    member_squares(0, 4)
    relay_tokens(0)

    @at_mid
    def _():
        onward("mid", 1, (0, 0), 2)
        own("mid", 2, 2)
        onward("mid", 1, (2, 0), 0)
        own("mid", 0, 4)

    @at_end
    def _():
        onward("end", 1, (0, 1), 1)

    pool()

    @at_mid
    def _():
        onward("mid", 0, (3, 0), 1, 0)
        onward("mid", 0, (1, 1), 1)
        send("mid", 1, 1, (2, 0))
        onward("mid", 2, (0, 0), 2)
        own("mid", 2, 3)

    @at_end
    def _():
        onward("end", 0, (2, 0), 0)
        onward("end", 2, (0, 1), 1)

    relay_tokens(1)

    @at_mid
    def _():
        onward("mid", 1, (3, 0), 1, 0)
        own("mid", 1, 2)
        onward("mid", 3, (0, 0), 2)
        own("mid", 2, 4)

    @at_end
    def _():
        onward("end", 0, (3, 0), 0)
        onward("end", 1, (1, 0), 0)
        own("end", 0, 4)
        onward("end", 3, (0, 1), 1)
        own("end", 1, 4)

    relay_tokens(2)

    @at_mid
    def _():
        onward("mid", 2, (2, 0), 1, 0)
        onward("mid", 4, (0, 0), 2)

    @at_end
    def _():
        onward("end", 1, (2, 0), 0)

    member_squares(4, 8)
    relay_tokens(3)

    @at_mid
    def _():
        onward("mid", 2, (3, 0), 1, 0)
        own("mid", 1, 3)
        onward("mid", 2, (1, 1), 1)
        onward("mid", 3, (2, 0), 1, 0)

    core_copy(core_peer).wait_recv()
    rest(0)
    keyval_rows(0, 4)

    @at_end
    def _():
        onward("end", 1, (3, 0), 0)
        onward("end", 4, (0, 1), 1)

    relay_tokens(4)

    @at_mid
    def _():
        onward("mid", 3, (3, 0), 1, 0)
        onward("mid", 4, (2, 0), 1, 0)

    relay_tokens(5)

    @at_end
    def _():
        onward("end", 2, (2, 0), 0)

    @at_mid
    def _():
        onward("mid", 4, (3, 0), 1, 0)
        own("mid", 1, 4)
        onward("mid", 4, (1, 1), 1)

    keyval_rows(4, 6)
    rest(1)
    query_block(1, 0, 1)

    @at_end
    def _():
        onward("end", 2, (3, 0), 0)

    query_block(1, 1, 3)
    relay_tokens(6)
    load_out.wait()
    own_out = out_copy(0, mp, y_peer)
    own_out.start()
    beside_out = out_copy(1, mp, core_peer)
    beside_out.start()
    need(2, 0, 2)
    partial_block(2, across(0) * part, part, True, 0, 3)
    partial_block(2, across(2) * part, part, False, 0, 3)

    @at_end
    def _():
        onward("end", 3, (1, 0), 0)

    need(2, 3)
    partial_block(2, across(3) * part, part, False, 0, 3)
    relay_tokens(7)
    keyval_rows(6, 8)
    query_block(1, 3, 4)
    partial_block(2, across(0) * part, part, True, 3, 4)
    partial_block(2, across(2) * part, part, False, 3, 4)
    partial_block(2, across(3) * part, part, False, 3, 4)
    rest(2)
    query_block(2, 0, 2)

    @at_end
    def _():
        onward("end", 3, (2, 0), 0)

    query_block(2, 2, 4)

    lane_head = (place_lane // GROUP) % 2
    heads_of = (((0, 2), (1, 3)), ((4, 5),), ((6, None),))
    couts, cins = (cout_a, cout_b, cout_c), (cin_a, cin_b, cin_c)

    def pick(h, right):
        right = right & (lane_head == h % 2)
        return jnp.where(right & (held == slot_wide), 1.0, 0.0).astype(HALF)[:, :64]

    def group_copy(p, j, m_slot):
        to = (mp + j) % 4
        return remote(
            couts[p].at[to], cins[p].at[dp, m_slot], a_send.at[p, j], a_recv.at[p, m_slot], dp, to
        )

    def context_copy(p, i, d_slot):
        return remote(
            cins[p].at[d_slot], cins[p].at[d_slot], c_send.at[p, i], c_recv.at[p, d_slot],
            (dp + i) % 8, mp,
        )

    def direct_copy(i, j, d_slot, m_slot):
        to = (mp + j) % 4
        return remote(
            cout_c.at[to], cin_c.at[d_slot, m_slot], e_out.at[i, j], e_in.at[d_slot, m_slot],
            (dp + i) % 8, to,
        )

    partners = [(i, j) for i in (4, 3, 5, 2, 6, 1, 7, 0) for j in range(4) if i or j]

    def share_part(p):
        for block, (top, bottom) in enumerate(heads_of[p]):
            rows = ctx[top // 2].reshape(64, 128).astype(HALF)
            value = jnp.dot(pick(top, upper), rows, preferred_element_type=FULL)
            if bottom is not None:
                rows = ctx[bottom // 2].reshape(64, 128).astype(HALF)
                value = value + jnp.dot(
                    pick(bottom, jnp.logical_not(upper)), rows, preferred_element_type=FULL
                )
            couts[p][:, :, block * 128 : (block + 1) * 128] = value.astype(HALF).reshape(
                4, 16, 128
            )
        if p == 2:
            for i, j in partners:
                direct_copy(i, j, dp, mp).start()
        else:
            for j in range(1, 4):
                group_copy(p, j, mp).start()
        cins[p][dp, mp] = couts[p][mp]

    def spread_part(p):
        for j in range(1, 4):
            group_copy(p, j, (mp + j) % 4).wait_recv()
        for i in (4, 3, 5, 2, 6, 1, 7):
            context_copy(p, i, dp).start()

    share_part(0)
    need(3, 0, 1)
    partial_block(3, high * 2 * part, 2 * part, True)

    @at_end
    def _():
        onward("end", 3, (3, 0), 0)

    need(3, 2)
    partial_block(3, across(2) * part, part, False)

    @at_end
    def _():
        onward("end", 4, (2, 0), 0)

    need(4, 0)
    partial_block(4, across(0) * part, part, True)

    @at_end
    def _():
        onward("end", 4, (3, 0), 0)

    spread_part(0)

    limit = counts[0] * 0
    for c in range(counts.shape[0]):
        limit = limit + jnp.where(owner[c] == dp, counts[c], 0)
    member_count = members.shape[0]
    member = mp * member_count + lax.broadcasted_iota(jnp.int32, (1, member_count), 1)
    scale = jnp.where(member < limit, logit_scale, 0.0) * lax.rsqrt(squares[...].T[0:1, :] + 1e-06)
    rest(3)
    query_block(3, 0, 4)
    share_part(1)
    spread_pool()
    need(4, 2)
    partial_block(4, across(2) * part, part, False)
    spread_part(1)
    need(4, 1)
    partial_block(4, across(1) * part, part, False)
    out_copy(0, y_peer, y_peer).wait_recv()
    onward_out = out_copy(2, y_peer, core_peer)
    onward_out.start()
    rest(4)
    query_block(4, 0, 4)
    share_part(2)
    out_copy(1, core_peer, core_peer).wait_recv()
    out_copy(2, far, core_peer).wait_recv()

    half_out = wot.shape[0]
    total_a = jnp.zeros((128, half_out), FULL)
    total_b = jnp.zeros((128, half_out), FULL)

    def lanes_from(m, first, length):
        return wot[:, m * part + first : m * part + first + length]

    for p in range(3):
        if p == 2:
            for i, j in partners:
                direct_copy(i, j, (dp + i) % 8, (mp + j) % 4).wait_recv()
        else:
            for i in range(1, 8):
                context_copy(p, i, (dp + i) % 8).wait_recv()
        length = cins[p].shape[3]
        for m in range(4):
            have = cins[p][:, m].reshape(128, length)
            first = (0, 512, 768)[p]
            total_a = total_a + lax.dot_general(
                have, lanes_from(m, first, length), NT, preferred_element_type=FULL
            )
            if p < 2:
                total_b = total_b + lax.dot_general(
                    have, lanes_from(m, first + length, length), NT, preferred_element_type=FULL
                )
    embedded = (
        total_a.reshape(8, 16, half_out)[:, :8]
        + total_b.reshape(8, 16, half_out)[:, 8:]
    ).reshape(64, half_out)
    for i in range(1, 8):
        pool_copy(i, (dp + i) % 8).wait_recv()
    pooled = pool_in[...].astype(FULL)
    embedded = embedded + jnp.concatenate(
        [pooled[:, :8].reshape(64, 256), pooled[:, 8:].reshape(64, 256)[:, : half_out - 256]],
        axis=1,
    )
    row = lax.broadcasted_iota(jnp.int32, (64, 64), 0)
    column = lax.broadcasted_iota(jnp.int32, (64, 64), 1)
    order = jnp.where(
        column == ((row // 4) % 8) * 8 + (row // 32) * 4 + row % 4, 1.0, 0.0
    ).astype(HALF)
    sums[...] = (
        jnp.dot(order, embedded.astype(HALF), preferred_element_type=FULL)
        .astype(HALF)
        .reshape(sums.shape)
    )

    core = mp % 2
    home = 2 * x + (z + 1) // 2 % 2

    def sum_copy(j, y):
        return remote(
            sums.at[j], rows_in.at[dp], d_send.at[j, y], d_recv.at[dp], owner_of(mp, j), 2 * y + x
        )

    def hand_copy(k, slot):
        return remote(
            rows_in.at[slot], rows_in.at[slot], e_send.at[k], d_recv.at[slot], dp, core_peer
        )

    for j in range(2):
        for y in range(2):
            mine = (owner_of(mp, j) == dp) & (2 * y + x == mp)

            @pl.when(jnp.logical_not(mine))
            def _():
                sum_copy(j, y).start()

            @pl.when(mine)
            def _():
                rows_in[dp] = sums[j]

    for k in range(4):
        slot = 2 * k + core

        @pl.when(jnp.logical_not((slot == dp) & (mp == home)))
        def _():
            hand_copy(k, slot).wait_recv()

        hand_copy(k, slot).start()
    for k in range(4):
        hand_copy(k, 2 * k + 1 - core).wait_recv()

    for slot in range(8):
        joined[:, slot * half_out : (slot + 1) * half_out] = rows_in[slot].astype(FULL)
    embedding = joined[...]
    dots = lax.dot_general(
        embedding.astype(HALF), members[...], NT, preferred_element_type=FULL
    )
    inverse = lax.rsqrt(jnp.sum(embedding * embedding, axis=-1, keepdims=True) + 1e-06)
    found = (dots * inverse * scale).astype(HALF)
    row = lax.broadcasted_iota(jnp.int32, (128, 32), 0)
    column = lax.broadcasted_iota(jnp.int32, (128, 32), 1)
    value = jnp.zeros((128, 128), FULL)
    for q in range(4):
        spread = jnp.where(
            ((row % 16) // 4 == q) & (column == (row // 16) * 4 + row % 4), 1.0, 0.0
        ).astype(HALF)
        value = value + jnp.dot(
            spread, found[:, q * 128 : (q + 1) * 128], preferred_element_type=FULL
        )
    replies[...] = value.astype(HALF).reshape(replies.shape)

    def reply_copy(i, slot):
        to = (dp + i) % 8
        return remote(replies.at[to], arrived.at[slot], f_send.at[i], f_recv.at[slot], to, mp)

    for i in range(1, 8):
        reply_copy(i, dp).start()
    arrived[dp] = replies[dp]
    for i in range(1, 8):
        reply_copy(i, (dp + i) % 8).wait_recv()
    have = arrived[...].reshape(128, 128)
    column = lax.broadcasted_iota(jnp.int32, (dialogs, 128), 1).astype(FULL)
    for q in range(4):
        fetch = jnp.where(column == reply_place + 4.0 * q, flag_col, 0.0).astype(HALF)
        out[:, q * 128 : (q + 1) * 128] = jnp.dot(fetch, have, preferred_element_type=FULL)

    for r in range(chunks):
        y_copy(r, mp).wait_send()
        forward_copy(r, y_peer).wait_send()
    core_copy(mp).wait_send()
    own_out.wait_send()
    beside_out.wait_send()
    onward_out.wait_send()

    @at_end
    def _():
        for way, c, kind in sent["end"]:
            weight_copy(way, c, kind).wait_send()

    @at_mid
    def _():
        for way, c, kind in sent["mid"]:
            weight_copy(way, c, kind).wait_send()

    for j in range(2):
        for y in range(2):
            @pl.when(jnp.logical_not((owner_of(mp, j) == dp) & (2 * y + x == mp)))
            def _():
                sum_copy(j, y).wait_send()

    for k in range(4):
        hand_copy(k, 2 * k + core).wait_send()
    for i in range(1, 4):
        pool_group(i, mp).wait_send()
        for p in range(2):
            group_copy(p, i, mp).wait_send()
    for i in range(1, 8):
        for p in range(2):
            context_copy(p, i, dp).wait_send()
    for i, j in partners:
        direct_copy(i, j, dp, mp).wait_send()
    for i in range(1, 8):
        reply_copy(i, dp).wait_send()
        pool_copy(i, dp).wait_send()


def fused(
    tokens, norm_gain, w_query, w_keyval, w_out, residents, lengths, cluster, owner, counts, flags
):
    dialogs, seq_len, part = tokens.shape
    total = dialogs * seq_len
    depth, queries = w_query.shape
    width = norm_gain.shape[0]
    member_count = residents.shape[1]
    half_out = w_out.shape[1]
    half = HEAD_DIM // 2
    freqs = rope_base ** (-np.arange(half, dtype=np.float64) * 2.0 / HEAD_DIM)
    angles = np.arange(seq_len, dtype=np.float64)[:, None] * freqs[None, :]
    cosine, sine = np.cos(angles), np.sin(angles)
    cosine = np.tile(np.concatenate([cosine, cosine], axis=1), (CHUNK, 1)).astype(np.float32)
    sine = np.tile(np.concatenate([-sine, sine], axis=1), (CHUNK, 1)).astype(np.float32)
    vmem = pl.BlockSpec(memory_space=pltpu.VMEM)
    smem = pl.BlockSpec(memory_space=pltpu.SMEM)
    hbm = pl.BlockSpec(memory_space=pltpu.HBM)
    sem = pltpu.SemaphoreType.DMA
    return pl.pallas_call(
        fused_kernel,
        out_shape=jax.ShapeDtypeStruct((dialogs, member_count), FULL),
        in_specs=[smem] * 5 + [hbm, hbm, hbm, vmem, hbm, hbm, vmem, vmem],
        out_specs=vmem,
        scratch_shapes=[
            pltpu.VMEM((total, width), HALF),
            pltpu.VMEM((4, width, 256), HALF),
            pltpu.VMEM((width, 128), HALF),
            pltpu.VMEM((half_out, width), HALF),
            pltpu.VMEM((member_count, width), HALF),
            pltpu.VMEM((depth, queries), HALF),
            pltpu.VMEM((depth, 2, 128), HALF),
            pltpu.VMEM((512, 128), FULL),
            pltpu.VMEM((total, 128), FULL),
            pltpu.VMEM((total, 128), HALF),
            pltpu.VMEM((total, 128), HALF),
            pltpu.VMEM((2, GROUP * seq_len, 256), HALF),
            pltpu.VMEM((4, 4, 16, 128), FULL),
            pltpu.VMEM((dialogs, total), HALF),
            pltpu.VMEM((total, 256), FULL),
            pltpu.VMEM((total, 128), FULL),
            pltpu.VMEM((4, 2, 16, 256), HALF),
            pltpu.VMEM((8, 16, 256), HALF),
            pltpu.VMEM((8, 16, 256), HALF),
            pltpu.VMEM((4, 16, 256), HALF),
            pltpu.VMEM((4, 16, 128), HALF),
            pltpu.VMEM((4, 16, 128), HALF),
            pltpu.VMEM((8, 4, 16, 256), HALF),
            pltpu.VMEM((8, 4, 16, 128), HALF),
            pltpu.VMEM((8, 4, 16, 128), HALF),
            pltpu.VMEM((2, 32, half_out), HALF),
            pltpu.VMEM((8, 32, half_out), HALF),
            pltpu.VMEM((32, width), FULL),
            pltpu.VMEM((member_count, 128), FULL),
            pltpu.VMEM((8, 16, 128), HALF),
            pltpu.VMEM((8, 16, 128), HALF),
            sem((5,)),
            sem((8,)),
            sem((8,)),
            sem,
            sem,
            sem((8,)),
            sem((8,)),
            sem((3, 5, 8)),
            sem((5, 8)),
            sem((3,)),
            sem((3,)),
            sem((4,)),
            sem((4,)),
            sem((8,)),
            sem((8,)),
            sem((3, 4)),
            sem((3, 4)),
            sem((3, 8)),
            sem((3, 8)),
            sem((2, 2)),
            sem((8,)),
            sem((4,)),
            sem((8,)),
            sem((8,)),
            sem((8, 4)),
            sem((8, 4)),
        ],
        compiler_params=pltpu.CompilerParams(
            collective_id=0, has_side_effects=True, vmem_limit_bytes=58 * 1024 * 1024
        ),
    )(
        lengths, cluster[:, 0], owner, counts, flags,
        tokens.reshape(total, part), w_query, w_keyval,
        norm_gain.reshape(-1, 128), w_out.T, residents[0], cosine, sine,
    )


def plain_project(tokens, norm_gain, w_query, w_keyval, lengths):
    gathered = lax.all_gather(tokens, "mp", axis=2, tiled=True)
    dialogs, seq_len, width = gathered.shape
    hidden = gathered.astype(jnp.float32)
    normed = (
        hidden * lax.rsqrt(jnp.mean(hidden * hidden, axis=-1, keepdims=True) + 1e-06) * norm_gain
    ).astype(jnp.bfloat16)
    normed_flat = normed.reshape(dialogs * seq_len, width)
    query_cols = w_query.shape[1]
    keyval_cols = w_keyval.shape[2]
    pieces = (
        lax.all_gather(w_query, "dp", axis=0, tiled=True),
        lax.all_gather(w_keyval, "dp", axis=0, tiled=True),
    )
    keyval_piece = pieces[1].reshape(pieces[1].shape[0], 2 * keyval_cols)
    query_sum = jnp.dot(normed_flat, pieces[0], preferred_element_type=jnp.float32)
    keyval_sum = jnp.dot(normed_flat, keyval_piece, preferred_element_type=jnp.float32)
    positions = jnp.arange(seq_len)
    local_heads = query_cols // HEAD_DIM
    local_kv = keyval_cols // HEAD_DIM
    query = jax.vmap(lambda block: rotate(block, positions))(
        query_sum.reshape(dialogs, seq_len, local_heads, HEAD_DIM)
    ).astype(jnp.bfloat16)
    keys = jax.vmap(lambda block: rotate(block, positions))(
        keyval_sum[:, :keyval_cols].reshape(dialogs, seq_len, local_kv, HEAD_DIM)
    ).astype(jnp.bfloat16)
    values = (
        keyval_sum[:, keyval_cols:]
        .reshape(dialogs, seq_len, local_kv, HEAD_DIM)
        .astype(jnp.bfloat16)
    )
    valid = (positions[None, :] < lengths[:, None]).astype(jnp.float32)
    pooled_input = (
        jnp.sum(hidden * valid[:, :, None], axis=1) / lengths.astype(jnp.float32)[:, None]
    )
    pooled_context = jax.vmap(attend)(query, keys, values, lengths).astype(jnp.bfloat16)
    return pooled_context, pooled_input


def plain_score(pooled_context, pooled_input, w_out, members, onehot, live):
    dialogs = pooled_context.shape[0]
    everyone = lax.all_gather(pooled_context, "dp", axis=0, tiled=True)
    slices = jnp.dot(everyone, w_out, preferred_element_type=jnp.float32).astype(jnp.bfloat16)
    slices = slices.reshape(-1, dialogs, w_out.shape[1])
    slices = lax.all_to_all(slices, "dp", split_axis=0, concat_axis=0, tiled=True)
    partial_out = slices.transpose(1, 0, 2).reshape(dialogs, -1)
    projected = lax.psum(partial_out, "mp").astype(jnp.float32)
    embedding = pooled_input + projected
    unit = embedding * lax.rsqrt(jnp.sum(embedding * embedding, axis=-1, keepdims=True) + 1e-06)
    unit = unit.astype(jnp.bfloat16)
    inverse_norm = lax.rsqrt(
        jnp.einsum("md,md->m", members, members, preferred_element_type=jnp.float32) + 1e-06
    )
    outgoing = jnp.einsum(
        "ocn,nd->ocd", onehot.astype(jnp.bfloat16), unit, preferred_element_type=jnp.float32
    ).astype(jnp.bfloat16)
    query_rows = lax.all_to_all(outgoing, "dp", split_axis=0, concat_axis=0, tiled=True)
    dots = lax.dot_general(
        query_rows,
        members,
        (((query_rows.ndim - 1,), (1,)), ((), ())),
        preferred_element_type=jnp.float32,
    )
    return lax.all_to_all(
        jnp.where(live[0] > 0, live[0] * dots * inverse_norm, 0.0).astype(jnp.bfloat16),
        "dp",
        split_axis=0,
        concat_axis=0,
        tiled=True,
    )


def general(
    tokens, norm_gain, w_query, w_keyval, w_out, residents, lengths, cluster, owner, counts, flags
):
    pooled_context, pooled_input = plain_project(tokens, norm_gain, w_query, w_keyval, lengths)
    dialogs = tokens.shape[0]
    my_index = lax.axis_index("dp")
    owner_count = lax.axis_size("dp")
    my_count = jnp.sum(jnp.where(owner == my_index, counts, 0))
    members = residents[0]
    member_count = members.shape[0]
    member_start = lax.axis_index("mp") * member_count
    live = jnp.where(member_start + jnp.arange(member_count) < my_count, logit_scale, 0.0)[None, :]
    table_size = owner.shape[0]
    cluster_ids = cluster[:, 0]
    destination = jnp.sum(
        jnp.where(jnp.arange(table_size)[None, :] == cluster_ids[:, None], owner[None, :], 0),
        axis=1,
    )
    capacity = max(1, -(-dialogs // owner_count))
    order = jnp.arange(dialogs)
    earlier = (destination[None, :] == destination[:, None]) & (order[None, :] < order[:, None])
    rank = jnp.sum(earlier.astype(jnp.int32), axis=1)
    onehot = (jnp.arange(owner_count)[:, None, None] == destination[None, None, :]) & (
        jnp.arange(capacity)[None, :, None] == rank[None, None, :]
    )
    returned = plain_score(pooled_context, pooled_input, w_out, members, onehot, live)
    similarity = jnp.einsum(
        "ocn,ocm->nm", onehot.astype(jnp.bfloat16), returned, preferred_element_type=jnp.float32
    )
    return similarity * flags.astype(jnp.float32)[:, None]


def local(*args):
    if lax.axis_size("dp") == 8 and lax.axis_size("mp") == 4:
        return fused(*args)
    return general(*args)


def solution(mesh):
    in_specs = (
        P("dp", None, "mp"),
        P(),
        P("dp", "mp"),
        P("dp", None, "mp"),
        P("mp", "dp"),
        P("dp", "mp"),
        P("dp"),
        P("dp"),
        P(),
        P(),
        P("dp"),
    )
    out_specs = P("dp", "mp")
    return jax.shard_map(local, mesh=mesh, in_specs=in_specs, out_specs=out_specs, check_vma=False)
```

```python
import math

import jax
import jax.numpy as jnp
import numpy as np
from jax import lax
from jax.experimental import pallas as pl
from jax.experimental.pallas import tpu as pltpu
from jax.sharding import PartitionSpec as P

HEAD_DIM = 128


rope_base = 1000000.0
logit_scale = 100.0


def rotate(values, positions):
    half = values.shape[-1] // 2
    freqs = rope_base ** (-jnp.arange(half, dtype=jnp.float32) * 2.0 / values.shape[-1])
    angles = positions.astype(jnp.float32)[:, None] * freqs[None, :]
    cosine = jnp.cos(angles)[:, None, :]
    sine = jnp.sin(angles)[:, None, :]
    first = values[..., :half]
    second = values[..., half:]
    return jnp.concatenate(
        [first * cosine - second * sine, second * cosine + first * sine], axis=-1
    )


def attend(query, keys, values, length):
    seq_len = query.shape[0]
    kv_count = keys.shape[1]
    group = query.shape[1] // kv_count
    grouped = query.reshape(seq_len, kv_count, group, query.shape[-1])
    scores = jnp.einsum(
        "qkgd,pkd->kgqp", grouped, keys, preferred_element_type=jnp.float32
    ) / math.sqrt(query.shape[-1])
    row_pos = jnp.arange(seq_len)[:, None]
    col_pos = jnp.arange(seq_len)[None, :]
    allowed = (col_pos <= row_pos) & (col_pos < length)
    scores = jnp.where(allowed, scores, -1e30)
    highest = jnp.max(scores, axis=-1, keepdims=True)
    expanded = jnp.exp(scores - highest)
    weights = (expanded / jnp.sum(expanded, axis=-1, keepdims=True)).astype(jnp.bfloat16)
    context = jnp.einsum("kgqp,pkd->qkgd", weights, values, preferred_element_type=jnp.float32)
    valid = (jnp.arange(seq_len) < length).astype(jnp.float32)
    pooled = jnp.sum(context * valid[:, None, None, None], axis=0) / length.astype(jnp.float32)
    return pooled.reshape(-1)


MESH = pl.DeviceIdType.MESH
HALF, FULL = jnp.bfloat16, jnp.float32
CHUNK = 4
GROUP = 8
NT = (((1,), (1,)), ((), ()))


def fused_kernel(
    lens, cluster, owner, counts, flags,
    tin, query_in, keyval_in, gain, w_out_in, members_in, cosine, sine,
    out,
    tok, wide, narrow, wot, members, qstage, kvstage, gcol, rs, kst, vst, qst, ctx, mask,
    acc_wide, acc_narrow, pool_mine, pool_out, pool_in, cout_a, cout_b, cout_c, cin_a, cin_b, cin_c, sums, rows_in, joined, squares, replies, arrived,
    l_sem, ty_send, ty_recv, tc_send, tc_recv, tf_send, tf_recv, wsend, wrecv,
    o_send, o_recv, g_send, g_recv, p_send, p_recv, a_send, a_recv, c_send, c_recv,
    d_send, d_recv, e_send, f_send, f_recv, e_out, e_in,
):
    dp = lax.axis_index("dp")
    mp = lax.axis_index("mp")
    z, x = dp // 2, dp % 2
    high = z // 2
    core_peer = mp + 1 - 2 * (mp % 2)
    y_peer = (mp + 2) % 4
    far = (core_peer + 2) % 4
    pair_z = z + 1 - 2 * (z % 2)
    x_peer = 2 * z + 1 - x
    total, part = tin.shape
    depth, queries = query_in.shape
    width = tok.shape[1]
    dialogs = lens.shape[0]
    seq_len = total // dialogs
    rows_each = CHUNK * seq_len
    chunks = total // rows_each
    end = (z == 0) | (z == 3)
    mid = (z == 1) | (z == 2)

    def across(k):
        return k + high * (3 - 2 * k)

    def slot_of(kind):
        k, prime = kind
        return 2 * across(k) + (1 - x if prime else x)

    def lanes_of(m):
        return pl.ds(pl.multiple_of(m * part, 128), part)

    def rows_of(r):
        return pl.ds(pl.multiple_of(r * rows_each, 64), rows_each)

    def remote(source, target, send, recv, dp_to, mp_to):
        return pltpu.make_async_remote_copy(
            src_ref=source, dst_ref=target, send_sem=send, recv_sem=recv,
            device_id={"dp": dp_to, "mp": mp_to}, device_id_type=MESH,
        )

    load_query = pltpu.make_async_copy(query_in, qstage, l_sem.at[0])
    load_keyval = pltpu.make_async_copy(keyval_in, kvstage, l_sem.at[1])
    load_tokens = pltpu.make_async_copy(tin, tok.at[:, lanes_of(mp)], l_sem.at[2])
    load_members = pltpu.make_async_copy(members_in, members, l_sem.at[3])
    load_out = pltpu.make_async_copy(w_out_in, wot.at[:, lanes_of(mp)], l_sem.at[4])
    load_keyval.start()
    load_query.start()

    barrier = pltpu.get_barrier_semaphore()

    def greet(dp_to, mp_to):
        pl.semaphore_signal(
            barrier, inc=1, device_id={"dp": dp_to, "mp": mp_to}, device_id_type=MESH
        )

    greet(dp, core_peer)
    greet(dp, y_peer)
    greet(x_peer, mp)
    greet(2 * pair_z + x, mp)

    @pl.when(mid)
    def _():
        greet(2 * across(2) + x, mp)

    load_tokens.start()
    load_members.start()
    load_out.start()

    first = (7 * dp) // 2
    for i in range(4):
        row = gain[pl.ds(first + i, 1), :]
        gcol[i * 128 : (i + 1) * 128, :] = jnp.broadcast_to(row, (128, 128)).T
    own_rows = pl.ds(pl.multiple_of(dp * depth, 64), depth)

    def gained(piece):
        factor = gcol[pl.ds(pl.multiple_of((dp % 2) * 64, 64), depth), :]
        return (piece.astype(FULL) * factor).astype(HALF)

    def fill_keyval():
        for i in range(2):
            wide[0, own_rows, i * 128 : (i + 1) * 128] = gained(kvstage[:, i, :])

    def fill_query(c):
        for h in range(2 * c - 2, min(2 * c, 7)):
            piece = gained(qstage[:, h * 128 : (h + 1) * 128])
            if h < 6:
                wide[c, own_rows, (h % 2) * 128 : (h % 2 + 1) * 128] = piece
            else:
                narrow[own_rows, :] = piece

    load_keyval.wait()
    fill_keyval()

    @pl.when(end)
    def _():
        pl.semaphore_wait(barrier, 4)

    @pl.when(mid)
    def _():
        pl.semaphore_wait(barrier, 5)

    def block_ref(c, slot):
        rows = pl.ds(pl.multiple_of(slot * depth, 64), depth)
        return wide.at[c, rows, :] if c < 4 else narrow.at[rows, :]

    ways = (x_peer, 2 * pair_z + x, 2 * across(2) + x)
    own_kind = {"end": (0, 0), "mid": (1, 0)}
    sent = {"end": [], "mid": []}
    waited = {"end": set(), "mid": set()}
    every = {
        "end": [(0, 1), (1, 0), (1, 1), (2, 0), (2, 1), (3, 0), (3, 1)],
        "mid": [(0, 0), (0, 1), (1, 1), (2, 0), (2, 1), (3, 0), (3, 1)],
    }

    def weight_copy(way, c, kind):
        slot = slot_of(kind)
        return remote(
            block_ref(c, slot), block_ref(c, slot), wsend.at[way, c, slot], wrecv.at[c, slot],
            ways[way], mp,
        )

    def send(role, way, c, kind):
        sent[role].append((way, c, kind))
        weight_copy(way, c, kind).start()

    def own(role, way, c):
        send(role, way, c, own_kind[role])

    def arrive(role, c, kind):
        if (c, kind) not in waited[role]:
            waited[role].add((c, kind))
            weight_copy(0, c, kind).wait_recv()

    def onward(role, c, kind, *to):
        arrive(role, c, kind)
        for way in to:
            send(role, way, c, kind)

    def at_end(f):
        pl.when(end)(f)

    def at_mid(f):
        pl.when(mid)(f)

    def rest(c):
        @at_end
        def _():
            for kind in every["end"]:
                arrive("end", c, kind)

        @at_mid
        def _():
            for kind in every["mid"]:
                arrive("mid", c, kind)

    def need(c, *groups):
        @at_end
        def _():
            for kind in every["end"]:
                if kind[0] in groups:
                    arrive("end", c, kind)

        @at_mid
        def _():
            for kind in every["mid"]:
                if kind[0] in groups:
                    arrive("mid", c, kind)

    def y_copy(r, m):
        return remote(
            tin.at[rows_of(r), :], tok.at[rows_of(r), lanes_of(m)], ty_send.at[r], ty_recv.at[r],
            dp, y_peer,
        )

    def forward_copy(r, m):
        return remote(
            tok.at[rows_of(r), lanes_of(m)], tok.at[rows_of(r), lanes_of(m)],
            tf_send.at[r], tf_recv.at[r], dp, core_peer,
        )

    def core_copy(m):
        return remote(tin, tok.at[:, lanes_of(m)], tc_send, tc_recv, dp, core_peer)

    def relay_tokens(r):
        y_copy(r, y_peer).wait_recv()
        forward_copy(r, y_peer).start()

    def out_copy(i, m, mp_to):
        return remote(
            wot.at[:, lanes_of(m)], wot.at[:, lanes_of(m)], o_send.at[i], o_recv.at[i], dp, mp_to
        )

    @at_end
    def _():
        own("end", 0, 0)
        own("end", 1, 0)

    @at_mid
    def _():
        own("mid", 1, 0)
        own("mid", 0, 0)
        own("mid", 2, 0)

    @pl.loop(0, chunks)
    def _(r):
        y_copy(r, mp).start()

    core_copy(mp).start()
    load_query.wait()
    fill_query(1)

    @at_end
    def _():
        own("end", 0, 1)
        own("end", 1, 1)

    @at_mid
    def _():
        own("mid", 1, 1)
        own("mid", 0, 1)
        own("mid", 2, 1)

    fill_query(2)
    fill_query(3)
    fill_query(4)

    @at_end
    def _():
        for c in (2, 3):
            own("end", 0, c)
            own("end", 1, c)

    @at_mid
    def _():
        for c in (2, 3):
            own("mid", 0, c)

    def owner_of(m, j):
        return 2 * (m % 2 + j * (3 - 2 * (m % 2))) + m // 2

    lane = lax.broadcasted_iota(jnp.int32, (dialogs, 128), 1)
    sub = lax.broadcasted_iota(jnp.int32, (dialogs, 128), 0)
    lane_dialog = GROUP * (lane // 16) + lane % GROUP
    to_col = jnp.zeros((dialogs, 128), jnp.int32)
    to_row = jnp.full((dialogs, 128), -64, jnp.int32)
    to_wide = jnp.full((dialogs, 128), -64, jnp.int32)
    len_col = jnp.zeros((dialogs, 128), jnp.int32)
    flag_col = jnp.zeros((dialogs, 128), jnp.int32)
    for d in range(dialogs):
        target = owner[cluster[d]]
        to_col = jnp.where(sub == d, target, to_col)
        to_row = jnp.where(lane == d, target, to_row)
        to_wide = jnp.where((lane_dialog == d) & (lane < 64), target, to_wide)
        len_col = jnp.where(sub == d, lens[d], len_col)
        flag_col = jnp.where(sub == d, flags[d], flag_col)
    len_col = len_col.astype(FULL)
    flag_col = flag_col.astype(FULL)
    rank_col = jnp.sum(
        jnp.where((to_col == to_row) & (lane < sub), 1.0, 0.0), axis=1, keepdims=True
    )
    rank_row = jnp.sum(
        jnp.where((to_col == to_row) & (sub < lane), 1.0, 0.0), axis=0, keepdims=True
    )
    rank_wide = jnp.sum(
        jnp.where((to_col == to_wide) & (sub < lane_dialog), 1.0, 0.0), axis=0, keepdims=True
    )
    slot_row = to_row[0:1].astype(FULL) * CHUNK + rank_row
    slot_wide = to_wide[0:1].astype(FULL) * CHUNK + rank_wide
    reply_place = to_col[:, 0:1].astype(FULL) * 16.0 + rank_col
    place = lax.broadcasted_iota(jnp.int32, (64, 128), 0)
    place_lane = lax.broadcasted_iota(jnp.int32, (64, 128), 1)
    upper = place % 16 < 8
    held = (owner_of(place // 16, (place % 8) // 4) * CHUNK + place % CHUNK).astype(FULL)
    slot_match = jnp.where(held == slot_row, 1.0, 0.0)
    upper_pick = jnp.where(upper, slot_match, 0.0).astype(HALF)[:, :dialogs]
    lower_pick = jnp.where(upper, 0.0, slot_match).astype(HALF)[:, :dialogs]

    index = lax.broadcasted_iota(jnp.int32, mask.shape, 1)
    start = lax.broadcasted_iota(jnp.int32, mask.shape, 0) * seq_len
    ahead = (index - start).astype(FULL)
    mask[...] = jnp.where((ahead >= 0.0) & (ahead < len_col[:, 0:1]), 1.0, 0.0).astype(HALF)
    load_tokens.wait()

    def pool_copy(i, source):
        to = (dp + i) % 8
        return remote(pool_out.at[to], pool_in.at[source], p_send.at[i], p_recv.at[source], to, mp)

    def pool_group(j, m_slot):
        to = (mp + j) % 4
        return remote(
            pool_mine.at[to], pool_out.at[pl.ds(2 * m_slot, 2)], g_send.at[j], g_recv.at[m_slot],
            dp, to,
        )

    def pool():
        mean = jnp.dot(mask[...], tok[:, lanes_of(mp)], preferred_element_type=FULL)
        mean = (mean / len_col[:, 0:1]).astype(HALF)
        block = width // 8
        for j in range(2):
            lead = mean[:, j * block : j * block + 256]
            back = mean[:, j * block + 256 : (j + 1) * block]
            lower = jnp.dot(lower_pick, back, preferred_element_type=FULL)
            pool_mine[:, j] = (
                (
                    jnp.dot(upper_pick, lead, preferred_element_type=FULL)
                    + jnp.concatenate([lower, jnp.zeros((64, 512 - block), FULL)], axis=1)
                )
                .astype(HALF)
                .reshape(4, 16, 256)
            )
        for j in range(1, 4):
            pool_group(j, mp).start()
        pool_out[pl.ds(2 * mp, 2)] = pool_mine[mp]

    def spread_pool():
        for j in range(1, 4):
            pool_group(j, (mp + j) % 4).wait_recv()
        for i in range(1, 8):
            pool_copy(i, dp).start()
        pool_in[dp] = pool_out[dp]

    def normalize(r):
        for half in range(2):
            rows = pl.ds(pl.multiple_of(r * rows_each + half * (rows_each // 2), 32), rows_each // 2)
            values = tok[rows, :].astype(FULL)
            mean_square = jnp.sum(values * values, axis=-1, keepdims=True) * (1.0 / width)
            rs[rows, :] = jnp.broadcast_to(lax.rsqrt(mean_square + 1e-06), (rows_each // 2, 128))

    def turn(piece):
        return piece * cosine[...] + pltpu.roll(piece, HEAD_DIM // 2, 1) * sine[...]

    def keyval_rows(low, top):
        @pl.loop(low, top)
        def _(r):
            forward_copy(r, far).wait_recv()
            normalize(r)
            rows = rows_of(r)
            product = jnp.dot(tok[rows, :], wide[0], preferred_element_type=FULL)
            kst[rows, :] = turn(product[:, :HEAD_DIM] * rs[rows, :]).astype(HALF)
            vst[rows, :] = (product[:, HEAD_DIM:] * rs[rows, :]).astype(HALF)

    rows_group = GROUP * seq_len

    def product_of(c, rows, first, length):
        depth_rows = pl.ds(first, length)
        weights = wide[c, depth_rows, :] if c < 4 else narrow[depth_rows, :]
        return jnp.dot(tok[rows, pl.ds(first, length)], weights, preferred_element_type=FULL)

    def total_of(c):
        return acc_wide if c < 4 else acc_narrow

    def partial_block(c, first, length, fresh, low=0, top=total // GROUP // seq_len):
        @pl.loop(low, top)
        def _(r):
            rows = pl.ds(pl.multiple_of(r * rows_group, 128), rows_group)
            product = product_of(c, rows, pl.multiple_of(first, 128), length)
            if fresh:
                total_of(c)[rows, :] = product
            else:
                total_of(c)[rows, :] += product

    def query_rows(c, r, slot):
        rows = pl.ds(pl.multiple_of(r * rows_group, 128), rows_group)
        if c < 2:
            product = product_of(c, rows, 0, width)
        else:
            last = pl.multiple_of(across(3 if c > 2 else 1) * part, 128)
            product = total_of(c)[rows, :] + product_of(c, rows, last, part)
        for h in range(product.shape[1] // HEAD_DIM):
            span = slice(h * HEAD_DIM, (h + 1) * HEAD_DIM)
            for half in range(2):
                here = slice(half * rows_each, (half + 1) * rows_each)
                some = pl.ds(
                    pl.multiple_of(r * rows_group + half * rows_each, 64), rows_each
                )
                qst[slot, here, span] = turn(product[here, span] * rs[some, :]).astype(HALF)

    def attend_rows(c, r, slot):
        heads = 2 if c < 4 else 1
        lanes = heads * seq_len
        key_pos = lax.broadcasted_iota(jnp.int32, (seq_len, lanes), 0)
        query_pos = lax.broadcasted_iota(jnp.int32, (seq_len, lanes), 1) % seq_len
        causal = key_pos <= query_pos
        position = lax.broadcasted_iota(jnp.int32, (1, lanes), 1) % seq_len
        pieces = []
        for item in range(GROUP):
            here = slice(item * seq_len, (item + 1) * seq_len)
            keys = kst[pl.ds(pl.multiple_of(r * rows_group + item * seq_len, 16), seq_len), :]
            stacked = qst[slot, here, :HEAD_DIM]
            if heads == 2:
                stacked = jnp.concatenate([stacked, qst[slot, here, HEAD_DIM:]], axis=0)
            scores = lax.dot_general(keys, stacked, NT, preferred_element_type=FULL)
            scores = jnp.where(causal, scores * (1.0 / math.sqrt(HEAD_DIM)), -1e30)
            expanded = jnp.exp(scores - jnp.max(scores, axis=0, keepdims=True))
            length = lens[r * GROUP + item]
            share = jnp.where(position < length, 1.0, 0.0) / (
                jnp.sum(expanded, axis=0, keepdims=True)
                * jnp.full((1, lanes), length, jnp.int32).astype(FULL)
            )
            pieces.append((expanded * share).astype(HALF))
        weights = jnp.concatenate(pieces, axis=0)
        head_row = lax.broadcasted_iota(jnp.int32, (16, lanes), 0) // GROUP
        head_lane = lax.broadcasted_iota(jnp.int32, (16, lanes), 1) // seq_len
        chosen = jnp.where(head_row == head_lane, 1.0, 0.0).astype(HALF)
        sums_of = lax.dot_general(chosen, weights, NT, preferred_element_type=FULL)
        item_row = lax.broadcasted_iota(jnp.int32, sums_of.shape, 0) % GROUP
        item_lane = lax.broadcasted_iota(jnp.int32, sums_of.shape, 1) // seq_len
        sums_of = jnp.where(item_row == item_lane, sums_of, 0.0)
        coarse = sums_of.astype(HALF).astype(FULL)
        both = jnp.concatenate([coarse, sums_of - coarse], axis=0).astype(HALF)
        rows = pl.ds(pl.multiple_of(r * rows_group, 128), rows_group)
        mixed = jnp.dot(both, vst[rows, :], preferred_element_type=FULL)
        ctx[c - 1, r] = mixed[:16] + mixed[16:]

    def query_block(c, low, top):
        query_rows(c, low, low % 2)

        @pl.loop(low + 1, top)
        def _(r):
            attend_rows(c, r - 1, (r - 1) % 2)
            query_rows(c, r, r % 2)

        attend_rows(c, top - 1, (top - 1) % 2)

    def member_squares(low, top):
        @pl.loop(low, top)
        def _(step):
            rows = pl.ds(pl.multiple_of(step * 64, 64), 64)
            values = members[rows, :].astype(FULL)
            squares[rows, :] = jnp.broadcast_to(
                jnp.sum(values * values, axis=-1, keepdims=True), (64, 128)
            )

    @at_mid
    def _():
        onward("mid", 0, (2, 0), 1, 0)
        onward("mid", 0, (0, 0), 2)

    @at_end
    def _():
        onward("end", 0, (0, 1), 1)

    load_members.wait()
    member_squares(0, 4)
    relay_tokens(0)

    @at_mid
    def _():
        onward("mid", 1, (0, 0), 2)
        own("mid", 2, 2)
        onward("mid", 1, (2, 0), 0)
        own("mid", 0, 4)

    @at_end
    def _():
        onward("end", 1, (0, 1), 1)

    pool()

    @at_mid
    def _():
        onward("mid", 0, (3, 0), 1, 0)
        onward("mid", 0, (1, 1), 1)
        send("mid", 1, 1, (2, 0))
        onward("mid", 2, (0, 0), 2)
        own("mid", 2, 3)

    @at_end
    def _():
        onward("end", 0, (2, 0), 0)
        onward("end", 2, (0, 1), 1)

    relay_tokens(1)

    @at_mid
    def _():
        onward("mid", 1, (3, 0), 1, 0)
        own("mid", 1, 2)
        onward("mid", 3, (0, 0), 2)
        own("mid", 2, 4)

    @at_end
    def _():
        onward("end", 0, (3, 0), 0)
        onward("end", 1, (1, 0), 0)
        own("end", 0, 4)
        onward("end", 3, (0, 1), 1)
        own("end", 1, 4)

    relay_tokens(2)

    @at_mid
    def _():
        onward("mid", 2, (2, 0), 1, 0)
        onward("mid", 4, (0, 0), 2)

    @at_end
    def _():
        onward("end", 1, (2, 0), 0)

    member_squares(4, 8)
    relay_tokens(3)

    @at_mid
    def _():
        onward("mid", 2, (3, 0), 1, 0)
        own("mid", 1, 3)
        onward("mid", 2, (1, 1), 1)
        onward("mid", 3, (2, 0), 1, 0)

    core_copy(core_peer).wait_recv()
    rest(0)
    keyval_rows(0, 4)

    @at_end
    def _():
        onward("end", 1, (3, 0), 0)
        onward("end", 4, (0, 1), 1)

    relay_tokens(4)

    @at_mid
    def _():
        onward("mid", 3, (3, 0), 1, 0)
        onward("mid", 4, (2, 0), 1, 0)

    relay_tokens(5)

    @at_end
    def _():
        onward("end", 2, (2, 0), 0)

    @at_mid
    def _():
        onward("mid", 4, (3, 0), 1, 0)
        own("mid", 1, 4)
        onward("mid", 4, (1, 1), 1)

    keyval_rows(4, 6)
    rest(1)
    query_block(1, 0, 1)

    @at_end
    def _():
        onward("end", 2, (3, 0), 0)

    query_block(1, 1, 3)
    relay_tokens(6)
    load_out.wait()
    own_out = out_copy(0, mp, y_peer)
    own_out.start()
    beside_out = out_copy(1, mp, core_peer)
    beside_out.start()
    need(2, 0, 2)
    partial_block(2, across(0) * part, part, True, 0, 3)
    partial_block(2, across(2) * part, part, False, 0, 3)

    @at_end
    def _():
        onward("end", 3, (1, 0), 0)

    need(2, 3)
    partial_block(2, across(3) * part, part, False, 0, 3)
    relay_tokens(7)
    keyval_rows(6, 8)
    query_block(1, 3, 4)
    partial_block(2, across(0) * part, part, True, 3, 4)
    partial_block(2, across(2) * part, part, False, 3, 4)
    partial_block(2, across(3) * part, part, False, 3, 4)
    rest(2)
    query_block(2, 0, 2)

    @at_end
    def _():
        onward("end", 3, (2, 0), 0)

    query_block(2, 2, 4)

    lane_head = (place_lane // GROUP) % 2
    heads_of = (((0, 2), (1, 3)), ((4, 5),), ((6, None),))
    couts, cins = (cout_a, cout_b, cout_c), (cin_a, cin_b, cin_c)

    def pick(h, right):
        right = right & (lane_head == h % 2)
        return jnp.where(right & (held == slot_wide), 1.0, 0.0).astype(HALF)[:, :64]

    def group_copy(p, j, m_slot):
        to = (mp + j) % 4
        return remote(
            couts[p].at[to], cins[p].at[dp, m_slot], a_send.at[p, j], a_recv.at[p, m_slot], dp, to
        )

    def context_copy(p, i, d_slot):
        return remote(
            cins[p].at[d_slot], cins[p].at[d_slot], c_send.at[p, i], c_recv.at[p, d_slot],
            (dp + i) % 8, mp,
        )

    def direct_copy(i, j, d_slot, m_slot):
        to = (mp + j) % 4
        return remote(
            cout_c.at[to], cin_c.at[d_slot, m_slot], e_out.at[i, j], e_in.at[d_slot, m_slot],
            (dp + i) % 8, to,
        )

    partners = [(i, j) for i in (4, 3, 5, 2, 6, 1, 7, 0) for j in range(4) if i or j]

    def share_part(p):
        for block, (top, bottom) in enumerate(heads_of[p]):
            rows = ctx[top // 2].reshape(64, 128).astype(HALF)
            value = jnp.dot(pick(top, upper), rows, preferred_element_type=FULL)
            if bottom is not None:
                rows = ctx[bottom // 2].reshape(64, 128).astype(HALF)
                value = value + jnp.dot(
                    pick(bottom, jnp.logical_not(upper)), rows, preferred_element_type=FULL
                )
            couts[p][:, :, block * 128 : (block + 1) * 128] = value.astype(HALF).reshape(
                4, 16, 128
            )
        if p == 2:
            for i, j in partners:
                direct_copy(i, j, dp, mp).start()
        else:
            for j in range(1, 4):
                group_copy(p, j, mp).start()
        cins[p][dp, mp] = couts[p][mp]

    def spread_part(p):
        for j in range(1, 4):
            group_copy(p, j, (mp + j) % 4).wait_recv()
        for i in (4, 3, 5, 2, 6, 1, 7):
            context_copy(p, i, dp).start()

    share_part(0)
    need(3, 0, 1)
    partial_block(3, high * 2 * part, 2 * part, True)

    @at_end
    def _():
        onward("end", 3, (3, 0), 0)

    need(3, 2)
    partial_block(3, across(2) * part, part, False)

    @at_end
    def _():
        onward("end", 4, (2, 0), 0)

    need(4, 0)
    partial_block(4, across(0) * part, part, True)

    @at_end
    def _():
        onward("end", 4, (3, 0), 0)

    spread_part(0)

    limit = counts[0] * 0
    for c in range(counts.shape[0]):
        limit = limit + jnp.where(owner[c] == dp, counts[c], 0)
    member_count = members.shape[0]
    member = mp * member_count + lax.broadcasted_iota(jnp.int32, (1, member_count), 1)
    scale = jnp.where(member < limit, logit_scale, 0.0) * lax.rsqrt(squares[...].T[0:1, :] + 1e-06)
    rest(3)
    query_block(3, 0, 4)
    share_part(1)
    need(4, 2)
    partial_block(4, across(2) * part, part, False)
    need(4, 1)
    partial_block(4, across(1) * part, part, False)
    out_copy(0, y_peer, y_peer).wait_recv()
    onward_out = out_copy(2, y_peer, core_peer)
    onward_out.start()
    rest(4)
    spread_part(1)
    spread_pool()
    query_block(4, 0, 4)
    share_part(2)
    out_copy(1, core_peer, core_peer).wait_recv()
    out_copy(2, far, core_peer).wait_recv()

    half_out = wot.shape[0]
    total_a = jnp.zeros((128, half_out), FULL)
    total_b = jnp.zeros((128, half_out), FULL)

    def lanes_from(m, first, length):
        return wot[:, m * part + first : m * part + first + length]

    for p in range(3):
        if p == 2:
            for i, j in partners:
                direct_copy(i, j, (dp + i) % 8, (mp + j) % 4).wait_recv()
        else:
            for i in range(1, 8):
                context_copy(p, i, (dp + i) % 8).wait_recv()
        length = cins[p].shape[3]
        for m in range(4):
            have = cins[p][:, m].reshape(128, length)
            first = (0, 512, 768)[p]
            total_a = total_a + lax.dot_general(
                have, lanes_from(m, first, length), NT, preferred_element_type=FULL
            )
            if p < 2:
                total_b = total_b + lax.dot_general(
                    have, lanes_from(m, first + length, length), NT, preferred_element_type=FULL
                )
    embedded = (
        total_a.reshape(8, 16, half_out)[:, :8]
        + total_b.reshape(8, 16, half_out)[:, 8:]
    ).reshape(64, half_out)
    for i in range(1, 8):
        pool_copy(i, (dp + i) % 8).wait_recv()
    pooled = pool_in[...].astype(FULL)
    embedded = embedded + jnp.concatenate(
        [pooled[:, :8].reshape(64, 256), pooled[:, 8:].reshape(64, 256)[:, : half_out - 256]],
        axis=1,
    )
    row = lax.broadcasted_iota(jnp.int32, (64, 64), 0)
    column = lax.broadcasted_iota(jnp.int32, (64, 64), 1)
    order = jnp.where(
        column == ((row // 4) % 8) * 8 + (row // 32) * 4 + row % 4, 1.0, 0.0
    ).astype(HALF)
    sums[...] = (
        jnp.dot(order, embedded.astype(HALF), preferred_element_type=FULL)
        .astype(HALF)
        .reshape(sums.shape)
    )

    core = mp % 2
    home = 2 * x + (z + 1) // 2 % 2

    def sum_copy(j, y):
        return remote(
            sums.at[j], rows_in.at[dp], d_send.at[j, y], d_recv.at[dp], owner_of(mp, j), 2 * y + x
        )

    def hand_copy(k, slot):
        return remote(
            rows_in.at[slot], rows_in.at[slot], e_send.at[k], d_recv.at[slot], dp, core_peer
        )

    for j in range(2):
        for y in range(2):
            mine = (owner_of(mp, j) == dp) & (2 * y + x == mp)

            @pl.when(jnp.logical_not(mine))
            def _():
                sum_copy(j, y).start()

            @pl.when(mine)
            def _():
                rows_in[dp] = sums[j]

    for k in range(4):
        slot = 2 * k + core

        @pl.when(jnp.logical_not((slot == dp) & (mp == home)))
        def _():
            hand_copy(k, slot).wait_recv()

        hand_copy(k, slot).start()
    for k in range(4):
        hand_copy(k, 2 * k + 1 - core).wait_recv()

    for slot in range(8):
        joined[:, slot * half_out : (slot + 1) * half_out] = rows_in[slot].astype(FULL)
    embedding = joined[...]
    dots = lax.dot_general(
        embedding.astype(HALF), members[...], NT, preferred_element_type=FULL
    )
    inverse = lax.rsqrt(jnp.sum(embedding * embedding, axis=-1, keepdims=True) + 1e-06)
    found = (dots * inverse * scale).astype(HALF)
    row = lax.broadcasted_iota(jnp.int32, (128, 32), 0)
    column = lax.broadcasted_iota(jnp.int32, (128, 32), 1)
    value = jnp.zeros((128, 128), FULL)
    for q in range(4):
        spread = jnp.where(
            ((row % 16) // 4 == q) & (column == (row // 16) * 4 + row % 4), 1.0, 0.0
        ).astype(HALF)
        value = value + jnp.dot(
            spread, found[:, q * 128 : (q + 1) * 128], preferred_element_type=FULL
        )
    replies[...] = value.astype(HALF).reshape(replies.shape)

    def reply_copy(i, slot):
        to = (dp + i) % 8
        return remote(replies.at[to], arrived.at[slot], f_send.at[i], f_recv.at[slot], to, mp)

    for i in range(1, 8):
        reply_copy(i, dp).start()
    arrived[dp] = replies[dp]
    for i in range(1, 8):
        reply_copy(i, (dp + i) % 8).wait_recv()
    have = arrived[...].reshape(128, 128)
    column = lax.broadcasted_iota(jnp.int32, (dialogs, 128), 1).astype(FULL)
    for q in range(4):
        fetch = jnp.where(column == reply_place + 4.0 * q, flag_col, 0.0).astype(HALF)
        out[:, q * 128 : (q + 1) * 128] = jnp.dot(fetch, have, preferred_element_type=FULL)

    for r in range(chunks):
        y_copy(r, mp).wait_send()
        forward_copy(r, y_peer).wait_send()
    core_copy(mp).wait_send()
    own_out.wait_send()
    beside_out.wait_send()
    onward_out.wait_send()

    @at_end
    def _():
        for way, c, kind in sent["end"]:
            weight_copy(way, c, kind).wait_send()

    @at_mid
    def _():
        for way, c, kind in sent["mid"]:
            weight_copy(way, c, kind).wait_send()

    for j in range(2):
        for y in range(2):
            @pl.when(jnp.logical_not((owner_of(mp, j) == dp) & (2 * y + x == mp)))
            def _():
                sum_copy(j, y).wait_send()

    for k in range(4):
        hand_copy(k, 2 * k + core).wait_send()
    for i in range(1, 4):
        pool_group(i, mp).wait_send()
        for p in range(2):
            group_copy(p, i, mp).wait_send()
    for i in range(1, 8):
        for p in range(2):
            context_copy(p, i, dp).wait_send()
    for i, j in partners:
        direct_copy(i, j, dp, mp).wait_send()
    for i in range(1, 8):
        reply_copy(i, dp).wait_send()
        pool_copy(i, dp).wait_send()


def fused(
    tokens, norm_gain, w_query, w_keyval, w_out, residents, lengths, cluster, owner, counts, flags
):
    dialogs, seq_len, part = tokens.shape
    total = dialogs * seq_len
    depth, queries = w_query.shape
    width = norm_gain.shape[0]
    member_count = residents.shape[1]
    half_out = w_out.shape[1]
    half = HEAD_DIM // 2
    freqs = rope_base ** (-np.arange(half, dtype=np.float64) * 2.0 / HEAD_DIM)
    angles = np.arange(seq_len, dtype=np.float64)[:, None] * freqs[None, :]
    cosine, sine = np.cos(angles), np.sin(angles)
    cosine = np.tile(np.concatenate([cosine, cosine], axis=1), (CHUNK, 1)).astype(np.float32)
    sine = np.tile(np.concatenate([-sine, sine], axis=1), (CHUNK, 1)).astype(np.float32)
    vmem = pl.BlockSpec(memory_space=pltpu.VMEM)
    smem = pl.BlockSpec(memory_space=pltpu.SMEM)
    hbm = pl.BlockSpec(memory_space=pltpu.HBM)
    sem = pltpu.SemaphoreType.DMA
    return pl.pallas_call(
        fused_kernel,
        out_shape=jax.ShapeDtypeStruct((dialogs, member_count), FULL),
        in_specs=[smem] * 5 + [hbm, hbm, hbm, vmem, hbm, hbm, vmem, vmem],
        out_specs=vmem,
        scratch_shapes=[
            pltpu.VMEM((total, width), HALF),
            pltpu.VMEM((4, width, 256), HALF),
            pltpu.VMEM((width, 128), HALF),
            pltpu.VMEM((half_out, width), HALF),
            pltpu.VMEM((member_count, width), HALF),
            pltpu.VMEM((depth, queries), HALF),
            pltpu.VMEM((depth, 2, 128), HALF),
            pltpu.VMEM((512, 128), FULL),
            pltpu.VMEM((total, 128), FULL),
            pltpu.VMEM((total, 128), HALF),
            pltpu.VMEM((total, 128), HALF),
            pltpu.VMEM((2, GROUP * seq_len, 256), HALF),
            pltpu.VMEM((4, 4, 16, 128), FULL),
            pltpu.VMEM((dialogs, total), HALF),
            pltpu.VMEM((total, 256), FULL),
            pltpu.VMEM((total, 128), FULL),
            pltpu.VMEM((4, 2, 16, 256), HALF),
            pltpu.VMEM((8, 16, 256), HALF),
            pltpu.VMEM((8, 16, 256), HALF),
            pltpu.VMEM((4, 16, 256), HALF),
            pltpu.VMEM((4, 16, 128), HALF),
            pltpu.VMEM((4, 16, 128), HALF),
            pltpu.VMEM((8, 4, 16, 256), HALF),
            pltpu.VMEM((8, 4, 16, 128), HALF),
            pltpu.VMEM((8, 4, 16, 128), HALF),
            pltpu.VMEM((2, 32, half_out), HALF),
            pltpu.VMEM((8, 32, half_out), HALF),
            pltpu.VMEM((32, width), FULL),
            pltpu.VMEM((member_count, 128), FULL),
            pltpu.VMEM((8, 16, 128), HALF),
            pltpu.VMEM((8, 16, 128), HALF),
            sem((5,)),
            sem((8,)),
            sem((8,)),
            sem,
            sem,
            sem((8,)),
            sem((8,)),
            sem((3, 5, 8)),
            sem((5, 8)),
            sem((3,)),
            sem((3,)),
            sem((4,)),
            sem((4,)),
            sem((8,)),
            sem((8,)),
            sem((3, 4)),
            sem((3, 4)),
            sem((3, 8)),
            sem((3, 8)),
            sem((2, 2)),
            sem((8,)),
            sem((4,)),
            sem((8,)),
            sem((8,)),
            sem((8, 4)),
            sem((8, 4)),
        ],
        compiler_params=pltpu.CompilerParams(
            collective_id=0, has_side_effects=True, vmem_limit_bytes=58 * 1024 * 1024
        ),
    )(
        lengths, cluster[:, 0], owner, counts, flags,
        tokens.reshape(total, part), w_query, w_keyval,
        norm_gain.reshape(-1, 128), w_out.T, residents[0], cosine, sine,
    )


def plain_project(tokens, norm_gain, w_query, w_keyval, lengths):
    gathered = lax.all_gather(tokens, "mp", axis=2, tiled=True)
    dialogs, seq_len, width = gathered.shape
    hidden = gathered.astype(jnp.float32)
    normed = (
        hidden * lax.rsqrt(jnp.mean(hidden * hidden, axis=-1, keepdims=True) + 1e-06) * norm_gain
    ).astype(jnp.bfloat16)
    normed_flat = normed.reshape(dialogs * seq_len, width)
    query_cols = w_query.shape[1]
    keyval_cols = w_keyval.shape[2]
    pieces = (
        lax.all_gather(w_query, "dp", axis=0, tiled=True),
        lax.all_gather(w_keyval, "dp", axis=0, tiled=True),
    )
    keyval_piece = pieces[1].reshape(pieces[1].shape[0], 2 * keyval_cols)
    query_sum = jnp.dot(normed_flat, pieces[0], preferred_element_type=jnp.float32)
    keyval_sum = jnp.dot(normed_flat, keyval_piece, preferred_element_type=jnp.float32)
    positions = jnp.arange(seq_len)
    local_heads = query_cols // HEAD_DIM
    local_kv = keyval_cols // HEAD_DIM
    query = jax.vmap(lambda block: rotate(block, positions))(
        query_sum.reshape(dialogs, seq_len, local_heads, HEAD_DIM)
    ).astype(jnp.bfloat16)
    keys = jax.vmap(lambda block: rotate(block, positions))(
        keyval_sum[:, :keyval_cols].reshape(dialogs, seq_len, local_kv, HEAD_DIM)
    ).astype(jnp.bfloat16)
    values = (
        keyval_sum[:, keyval_cols:]
        .reshape(dialogs, seq_len, local_kv, HEAD_DIM)
        .astype(jnp.bfloat16)
    )
    valid = (positions[None, :] < lengths[:, None]).astype(jnp.float32)
    pooled_input = (
        jnp.sum(hidden * valid[:, :, None], axis=1) / lengths.astype(jnp.float32)[:, None]
    )
    pooled_context = jax.vmap(attend)(query, keys, values, lengths).astype(jnp.bfloat16)
    return pooled_context, pooled_input


def plain_score(pooled_context, pooled_input, w_out, members, onehot, live):
    dialogs = pooled_context.shape[0]
    everyone = lax.all_gather(pooled_context, "dp", axis=0, tiled=True)
    slices = jnp.dot(everyone, w_out, preferred_element_type=jnp.float32).astype(jnp.bfloat16)
    slices = slices.reshape(-1, dialogs, w_out.shape[1])
    slices = lax.all_to_all(slices, "dp", split_axis=0, concat_axis=0, tiled=True)
    partial_out = slices.transpose(1, 0, 2).reshape(dialogs, -1)
    projected = lax.psum(partial_out, "mp").astype(jnp.float32)
    embedding = pooled_input + projected
    unit = embedding * lax.rsqrt(jnp.sum(embedding * embedding, axis=-1, keepdims=True) + 1e-06)
    unit = unit.astype(jnp.bfloat16)
    inverse_norm = lax.rsqrt(
        jnp.einsum("md,md->m", members, members, preferred_element_type=jnp.float32) + 1e-06
    )
    outgoing = jnp.einsum(
        "ocn,nd->ocd", onehot.astype(jnp.bfloat16), unit, preferred_element_type=jnp.float32
    ).astype(jnp.bfloat16)
    query_rows = lax.all_to_all(outgoing, "dp", split_axis=0, concat_axis=0, tiled=True)
    dots = lax.dot_general(
        query_rows,
        members,
        (((query_rows.ndim - 1,), (1,)), ((), ())),
        preferred_element_type=jnp.float32,
    )
    return lax.all_to_all(
        jnp.where(live[0] > 0, live[0] * dots * inverse_norm, 0.0).astype(jnp.bfloat16),
        "dp",
        split_axis=0,
        concat_axis=0,
        tiled=True,
    )


def general(
    tokens, norm_gain, w_query, w_keyval, w_out, residents, lengths, cluster, owner, counts, flags
):
    pooled_context, pooled_input = plain_project(tokens, norm_gain, w_query, w_keyval, lengths)
    dialogs = tokens.shape[0]
    my_index = lax.axis_index("dp")
    owner_count = lax.axis_size("dp")
    my_count = jnp.sum(jnp.where(owner == my_index, counts, 0))
    members = residents[0]
    member_count = members.shape[0]
    member_start = lax.axis_index("mp") * member_count
    live = jnp.where(member_start + jnp.arange(member_count) < my_count, logit_scale, 0.0)[None, :]
    table_size = owner.shape[0]
    cluster_ids = cluster[:, 0]
    destination = jnp.sum(
        jnp.where(jnp.arange(table_size)[None, :] == cluster_ids[:, None], owner[None, :], 0),
        axis=1,
    )
    capacity = max(1, -(-dialogs // owner_count))
    order = jnp.arange(dialogs)
    earlier = (destination[None, :] == destination[:, None]) & (order[None, :] < order[:, None])
    rank = jnp.sum(earlier.astype(jnp.int32), axis=1)
    onehot = (jnp.arange(owner_count)[:, None, None] == destination[None, None, :]) & (
        jnp.arange(capacity)[None, :, None] == rank[None, None, :]
    )
    returned = plain_score(pooled_context, pooled_input, w_out, members, onehot, live)
    similarity = jnp.einsum(
        "ocn,ocm->nm", onehot.astype(jnp.bfloat16), returned, preferred_element_type=jnp.float32
    )
    return similarity * flags.astype(jnp.float32)[:, None]


def local(*args):
    if lax.axis_size("dp") == 8 and lax.axis_size("mp") == 4:
        return fused(*args)
    return general(*args)


def solution(mesh):
    in_specs = (
        P("dp", None, "mp"),
        P(),
        P("dp", "mp"),
        P("dp", None, "mp"),
        P("mp", "dp"),
        P("dp", "mp"),
        P("dp"),
        P("dp"),
        P(),
        P(),
        P("dp"),
    )
    out_specs = P("dp", "mp")
    return jax.shard_map(local, mesh=mesh, in_specs=in_specs, out_specs=out_specs, check_vma=False)
```
